32 devices in a mesh: dp: 16 (over z, y, x), rep: 2 (over core).
Axes of the slice: x: 2, y: 2, z: 4, core: 2. Of those that a mesh axis runs over, the one named last changes fastest.
Arguments:
- images: bfloat16 [1024, 145, 768], P(('dp', 'rep')), may hold values from -6 to 6
- groups: int32 [1024], P(('dp', 'rep')), may hold values from 0 to 1, as said below
- captions: bfloat16 [1024, 16, 768], P(('dp', 'rep')), may hold values from -6 to 6
- cap_lengths: int32 [1024], P(('dp', 'rep')), may hold values from 4 to 16, as said below
- img_gain_a: bfloat16 [768], P('rep'), may hold values from 0.5 to 1.5
- img_w_qkv: bfloat16 [768, 2304], P('rep'), may hold values from -0.21875 to 0.21875
- img_b_qv: bfloat16 [1536], P('rep'), may hold values from -3 to 3
- img_w_out: bfloat16 [768, 768], P('rep'), may hold values from -0.625 to 0.625
- img_gain_m: bfloat16 [768], P('rep'), may hold values from 0.5 to 1.5
- img_w_up: bfloat16 [768, 3072], P('rep'), may hold values from -0.21875 to 0.21875
- img_b_up: bfloat16 [3072], P('rep'), may hold values from -3 to 3
- img_w_down: bfloat16 [3072, 768], P('rep'), may hold values from -0.109375 to 0.109375
- gain_attn: bfloat16 [768], replicated, may hold values from 0.5 to 1.5
- w_qkv: bfloat16 [768, 2304], replicated, may hold values from -0.21875 to 0.21875
- b_qv: bfloat16 [1536], replicated, may hold values from -3 to 3
- w_out: bfloat16 [768, 768], replicated, may hold values from -0.625 to 0.625
- gain_mlp: bfloat16 [768], replicated, may hold values from 0.5 to 1.5
- w_up: bfloat16 [768, 3072], replicated, may hold values from -0.21875 to 0.21875
- b_up: bfloat16 [3072], replicated, may hold values from -3 to 3
- w_down: bfloat16 [3072, 768], replicated, may hold values from -0.109375 to 0.109375
- text_proj: bfloat16 [768, 768], replicated, may hold values from -0.21875 to 0.21875
Outputs:
- pair_loss: float32 [1024], P(('dp', 'rep'))
- caption_grad: float32 [1024, 16, 768], P(('dp', 'rep'))
- grad_gain_attn: float32 [768], P('rep')
- grad_w_qkv: float32 [768, 2304], P(None, 'rep')
- grad_b_qv: float32 [1536], P('rep')
- grad_w_out: float32 [768, 768], P(None, 'rep')
- grad_gain_mlp: float32 [768], P('rep')
- grad_w_up: float32 [768, 3072], P(None, 'rep')
- grad_b_up: float32 [3072], P('rep')
- grad_w_down: float32 [3072, 768], P(None, 'rep')
The draws below stay inside these ranges and needn't reach their ends.
Inputs may be any that keep to these rules, and one draw needn't show every extreme that they name: `groups`: 1 marks an image of 145 tokens, 0 one of 50 tokens whose later positions are unused; the 32 pairs of every device hold images of both kinds. Positions of a caption from cap_lengths on are padding; the 32 pairs of every device hold a caption of 16 tokens.
All inputs are finite; a program needn't handle non-finite values.
Results may differ from the reference program's by a relative error of at most 0.0165.
Values may be sent and summed in bfloat16 or wider, within the bound.
No kernel may reach another device: no remote copies, remote signals or barrier semaphores. Data moves between devices by JAX's collectives and lax.ppermute only.
A program may use at most 192 MiB of HBM per device.

```python
import math
import jax
import jax.numpy as jnp
from jax import lax

D = 768
HEADS = 12
FF = 3072
ILEN = 145
LOWLEN = 50
CAP = 16
P_DEV = 32
IMG_BLK = 4
PAIRS = 1024


def draw_groups(key, part):
    blocks = PAIRS // P_DEV
    first, second, third = jax.random.split(jax.random.fold_in(key, 11), 3)
    levels = jax.random.randint(first, (blocks, 1), 1, 9)
    rolled = jax.random.randint(second, (blocks, P_DEV), 0, 16)
    marks = (rolled < levels).astype(jnp.int32)
    where_one = jax.random.randint(third, (blocks, 1), 0, P_DEV // 2)
    places = jnp.arange(P_DEV, dtype=jnp.int32)[None, :]
    marks = jnp.where(places == where_one, 1, marks)
    marks = jnp.where(places == where_one + P_DEV // 2, 0, marks)
    return marks.reshape(PAIRS).astype(jnp.int32)


def draw_cap_lengths(key, part):
    blocks = PAIRS // P_DEV
    first, second = jax.random.split(jax.random.fold_in(key, 23), 2)
    counts_drawn = jax.random.randint(first, (blocks, P_DEV), 4, CAP + 1)
    where_full = jax.random.randint(second, (blocks, 1), 0, P_DEV)
    places = jnp.arange(P_DEV, dtype=jnp.int32)[None, :]
    counts_drawn = jnp.where(places == where_full, CAP, counts_drawn)
    return counts_drawn.reshape(PAIRS).astype(jnp.int32)


def shard_levels(key, dims, pieces, least, top_value):
    gain, own = 1.0, jax.random.fold_in(key, 6)
    for position, blocks in pieces:
        steps = jnp.exp(jax.random.uniform(jax.random.fold_in(own, position), (blocks,), jnp.float32, least / len(pieces), top_value / len(pieces)))
        gain = gain * jnp.repeat(steps, dims[position] // blocks).reshape([-1 if axis == position else 1 for axis in range(len(dims))])
    return gain


def centred(own_key, shape, deviation, most, pieces=(), kind=jnp.bfloat16):
    level = shard_levels(own_key, shape, pieces, -0.22, 0.18) if pieces else 1.0
    values = jax.random.normal(own_key, shape, jnp.float32) * deviation * level
    return jnp.minimum(jnp.maximum(values, -most), most).astype(kind)


def setup_inputs(seed: int = 0) -> dict:
    splits = jax.random.split(jax.random.key(seed), 22)
    return {
        "images": centred(splits[0], (PAIRS, ILEN, D), 1.0, 6.0, ((0, 32),)),
        "groups": draw_groups(jax.random.fold_in(splits[21], 71), 0),
        "captions": centred(splits[2], (PAIRS, CAP, D), 1.0, 6.0, ((0, 32),)),
        "cap_lengths": draw_cap_lengths(jax.random.fold_in(splits[21], 71), 0),
        "img_gain_a": jnp.clip(1.0 + 0.1 * jax.random.normal(splits[4], (D,), jnp.float32), 0.5, 1.5).astype(jnp.bfloat16),
        "img_w_qkv": centred(splits[5], (D, 3 * D), D ** -0.5, 0.21875, ((0, 2),)),
        "img_b_qv": centred(splits[6], (2 * D,), 0.5, 3.0, ((0, 2),)),
        "img_w_out": centred(splits[7], (D, D), (D // 8) ** -0.5, 0.625, ((0, 2),)),
        "img_gain_m": jnp.clip(1.0 + 0.1 * jax.random.normal(splits[8], (D,), jnp.float32), 0.5, 1.5).astype(jnp.bfloat16),
        "img_w_up": centred(splits[9], (D, FF), D ** -0.5, 0.21875, ((0, 2),)),
        "img_b_up": centred(splits[10], (FF,), 0.5, 3.0, ((0, 2),)),
        "img_w_down": centred(splits[11], (FF, D), FF ** -0.5, 0.109375, ((0, 2),)),
        "gain_attn": jnp.clip(1.0 + 0.1 * jax.random.normal(splits[12], (D,), jnp.float32), 0.5, 1.5).astype(jnp.bfloat16),
        "w_qkv": centred(splits[13], (D, 3 * D), D ** -0.5, 0.21875),
        "b_qv": centred(splits[14], (2 * D,), 0.5, 3.0),
        "w_out": centred(splits[15], (D, D), (D // 8) ** -0.5, 0.625),
        "gain_mlp": jnp.clip(1.0 + 0.1 * jax.random.normal(splits[16], (D,), jnp.float32), 0.5, 1.5).astype(jnp.bfloat16),
        "w_up": centred(splits[17], (D, FF), D ** -0.5, 0.21875),
        "b_up": centred(splits[18], (FF,), 0.5, 3.0),
        "w_down": centred(splits[19], (FF, D), FF ** -0.5, 0.109375),
        "text_proj": centred(splits[20], (D, D), D ** -0.5, 0.21875),
    }


SCALE = 100.0
EPS = 1e-06
NEGATIVE = -1e+30
HIGHEST = lax.Precision.HIGHEST

@jax.custom_vjp
def low(v):
    return lax.optimization_barrier(v.astype(jnp.bfloat16)).astype(jnp.float32)

@jax.custom_vjp
def low_back(v):
    return v

def low_keep(v):
    return (low(v), None)

def low_pass(kept, grad):
    return (grad,)

def back_keep(v):
    return (v, None)

def back_low(kept, grad):
    return (low(grad),)
low.defvjp(low_keep, low_pass)
low_back.defvjp(back_keep, back_low)

def matmul(left_side, right_side):
    return jnp.dot(left_side, right_side, precision=HIGHEST)

def layer_norm(values, gain_vec):
    center = values - lax.optimization_barrier(jnp.mean(values, -1, keepdims=True))
    return center * lax.rsqrt(lax.optimization_barrier(jnp.mean(center * center, -1, keepdims=True)) + EPS) * gain_vec

def residual_block(tokens, length, params):
    gain_a, weight_qkv, bias_qv, weight_out, gain_m, weight_up, bias_up, weight_down = params
    number, span_len, model_dim = tokens.shape
    head_dim = model_dim // HEADS
    flat_rows = tokens.reshape(number * span_len, model_dim)
    input_low = low(layer_norm(flat_rows, gain_a))
    bias_full = jnp.concatenate([bias_qv[:model_dim], jnp.zeros((model_dim,), jnp.float32), bias_qv[model_dim:]])
    projected = low(low_back(matmul(input_low, weight_qkv) + bias_full))
    projected = projected.reshape(number, span_len, 3, HEADS, head_dim)
    scores = jnp.einsum('bqhd,bkhd->bhqk', projected[:, :, 0], projected[:, :, 1], precision=HIGHEST) * (1.0 / math.sqrt(head_dim))
    valid_key = jnp.arange(span_len, dtype=jnp.int32)[None, :] < length[:, None]
    scores = low_back(jnp.where(valid_key[:, None, None, :], scores, NEGATIVE))
    maxima = lax.optimization_barrier(jnp.max(scores, -1, keepdims=True))
    powers = jnp.exp(scores - maxima)
    attention = low(powers / lax.optimization_barrier(jnp.sum(powers, -1, keepdims=True)))
    mixed_heads = low(low_back(jnp.einsum('bhqk,bkhd->bqhd', attention, projected[:, :, 2], precision=HIGHEST)))
    after_attn = flat_rows + low_back(matmul(mixed_heads.reshape(number * span_len, model_dim), weight_out))
    mlp_in = low(layer_norm(after_attn, gain_m))
    hidden = low(jax.nn.gelu(low_back(matmul(mlp_in, weight_up) + bias_up), approximate=False))
    result = after_attn + low_back(matmul(hidden, weight_down))
    valid_mask = valid_key.astype(jnp.float32)[:, :, None]
    return lax.optimization_barrier(jnp.sum(result.reshape(number, span_len, model_dim) * valid_mask, 1)) / length.astype(jnp.float32)[:, None]

def half_loss(scores, own_pair):
    maxima = lax.optimization_barrier(jnp.max(scores, -1, keepdims=True))
    log_total = maxima[:, 0] + jnp.log(lax.optimization_barrier(jnp.sum(jnp.exp(scores - maxima), -1)))
    return log_total - lax.optimization_barrier(jnp.sum(scores * own_pair, -1))

def reference(images, groups, captions, cap_lengths, img_gain_a, img_w_qkv, img_b_qv, img_w_out, img_gain_m, img_w_up, img_b_up, img_w_down, gain_attn, w_qkv, b_qv, w_out, gain_mlp, w_up, b_up, w_down, text_proj):
    frozen = tuple((member.astype(jnp.float32) for member in (img_gain_a, img_w_qkv, img_b_qv, img_w_out, img_gain_m, img_w_up, img_b_up, img_w_down)))
    image_blocks = PAIRS // IMG_BLK
    img_len = jnp.where(groups == 1, ILEN, LOWLEN).astype(jnp.int32)

    def image_block(block_item):
        pixels, length = block_item
        pooled = residual_block(pixels.astype(jnp.float32), length, frozen)
        return low(pooled * lax.rsqrt(lax.optimization_barrier(jnp.sum(pooled * pooled, -1, keepdims=True)) + EPS))
    image_emb = lax.map(image_block, (images.reshape(image_blocks, IMG_BLK, ILEN, D), img_len.reshape(image_blocks, IMG_BLK))).reshape(PAIRS, D)
    projection = text_proj.astype(jnp.float32)
    text_blocks = PAIRS // P_DEV

    def loss_of(params, caption_rows):

        def text_block(block_item):
            caption_part, length = block_item
            pooled = residual_block(caption_part, length, params)
            proj_out = low_back(matmul(low(pooled), projection))
            return low(proj_out * lax.rsqrt(lax.optimization_barrier(jnp.sum(proj_out * proj_out, -1, keepdims=True)) + EPS))
        text_emb = lax.map(jax.checkpoint(text_block), (caption_rows.reshape(text_blocks, P_DEV, CAP, D), cap_lengths.reshape(text_blocks, P_DEV))).reshape(PAIRS, D)

        def pair_block(block_item):
            text_rows, image_rows, block_index = block_item
            columns = jnp.arange(PAIRS, dtype=jnp.int32)
            own_pair = (columns[None, :] == block_index * P_DEV + jnp.arange(P_DEV, dtype=jnp.int32)[:, None]).astype(jnp.float32)
            text_scores = low_back(matmul(text_rows, image_emb.T) * SCALE)
            image_scores = low_back(matmul(image_rows, text_emb.T) * SCALE)
            return 0.5 * half_loss(text_scores, own_pair) + 0.5 * half_loss(image_scores, own_pair)
        losses = lax.map(jax.checkpoint(pair_block), (text_emb.reshape(text_blocks, P_DEV, D), image_emb.reshape(text_blocks, P_DEV, D), jnp.arange(text_blocks, dtype=jnp.int32)))
        return losses.reshape(PAIRS)
    params = tuple((member.astype(jnp.float32) for member in (gain_attn, w_qkv, b_qv, w_out, gain_mlp, w_up, b_up, w_down)))
    losses, pullback = jax.vjp(loss_of, params, captions.astype(jnp.float32))
    grad_params, grad_caption = pullback(jnp.ones_like(losses))
    return (losses, grad_caption, grad_params[0], grad_params[1], grad_params[2], grad_params[3], grad_params[4], grad_params[5], grad_params[6], grad_params[7])
```

```python
import math

import jax
import jax.numpy as jnp
from jax import lax
from jax.sharding import PartitionSpec as P

D = 768
HEADS = 12
ILEN = 145
LOWLEN = 50
CAP = 16
IMG_BLK = 4


SCALE = 100.0
EPS = 1e-06
NEGATIVE = -1e30


def contract(left_side, right_side, left_dim, right_dim):
    return lax.dot_general(
        left_side,
        right_side,
        (((left_dim,), (right_dim,)), ((), ())),
        preferred_element_type=jnp.float32,
    )


def normalize(values):
    center = values - jnp.mean(values, -1, keepdims=True)
    inverse = lax.rsqrt(jnp.mean(center * center, -1, keepdims=True) + EPS)
    return (center * inverse, inverse)


def norm_back(grad_normed, normed, inverse):
    return inverse * (
        grad_normed
        - jnp.mean(grad_normed, -1, keepdims=True)
        - normed * jnp.mean(grad_normed * normed, -1, keepdims=True)
    )


def gelu_slope(values):
    return 0.5 * (1.0 + jax.scipy.special.erf(values / math.sqrt(2.0))) + values * jnp.exp(
        -0.5 * values * values
    ) / math.sqrt(2.0 * math.pi)


def block_forward(tokens, length, params):
    gain_a, weight_qkv, bias_qv, weight_out, gain_m, weight_up, bias_up, weight_down = params
    number, span_len, model_dim = tokens.shape
    head_dim = model_dim // HEADS
    scale_q = 1.0 / math.sqrt(head_dim)
    flat_rows = tokens.reshape(number * span_len, model_dim).astype(jnp.float32)
    normed_one, inverse_one = normalize(flat_rows)
    input_low = (normed_one * gain_a.astype(jnp.float32)).astype(jnp.bfloat16)
    bias_full = jnp.concatenate(
        [
            bias_qv[:model_dim].astype(jnp.float32),
            jnp.zeros((model_dim,), jnp.float32),
            bias_qv[model_dim:].astype(jnp.float32),
        ]
    )
    projected = (
        jnp.dot(input_low, weight_qkv, preferred_element_type=jnp.float32) + bias_full
    ).astype(jnp.bfloat16)
    projected = projected.reshape(number, span_len, 3, HEADS, head_dim)
    query_rows = projected[:, :, 0]
    key_rows = projected[:, :, 1]
    value_rows = projected[:, :, 2]
    valid_key = jnp.arange(span_len, dtype=jnp.int32)[None, :] < length[:, None]
    scores = (
        jnp.einsum("bqhd,bkhd->bhqk", query_rows, key_rows, preferred_element_type=jnp.float32)
        * scale_q
    )
    scores = jnp.where(valid_key[:, None, None, :], scores, NEGATIVE)
    maxima = jnp.max(scores, -1, keepdims=True)
    powers = jnp.exp(scores - maxima)
    attention = powers / jnp.sum(powers, -1, keepdims=True)
    attn_low = attention.astype(jnp.bfloat16)
    mixed_heads = (
        jnp.einsum("bhqk,bkhd->bqhd", attn_low, value_rows, preferred_element_type=jnp.float32)
        .astype(jnp.bfloat16)
        .reshape(number * span_len, model_dim)
    )
    after_attn = flat_rows + jnp.dot(mixed_heads, weight_out, preferred_element_type=jnp.float32)
    normed_two, inverse_two = normalize(after_attn)
    mlp_in = (normed_two * gain_m.astype(jnp.float32)).astype(jnp.bfloat16)
    pre_act = jnp.dot(mlp_in, weight_up, preferred_element_type=jnp.float32) + bias_up.astype(
        jnp.float32
    )
    hidden = jax.nn.gelu(pre_act, approximate=False).astype(jnp.bfloat16)
    result = after_attn + jnp.dot(hidden, weight_down, preferred_element_type=jnp.float32)
    valid_mask = valid_key.astype(jnp.float32)[:, :, None]
    pooled = (
        jnp.sum(result.reshape(number, span_len, model_dim) * valid_mask, 1)
        / length.astype(jnp.float32)[:, None]
    )
    saved = (
        normed_one,
        inverse_one,
        input_low,
        query_rows,
        key_rows,
        value_rows,
        attention,
        attn_low,
        mixed_heads,
        normed_two,
        inverse_two,
        mlp_in,
        pre_act,
        hidden,
        valid_key,
    )
    return (pooled, saved)


def image_embed(pixels, length, params):
    pooled, saved = block_forward(pixels, length, params)
    return (pooled * lax.rsqrt(jnp.sum(pooled * pooled, -1, keepdims=True) + EPS)).astype(
        jnp.bfloat16
    )


MOST_PAIRS = 2048


def dp_bits(size):
    bits, bit = [], 1
    while bit < size:
        bits.append(bit)
        bit *= 2
    return bits


def swap(values, axis, bit):
    size = lax.axis_size(axis)
    return lax.ppermute(values, axis, [(place, place ^ bit) for place in range(size)])


def gather_relative(values):
    for bit in reversed(dp_bits(lax.axis_size("dp"))):
        values = jnp.concatenate([values, swap(values, "dp", bit)], 0)
    return jnp.concatenate([values, swap(values, "rep", 1)], 0)


def relative_chunks():
    bits = dp_bits(lax.axis_size("dp"))
    offsets = [0]
    for bit in reversed(bits):
        offsets = offsets + [entry + bit for entry in offsets]
    places = sorted(range(len(offsets)), key=lambda place: place)
    table = []
    for place in places:
        total, rest = 0, place
        for level, bit in enumerate(reversed(bits)):
            if place & (1 << level):
                total += bit
        table.append(total)
    return lax.axis_index("dp") ^ jnp.array(table, jnp.int32)


def reduce_halving(chunks):
    for bit in dp_bits(lax.axis_size("dp")):
        half = chunks.shape[0] // 2
        arrived = swap(chunks[half:].astype(jnp.bfloat16), "dp", bit)
        chunks = chunks[:half] + arrived.astype(jnp.float32)
    return chunks


def spread_doubling(chunks):
    for bit in reversed(dp_bits(lax.axis_size("dp"))):
        chunks = jnp.concatenate([chunks, swap(chunks, "dp", bit)], 0)
    return chunks


def sum_over_chips(own_half, order):
    size = lax.axis_size("dp")
    rows, columns = own_half.shape
    chunks = own_half.reshape(size, rows // size, columns)[order]
    done = spread_doubling(reduce_halving(chunks).astype(jnp.bfloat16))
    return done[jnp.argsort(order)].reshape(rows, columns).astype(jnp.float32)


def sum_over_pair(left_side, right_side):
    half = right_side.shape[1] // 2
    mine = lax.axis_index("rep")
    own_side = lax.dynamic_slice_in_dim(right_side, mine * half, half, 1)
    other_side = lax.dynamic_slice_in_dim(right_side, (1 - mine) * half, half, 1)
    arrived = swap(contract(left_side, other_side, 0, 0).astype(jnp.bfloat16), "rep", 1)
    return contract(left_side, own_side, 0, 0) + arrived.astype(jnp.float32)


def softmax_parts(scores, axis):
    maxima = jnp.max(scores, axis, keepdims=True)
    powers = jnp.exp(scores - maxima)
    totals = jnp.sum(powers, axis, keepdims=True)
    return powers / totals, maxima + jnp.log(totals)


def text_unit(pooled_low, text_proj):
    proj_out = jnp.dot(pooled_low, text_proj, preferred_element_type=jnp.float32)
    inverse_z = lax.rsqrt(jnp.sum(proj_out * proj_out, -1, keepdims=True) + EPS)
    return proj_out * inverse_z, inverse_z


def branch_grad(grad_unit, unit_text, inverse_z, text_proj, lengths):
    grad_projout = (
        inverse_z * (grad_unit - unit_text * jnp.sum(unit_text * grad_unit, -1, keepdims=True))
    ).astype(jnp.bfloat16)
    return contract(grad_projout, text_proj, 1, 1) / lengths


def loss_whole(pooled_all, image_all, text_proj, lengths_all, local_pairs):
    unit_text, inverse_z = text_unit(pooled_all, text_proj)
    total = pooled_all.shape[0]
    scores = contract(unit_text.astype(jnp.bfloat16), image_all, 1, 1) * SCALE
    by_text, text_total = softmax_parts(scores, 1)
    by_image, image_total = softmax_parts(scores, 0)
    same = (
        jnp.arange(total, dtype=jnp.int32)[:, None] == jnp.arange(total, dtype=jnp.int32)[None, :]
    ).astype(jnp.float32)
    own = jnp.sum(scores[:local_pairs] * same[:local_pairs], -1)
    pair_loss = 0.5 * (text_total[:local_pairs, 0] - own) + 0.5 * (
        image_total[0, :local_pairs] - own
    )
    sgrad = (0.5 * (by_text - same) + 0.5 * (by_image - same)).astype(jnp.bfloat16)
    grad_unit = contract(sgrad, image_all, 1, 0) * SCALE
    grads = branch_grad(grad_unit, unit_text, inverse_z, text_proj, lengths_all)
    return pair_loss, grads[:local_pairs], grads.astype(jnp.bfloat16)


def loss_rows(pooled_all, image_all, text_proj, lengths_all, local_pairs):
    unit_all, inverse_all = text_unit(pooled_all, text_proj)
    unit_text, inverse_z = unit_all[:local_pairs], inverse_all[:local_pairs]
    text_all = unit_all.astype(jnp.bfloat16)
    total = pooled_all.shape[0]
    text_scores = contract(text_all[:local_pairs], image_all, 1, 1) * SCALE
    image_scores = contract(image_all[:local_pairs], text_all, 1, 1) * SCALE
    by_text, text_total = softmax_parts(text_scores, 1)
    image_total = softmax_parts(image_scores, 1)[1]
    every_total = gather_relative(image_total)
    same = (
        jnp.arange(local_pairs, dtype=jnp.int32)[:, None]
        == jnp.arange(total, dtype=jnp.int32)[None, :]
    ).astype(jnp.float32)
    own = jnp.sum(text_scores * same, -1)
    pair_loss = 0.5 * (text_total[:, 0] - own) + 0.5 * (image_total[:, 0] - own)
    by_image = jnp.exp(text_scores - every_total[:, 0][None, :])
    sgrad = (0.5 * (by_text - same) + 0.5 * (by_image - same)).astype(jnp.bfloat16)
    grad_unit = contract(sgrad, image_all, 1, 0) * SCALE
    grads = branch_grad(grad_unit, unit_text, inverse_z, text_proj, lengths_all[:local_pairs])
    return pair_loss, grads, grads.astype(jnp.bfloat16)


def local(
    images,
    groups,
    captions,
    cap_lengths,
    img_gain_a,
    img_w_qkv,
    img_b_qv,
    img_w_out,
    img_gain_m,
    img_w_up,
    img_b_up,
    img_w_down,
    gain_attn,
    w_qkv,
    b_qv,
    w_out,
    gain_mlp,
    w_up,
    b_up,
    w_down,
    text_proj,
):
    frozen = (
        lax.all_gather(img_gain_a, "rep", axis=0, tiled=True),
        lax.all_gather(img_w_qkv, "rep", axis=0, tiled=True),
        lax.all_gather(img_b_qv, "rep", axis=0, tiled=True),
        lax.all_gather(img_w_out, "rep", axis=0, tiled=True),
        lax.all_gather(img_gain_m, "rep", axis=0, tiled=True),
        lax.all_gather(img_w_up, "rep", axis=0, tiled=True),
        lax.all_gather(img_b_up, "rep", axis=0, tiled=True),
        lax.all_gather(img_w_down, "rep", axis=0, tiled=True),
    )
    local_pairs = images.shape[0]
    ordering = jnp.argsort(groups, stable=True)
    sorted_len = jnp.where(groups[ordering] == 1, ILEN, LOWLEN).astype(jnp.int32)
    blocks = local_pairs // IMG_BLK
    stacked = images[ordering].reshape(blocks, IMG_BLK, ILEN, D)

    def image_block(block_item):
        pixels, length = block_item
        return lax.cond(
            jnp.max(length) > LOWLEN,
            lambda: image_embed(pixels, length, frozen),
            lambda: image_embed(pixels[:, :LOWLEN], length, frozen),
        )

    params = (gain_attn, w_qkv, b_qv, w_out, gain_mlp, w_up, b_up, w_down)
    pooled, saved = block_forward(captions, cap_lengths, params)
    (
        normed_one,
        inverse_one,
        input_low,
        query_rows,
        key_rows,
        value_rows,
        attention,
        attn_low,
        mixed_heads,
        normed_two,
        inverse_two,
        mlp_in,
        pre_act,
        hidden,
        valid_key,
    ) = saved
    valid_rows = valid_key.astype(jnp.float32)[:, :, None]
    hidden_sum = jnp.sum(
        hidden.astype(jnp.float32).reshape(local_pairs, CAP, -1) * valid_rows, 1
    ).astype(jnp.bfloat16)
    slope = gelu_slope(pre_act).reshape(local_pairs, CAP, -1) * valid_rows
    lengths = cap_lengths.astype(jnp.float32)[:, None]
    total_pairs = local_pairs * lax.axis_size("dp") * lax.axis_size("rep")
    whole = total_pairs <= MOST_PAIRS
    sent = [
        pooled.astype(jnp.bfloat16),
        jnp.broadcast_to(lengths, (local_pairs, 128)).astype(jnp.bfloat16),
    ]
    early = gather_relative(jnp.concatenate(sent + [hidden_sum] if whole else sent, 1))
    sorted_emb = lax.map(image_block, (stacked, sorted_len.reshape(blocks, IMG_BLK))).reshape(
        local_pairs, D
    )
    image_emb = sorted_emb[jnp.argsort(ordering)]
    image_all = gather_relative(image_emb)
    pooled_all = early[:, :D]
    lengths_all = early[:, D : D + 1].astype(jnp.float32)
    loss_of = loss_whole if whole else loss_rows
    pair_loss, grad_pooled, branch_all = loss_of(
        pooled_all, image_all, text_proj, lengths_all, local_pairs
    )
    order = relative_chunks()
    if whole:
        half_dim = D // 2
        grad_w_down = contract(
            early[:, D + 128 :],
            lax.dynamic_slice_in_dim(branch_all, lax.axis_index("rep") * half_dim, half_dim, 1),
            0,
            0,
        )
    else:
        grad_w_down = sum_over_chips(sum_over_pair(hidden_sum, branch_all), order)
    rows_total = local_pairs * CAP
    grad_rows = (grad_pooled[:, None, :] * valid_rows).reshape(rows_total, D)
    grad_hidden = contract(branch_all[:local_pairs], w_down, 1, 1)
    grad_pre = (grad_hidden[:, None, :] * slope).astype(jnp.bfloat16).reshape(rows_total, -1)
    grad_b_up = jnp.sum(grad_pre.astype(jnp.float32), 0)
    grad_w_up = sum_over_chips(sum_over_pair(mlp_in, grad_pre), order)
    grad_mlp_in = contract(grad_pre, w_up, 1, 1)
    grad_gain_mlp = jnp.sum(grad_mlp_in * normed_two, 0)
    grad_after = grad_rows + norm_back(
        grad_mlp_in * gain_mlp.astype(jnp.float32), normed_two, inverse_two
    )
    grad_out_low = grad_after.astype(jnp.bfloat16)
    grad_w_out = sum_over_chips(sum_over_pair(mixed_heads, grad_out_low), order)
    head_dim = D // HEADS
    scale_q = 1.0 / math.sqrt(head_dim)
    grad_mixed = (
        contract(grad_out_low, w_out, 1, 1)
        .astype(jnp.bfloat16)
        .reshape(local_pairs, CAP, HEADS, head_dim)
    )
    grad_attention = jnp.einsum(
        "bqhd,bkhd->bhqk", grad_mixed, value_rows, preferred_element_type=jnp.float32
    )
    grad_value = jnp.einsum(
        "bhqk,bqhd->bkhd", attn_low, grad_mixed, preferred_element_type=jnp.float32
    )
    grad_scores = (
        attention * (grad_attention - jnp.sum(grad_attention * attention, -1, keepdims=True))
    ).astype(jnp.bfloat16)
    grad_query = (
        jnp.einsum("bhqk,bkhd->bqhd", grad_scores, key_rows, preferred_element_type=jnp.float32)
        * scale_q
    )
    grad_key = (
        jnp.einsum("bhqk,bqhd->bkhd", grad_scores, query_rows, preferred_element_type=jnp.float32)
        * scale_q
    )
    grad_projected = (
        jnp.stack([grad_query, grad_key, grad_value], 2)
        .reshape(rows_total, 3 * D)
        .astype(jnp.bfloat16)
    )
    projected_f32 = grad_projected.astype(jnp.float32)
    grad_b_qv = jnp.concatenate(
        [jnp.sum(projected_f32[:, :D], 0), jnp.sum(projected_f32[:, 2 * D :], 0)]
    )
    grad_w_qkv = sum_over_chips(sum_over_pair(input_low, grad_projected), order)
    grad_input = contract(grad_projected, w_qkv, 1, 1)
    grad_gain_attn = jnp.sum(grad_input * normed_one, 0)
    caption_grad = (
        grad_after + norm_back(grad_input * gain_attn.astype(jnp.float32), normed_one, inverse_one)
    ).reshape(local_pairs, CAP, D)
    small = (grad_gain_attn, grad_b_qv, grad_gain_mlp, grad_b_up)
    packed = jnp.concatenate([entry.reshape(2, -1) for entry in small], 1)
    packed = lax.psum(packed, ("dp", "rep"))[lax.axis_index("rep")]
    summed, start = [], 0
    for entry in small:
        size = entry.shape[0] // 2
        summed.append(packed[start : start + size])
        start += size
    return (
        pair_loss,
        caption_grad,
        summed[0],
        grad_w_qkv,
        summed[1],
        grad_w_out,
        summed[2],
        grad_w_up,
        summed[3],
        grad_w_down,
    )


def solution(mesh):
    in_specs = (
        P(("dp", "rep"), None, None),
        P(("dp", "rep")),
        P(("dp", "rep"), None, None),
        P(("dp", "rep")),
        P("rep"),
        P("rep", None),
        P("rep"),
        P("rep", None),
        P("rep"),
        P("rep", None),
        P("rep"),
        P("rep", None),
        P(),
        P(),
        P(),
        P(),
        P(),
        P(),
        P(),
        P(),
        P(),
    )
    out_specs = (
        P(("dp", "rep")),
        P(("dp", "rep"), None, None),
        P("rep"),
        P(None, "rep"),
        P("rep"),
        P(None, "rep"),
        P("rep"),
        P(None, "rep"),
        P("rep"),
        P(None, "rep"),
    )
    return jax.shard_map(local, mesh=mesh, in_specs=in_specs, out_specs=out_specs, check_vma=False)
```

```python
import functools
import math

import jax
import jax.numpy as jnp
from jax import lax
from jax.experimental import pallas as pl
from jax.experimental.pallas import tpu as pltpu
from jax.sharding import PartitionSpec as P

D = 768
HEADS = 12
FF = 3072
ILEN = 145
LOWLEN = 50
CAP = 16

SCALE = 100.0
EPS = 1e-06
NEGATIVE = -1e30
LOG2E = math.log2(math.e)
MOST_PAIRS = 2048
VMEM_BYTES = 58 * 1024 * 1024

UNIT = 160
UNITS = 2
PART = 48
SPAN = 29
QB = 128
BW = 3 * D // 2 + D // 2 + 128
EARLY = D + 128
CHUNKS = 16

f32 = jnp.float32
bf16 = jnp.bfloat16


def dot(left_side, right_side):
    return jnp.dot(left_side, right_side, preferred_element_type=f32)


def dot_nt(left_side, right_side):
    return lax.dot_general(
        left_side, right_side, (((1,), (1,)), ((), ())), preferred_element_type=f32
    )


def dot_tn(left_side, right_side):
    return lax.dot_general(
        left_side, right_side, (((0,), (0,)), ((), ())), preferred_element_type=f32
    )


def normalize(values):
    center = values - jnp.mean(values, -1, keepdims=True)
    inverse = lax.rsqrt(jnp.mean(center * center, -1, keepdims=True) + EPS)
    return center * inverse, inverse


def norm_back(grad, normed, inverse):
    return inverse * (
        grad
        - jnp.mean(grad, -1, keepdims=True)
        - normed * jnp.mean(grad * normed, -1, keepdims=True)
    )


def normal_cdf(values):
    return 0.5 + 0.5 * lax.erf(values * (1.0 / math.sqrt(2.0)))


def split_low(values):
    big = values.astype(bf16)
    return big, (values - big.astype(f32)).astype(bf16)


def tower_kernel(
    groups_ref,
    mine_ref,
    x_hbm,
    vec_own_ref,
    vec_other_ref,
    qkv_own,
    qkv_other,
    out_own,
    out_other,
    up_own,
    up_other,
    down_own,
    down_other,
    emb_ref,
    order,
    x_ref,
    x_wide,
    wqkv,
    wout,
    wup,
    wdown,
    gain_a,
    bqkv,
    gain_m,
    bup,
    xs,
    qkv,
    mixed,
    asum,
    hsum,
    aparts,
    hparts,
    sems,
):
    total = x_ref.shape[1]
    pitch = total + 8
    mine = mine_ref[0]
    copies = []
    for k in range(ILEN // SPAN):
        span = pl.ds(k * SPAN, SPAN)
        copies.append(pltpu.make_async_copy(x_hbm.at[span], x_ref.at[span], sems.at[8 + k]))
    for k, (own, other, whole) in enumerate(
        (
            (qkv_own, qkv_other, wqkv),
            (out_own, out_other, wout),
            (up_own, up_other, wup),
            (down_own, down_other, wdown),
        )
    ):
        half = own.shape[0]
        copies.append(
            pltpu.make_async_copy(own, whole.at[pl.ds(mine * half, half)], sems.at[2 * k])
        )
        copies.append(
            pltpu.make_async_copy(
                other, whole.at[pl.ds((1 - mine) * half, half)], sems.at[2 * k + 1]
            )
        )
    for copy in copies:
        copy.start()

    vec_own = vec_own_ref[...].astype(f32)
    vec_other = vec_other_ref[...].astype(f32)
    low = jnp.where(mine == 0, vec_own, vec_other)
    high = jnp.where(mine == 0, vec_other, vec_own)
    start = 0
    for dest, size, at in (
        (gain_a, D // 2, (0, D // 2)),
        (bqkv, D, (0, 2 * D)),
        (gain_m, D // 2, (0, D // 2)),
        (bup, FF // 2, (0, FF // 2)),
    ):
        dest[:, at[0] : at[0] + size] = low[:, start : start + size]
        dest[:, at[1] : at[1] + size] = high[:, start : start + size]
        start += size
    bqkv[:, D : 2 * D] = jnp.zeros((1, D), f32)

    def count(i, found):
        return found + groups_ref[i]

    n_hi = lax.fori_loop(0, total, count, 0)

    def place_one(i, state):
        hi, lo = state
        group = groups_ref[i]
        order[jnp.where(group == 1, hi, lo)] = i
        return hi + group, lo + 1 - group

    lax.fori_loop(0, total, place_one, (0, n_hi))
    n_units = n_hi + (total - n_hi + 2) // 3

    xs[...] = jnp.zeros_like(xs)
    first = lax.broadcasted_iota(jnp.int32, (1, 128), 1) < 64
    key_at = lax.broadcasted_iota(jnp.int32, (UNIT, UNIT), 1)
    row_at = lax.broadcasted_iota(jnp.int32, (UNIT, UNIT), 0)
    sub = lax.broadcasted_iota(jnp.int32, (8, 1), 0)

    def place(unit, k):
        last = jnp.minimum(unit, n_units - 1)
        is_hi = last < n_hi
        where = jnp.where(is_hi, last, n_hi + 3 * (last - n_hi) + k)
        return order[jnp.minimum(where, total - 1)], is_hi

    def keep_parts(values, j, dest, col, width):
        rows = values.reshape(UNIT // 8, 8, width)
        parts = [
            jnp.sum(rows[0:6], 0),
            rows[6],
            jnp.sum(rows[7:12], 0),
            rows[12],
            jnp.sum(rows[13:18], 0),
            rows[18],
        ]
        for k, part in enumerate(parts):
            dest[j * PART + k * 8 : j * PART + k * 8 + 8, col : col + width] = part

    loads = copies[: ILEN // SPAN]
    copies = copies[ILEN // SPAN :]

    def widen(t, carry):
        for panel in range(D // 128):
            x_wide[panel, pl.ds(pl.multiple_of(t * pitch, 8), total), :] = x_ref[
                t, :, panel * 128 : (panel + 1) * 128
            ].astype(f32)
        return carry

    for k, load in enumerate(loads):
        load.wait()
        lax.fori_loop(k * SPAN, (k + 1) * SPAN, widen, 0)
    for copy in copies[:2]:
        copy.wait()

    def body(step, carry):
        for j in range(UNITS):
            unit = step * UNITS + j
            one, is_hi = place(unit, 0)
            two, three = place(unit, 1)[0], place(unit, 2)[0]
            base = j * UNIT

            @pl.when(is_hi)
            def _():
                for panel in range(D // 128):
                    xs[base : base + ILEN, panel * 128 : (panel + 1) * 128] = x_wide[
                        panel, pl.ds(one, ILEN, stride=pitch), :
                    ]

            @pl.when(jnp.logical_not(is_hi))
            def _():
                for k, index in enumerate((one, two, three)):
                    for panel in range(D // 128):
                        xs[
                            base + LOWLEN * k : base + LOWLEN * (k + 1),
                            panel * 128 : (panel + 1) * 128,
                        ] = x_wide[panel, pl.ds(index, LOWLEN, stride=pitch), :]

        low_rows = (normalize(xs[...])[0] * gain_a[...]).astype(bf16)
        for col in range(0, 3 * D, 256):
            values = dot(low_rows, wqkv[:, col : col + 256]) + bqkv[:, col : col + 256]
            if col < D:
                values = values * (LOG2E / 8.0)
            qkv[:, col : col + 256] = values.astype(bf16)

        @pl.when(step == 0)
        def _():
            for copy in copies[2:6]:
                copy.wait()

        for j in range(UNITS):
            is_hi = place(step * UNITS + j, 0)[1]
            base = j * UNIT
            key_seg = jnp.where(key_at < LOWLEN, 0, jnp.where(key_at < 2 * LOWLEN, 1, 2))
            row_seg = jnp.where(row_at < LOWLEN, 0, jnp.where(row_at < 2 * LOWLEN, 1, 2))
            short_ok = jnp.logical_and(key_seg == row_seg, key_at < 3 * LOWLEN)
            allowed = jnp.where(
                is_hi, (key_at < ILEN).astype(jnp.int32), short_ok.astype(jnp.int32)
            )
            bias = jnp.where(allowed > 0, 0.0, NEGATIVE)
            for p in range(HEADS // 2):
                lanes = slice(p * 128, (p + 1) * 128)
                query = qkv[base : base + UNIT, lanes]
                key = qkv[base : base + UNIT, D + p * 128 : D + (p + 1) * 128]
                value = qkv[base : base + UNIT, 2 * D + p * 128 : 2 * D + (p + 1) * 128]
                value_one = jnp.concatenate([value, jnp.ones_like(value)], 1)
                outs = []
                for h in range(2):
                    head = first if h == 0 else jnp.logical_not(first)
                    scores = dot_nt(jnp.where(head, query, jnp.zeros_like(query)), key) + bias
                    powers = jnp.exp2(scores - jnp.max(scores, 1, keepdims=True)).astype(bf16)
                    summed = dot(powers, value_one)
                    outs.append(summed[:, :128] / summed[:, 128:])
                mixed[base : base + UNIT, lanes] = jnp.where(first, outs[0], outs[1]).astype(bf16)
        for col in range(0, D, 256):
            xs[:, col : col + 256] += dot(mixed[...], wout[:, col : col + 256])
        for j in range(UNITS):
            keep_parts(xs[j * UNIT : (j + 1) * UNIT, :], j, aparts, 0, D)
        low_two = (normalize(xs[...])[0] * gain_m[...]).astype(bf16)
        width = 1024
        for col in range(0, FF, width):
            pre_act = dot(low_two, wup[:, col : col + width]) + bup[:, col : col + width]
            hidden = pre_act * normal_cdf(pre_act)
            for j in range(UNITS):
                keep_parts(hidden[j * UNIT : (j + 1) * UNIT], j, hparts, col, width)
        for j in range(UNITS):
            unit = step * UNITS + j
            one, is_hi = place(unit, 0)
            two, three = place(unit, 1)[0], place(unit, 2)[0]

            def rows_of(index):
                return pl.ds(pl.multiple_of(index * 8, 8), 8)

            @pl.when(is_hi)
            def _():
                for src, dest in ((aparts, asum), (hparts, hsum)):
                    part = [src[j * PART + k * 8 : j * PART + k * 8 + 8, :] for k in range(6)]
                    dest[rows_of(one), :] = (
                        (part[0] + part[1])
                        + (part[2] + part[3])
                        + (part[4] + jnp.where(sub < 1, part[5], 0.0))
                    )

            @pl.when(jnp.logical_not(is_hi))
            def _():
                for src, dest in ((aparts, asum), (hparts, hsum)):
                    part = [src[j * PART + k * 8 : j * PART + k * 8 + 8, :] for k in range(6)]
                    dest[rows_of(three), :] = (
                        jnp.where(sub < 4, 0.0, part[3])
                        + part[4]
                        + jnp.where(sub < 6, part[5], 0.0)
                    )
                    dest[rows_of(two), :] = (
                        jnp.where(sub < 2, 0.0, part[1])
                        + part[2]
                        + jnp.where(sub < 4, part[3], 0.0)
                    )
                    dest[rows_of(one), :] = part[0] + jnp.where(sub < 2, part[1], 0.0)

        return carry

    lax.fori_loop(0, (n_units + UNITS - 1) // UNITS, body, 0)
    for copy in copies[6:]:
        copy.wait()
    which = lax.broadcasted_iota(jnp.int32, (total, 128), 0)
    scale = jnp.zeros((total, 128), f32)
    for i in range(total):
        scale = jnp.where(
            which == i, jnp.where(groups_ref[i] == 1, 1.0 / ILEN, 1.0 / LOWLEN), scale
        )
    scale = scale[:, 0:1]
    big, rest = split_low(jnp.sum(hsum[...].reshape(total, 8, FF), 1) * scale)
    product = dot(jnp.concatenate([big, rest], 0), wdown[...])
    pooled = jnp.sum(asum[...].reshape(total, 8, D), 1) * scale + product[:total] + product[total:]
    emb_ref[...] = (
        pooled * lax.rsqrt(jnp.sum(pooled * pooled, -1, keepdims=True) + EPS)
    ).astype(bf16)


VM = pl.BlockSpec(memory_space=pltpu.VMEM)
SM = pl.BlockSpec(memory_space=pltpu.SMEM)
ANY = pl.BlockSpec(memory_space=pl.ANY)
PARAMS = pltpu.CompilerParams(vmem_limit_bytes=VMEM_BYTES)


def image_tower(images, groups, mine, vec_own, vec_other, weights):
    number = images.shape[1]
    rows = UNITS * UNIT
    flops = number * 100 * 2 * (4 * D * D + D * FF)
    return pl.pallas_call(
        tower_kernel,
        out_shape=jax.ShapeDtypeStruct((number, D), bf16),
        in_specs=[SM, SM, ANY, VM, VM] + [ANY] * 8,
        out_specs=VM,
        scratch_shapes=[
            pltpu.SMEM((number,), jnp.int32),
            pltpu.VMEM(images.shape, bf16),
            pltpu.VMEM((D // 128, ILEN * (number + 8), 128), f32),
            pltpu.VMEM((D, 3 * D), bf16),
            pltpu.VMEM((D, D), bf16),
            pltpu.VMEM((D, FF), bf16),
            pltpu.VMEM((FF, D), bf16),
            pltpu.VMEM((1, D), f32),
            pltpu.VMEM((1, 3 * D), f32),
            pltpu.VMEM((1, D), f32),
            pltpu.VMEM((1, FF), f32),
            pltpu.VMEM((rows, D), f32),
            pltpu.VMEM((rows, 3 * D), bf16),
            pltpu.VMEM((rows, D), bf16),
            pltpu.VMEM((number * 8, D), f32),
            pltpu.VMEM((number * 8, FF), f32),
            pltpu.VMEM((UNITS * PART, D), f32),
            pltpu.VMEM((UNITS * PART, FF), f32),
            pltpu.SemaphoreType.DMA((8 + ILEN // SPAN,)),
        ],
        compiler_params=PARAMS,
        cost_estimate=pl.CostEstimate(
            flops=flops, bytes_accessed=24 * 1024 * 1024, transcendentals=0
        ),
        name="image_tower",
    )(groups, mine, images, vec_own, vec_other, *weights)


def lens_along(lens_ref, start, number):
    owner = lax.broadcasted_iota(jnp.int32, (1, number * CAP), 1) // CAP
    lens = jnp.zeros((1, number * CAP), jnp.int32)
    for c in range(number):
        lens = jnp.where(owner == c, lens_ref[start + c], lens)
    return lens


def score_bias(lens_ref, block):
    per = QB // CAP
    position = lax.broadcasted_iota(jnp.int32, (1, QB), 1) % CAP
    valid = position < lens_along(lens_ref, block * per, per)
    rows = lax.broadcasted_iota(jnp.int32, (QB, QB), 0) // CAP
    columns = lax.broadcasted_iota(jnp.int32, (QB, QB), 1) // CAP
    return jnp.where(jnp.logical_and(rows == columns, valid), 0.0, NEGATIVE)


def forward_kernel(
    lens_ref,
    x_ref,
    vec_ref,
    wqkv_ref,
    wout_ref,
    wup_ref,
    wdown_ref,
    qkv,
    mixed,
    after,
    mlp,
    slope,
    early,
    hidden_low,
    hidden,
):
    rows = x_ref.shape[0]
    number = rows // CAP
    first = lax.broadcasted_iota(jnp.int32, (1, 128), 1) < 64
    normed, _ = normalize(x_ref[...].astype(f32))
    low = (normed * vec_ref[:, 0:D]).astype(bf16)
    for col in range(0, 3 * D, 256):
        values = dot(low, wqkv_ref[:, col : col + 256])
        if col < D:
            values = values + vec_ref[:, D + col : D + col + 256]
        if col >= 2 * D:
            values = values + vec_ref[:, col : col + 256]
        values = values.astype(bf16)
        if col < D:
            values = values * jnp.asarray(0.125, bf16)
        qkv[:, col : col + 256] = values
    def one_block(block, carry):
        bias = score_bias(lens_ref, block)
        span = pl.ds(pl.multiple_of(block * QB, QB), QB)
        for p in range(HEADS // 2):
            query = qkv[span, p * 128 : (p + 1) * 128]
            key = qkv[span, D + p * 128 : D + (p + 1) * 128]
            value = qkv[span, 2 * D + p * 128 : 2 * D + (p + 1) * 128]
            value_one = jnp.concatenate([value, jnp.ones_like(value)], 1)
            outs = []
            for h in range(2):
                head = first if h == 0 else jnp.logical_not(first)
                scores = dot_nt(jnp.where(head, query, jnp.zeros_like(query)), key) * LOG2E + bias
                powers = jnp.exp2(scores - jnp.max(scores, 1, keepdims=True)).astype(bf16)
                summed = dot(powers, value_one)
                outs.append(summed[:, :128] / summed[:, 128:])
            mixed[span, p * 128 : (p + 1) * 128] = jnp.where(first, outs[0], outs[1]).astype(bf16)
        return carry

    lax.fori_loop(0, rows // QB, one_block, 0)
    for col in range(0, D, 256):
        after[:, col : col + 256] = x_ref[:, col : col + 256].astype(f32) + dot(
            mixed[...], wout_ref[:, col : col + 256]
        )
    mlp[...] = (normalize(after[...])[0] * vec_ref[:, 3 * D : 4 * D]).astype(bf16)
    lens = lens_along(lens_ref, 0, number)
    position = lax.broadcasted_iota(jnp.int32, (1, rows), 1)
    owner = (
        lax.broadcasted_iota(jnp.int32, (number, rows), 0)
        == lax.broadcasted_iota(jnp.int32, (number, rows), 1) // CAP
    )
    members = jnp.where(jnp.logical_and(owner, position % CAP < lens), 1.0, 0.0)
    pool = members.astype(bf16)
    count = jnp.sum(members, 1, keepdims=True)
    width = 512
    for col in range(0, FF, width):
        span = slice(col, col + width)
        pre_act = dot(mlp[...], wup_ref[:, span]) + vec_ref[:, 4 * D + col : 4 * D + col + width]
        phi = normal_cdf(pre_act)
        hidden[:, span] = (pre_act * phi).astype(bf16)
        density = jnp.exp2(pre_act * pre_act * (-0.5 * LOG2E)) * (1.0 / math.sqrt(2.0 * math.pi))
        slope[:, span] = (phi + pre_act * density).astype(bf16)
    big, rest = split_low(dot(pool, hidden[...]))
    after_big, after_rest = split_low(after[...])
    pooled = (
        dot(pool, after_big)
        + dot(pool, after_rest)
        + dot(big, wdown_ref[...])
        + dot(rest, wdown_ref[...])
    )
    early[:, 0:D] = (pooled / count).astype(bf16)
    early[:, D:EARLY] = jnp.broadcast_to(count, (number, EARLY - D)).astype(bf16)
    hidden_low[...] = big


def text_forward(captions, lens, vec, w_qkv, w_out, w_up, w_down):
    rows = captions.shape[0]
    shape = jax.ShapeDtypeStruct
    return pl.pallas_call(
        forward_kernel,
        out_shape=[
            shape((rows, 3 * D), bf16),
            shape((rows, D), bf16),
            shape((rows, D), f32),
            shape((rows, D), bf16),
            shape((rows, FF), bf16),
            shape((rows // CAP, EARLY), bf16),
            shape((rows // CAP, FF), bf16),
        ],
        in_specs=[SM] + [VM] * 6,
        out_specs=[VM] * 7,
        scratch_shapes=[pltpu.VMEM((rows, FF), bf16)],
        compiler_params=PARAMS,
        cost_estimate=pl.CostEstimate(
            flops=2 * rows * (4 * D * D + 2 * D * FF),
            bytes_accessed=24 * 1024 * 1024,
            transcendentals=0,
        ),
        name="text_forward",
    )(lens, captions, vec, w_qkv, w_out, w_up, w_down)


def put_chunks(dest, values, place_ref, stream, col):
    rows = values.shape[0] // CHUNKS
    for chunk in range(CHUNKS):
        at = pl.multiple_of(place_ref[stream, chunk] * rows, 16)
        dest[pl.ds(at, rows), col : col + values.shape[1]] = values[
            chunk * rows : (chunk + 1) * rows
        ].astype(dest.dtype)


def up_kernel(
    place_ref, mine_ref, lens_ref, branch_ref, slope_ref, mlp_ref, wdown_ref,
    grad_pre, own, other, grad_bup, grad_hidden, mlp_t,
):
    number = slope_ref.shape[0] // CAP
    half = FF // 2
    mine = mine_ref[0]
    for col in range(0, FF, 512):
        grad_hidden[:, col : col + 512] = dot_nt(branch_ref[...], wdown_ref[col : col + 512, :])
    position = lax.broadcasted_iota(jnp.int32, (CAP, 1), 0)
    for c in range(number):
        span = slice(c * CAP, (c + 1) * CAP)
        keep = jnp.where(position < lens_ref[c], 1.0, 0.0)
        grad_pre[span, :] = (
            grad_hidden[c : c + 1, :] * slope_ref[span, :].astype(f32) * keep
        ).astype(bf16)
    mlp_t[...] = mlp_ref[...].T
    for which, dest in ((1 - mine, other), (mine, own)):
        for col in range(0, half, 384):
            lanes = pl.ds(pl.multiple_of(which * half + col, 128), 384)
            put_chunks(dest, dot(mlp_t[...], grad_pre[:, lanes]), place_ref, 2 * col // half, col)
    for col in range(0, FF, 512):
        grad_bup[:, col : col + 512] = jnp.sum(
            grad_pre[:, col : col + 512].astype(f32), 0, keepdims=True
        )


def up_backward(place, mine, lens, branch, slope, mlp, w_down):
    rows = slope.shape[0]
    shape = jax.ShapeDtypeStruct
    return pl.pallas_call(
        up_kernel,
        out_shape=[
            shape((rows, FF), bf16),
            shape((D, FF // 2), f32),
            shape((D, FF // 2), bf16),
            shape((1, FF), f32),
        ],
        in_specs=[SM, SM, SM] + [VM] * 4,
        out_specs=[VM] * 4,
        scratch_shapes=[pltpu.VMEM((rows // CAP, FF), f32), pltpu.VMEM((D, rows), bf16)],
        compiler_params=PARAMS,
        cost_estimate=pl.CostEstimate(
            flops=2 * rows * D * FF, bytes_accessed=20 * 1024 * 1024, transcendentals=0
        ),
        name="up_backward",
    )(place, mine, lens, branch, slope, mlp, w_down)


def mlp_kernel(
    lens_ref, pre_ref, grad_ref, after_ref, vec_ref, wup_ref, wout_ref,
    grad_after, grad_mixed, grad_gain, grad_out,
):
    number = after_ref.shape[0] // CAP
    grad_mlp = dot_nt(pre_ref[...], wup_ref[...])
    normed_two, inverse_two = normalize(after_ref[...])
    grad_gain[...] = jnp.sum(grad_mlp * normed_two, 0, keepdims=True)
    grad_after[...] = norm_back(grad_mlp * vec_ref[:, 3 * D : 4 * D], normed_two, inverse_two)
    position = lax.broadcasted_iota(jnp.int32, (CAP, 1), 0)
    for c in range(number):
        keep = jnp.where(position < lens_ref[c], 1.0, 0.0)
        grad_after[c * CAP : (c + 1) * CAP, :] += grad_ref[c : c + 1, :] * keep
    grad_out[...] = grad_after[...].astype(bf16)
    for col in range(0, D, 256):
        grad_mixed[:, col : col + 256] = dot_nt(
            grad_out[...], wout_ref[col : col + 256, :]
        ).astype(bf16)


def mlp_backward(lens, grad_pre, grads, after, vec, w_up, w_out):
    rows = after.shape[0]
    shape = jax.ShapeDtypeStruct
    return pl.pallas_call(
        mlp_kernel,
        out_shape=[shape((rows, D), f32), shape((rows, D), bf16), shape((1, D), f32)],
        in_specs=[SM] + [VM] * 6,
        out_specs=[VM] * 3,
        scratch_shapes=[pltpu.VMEM((rows, D), bf16)],
        compiler_params=PARAMS,
        cost_estimate=pl.CostEstimate(
            flops=2 * rows * (D * D + D * FF), bytes_accessed=20 * 1024 * 1024, transcendentals=0
        ),
        name="mlp_backward",
    )(lens, grad_pre, grads, after, vec, w_up, w_out)


def attention_kernel(lens_ref, qkv_ref, mixed_ref, grad_proj, *, start):
    blocks = grad_proj.shape[0] // QB
    first = lax.broadcasted_iota(jnp.int32, (1, 128), 1) < 64

    def one_block(block, carry):
        bias = score_bias(lens_ref, start // QB + block)
        span = pl.ds(pl.multiple_of(start + block * QB, QB), QB)
        dest = pl.ds(pl.multiple_of(block * QB, QB), QB)
        for p in range(HEADS // 2):
            at = p * 128
            query = qkv_ref[span, at : at + 128]
            key = qkv_ref[span, D + at : D + at + 128]
            value = qkv_ref[span, 2 * D + at : 2 * D + at + 128]
            grad = mixed_ref[span, at : at + 128]
            grad_q, grad_k, grad_v = [], [], []
            for h in range(2):
                head = first if h == 0 else jnp.logical_not(first)
                scores = dot_nt(jnp.where(head, query, jnp.zeros_like(query)), key) * LOG2E + bias
                powers = jnp.exp2(scores - jnp.max(scores, 1, keepdims=True))
                attention = powers / jnp.sum(powers, 1, keepdims=True)
                grad_att = dot_nt(jnp.where(head, grad, jnp.zeros_like(grad)), value)
                grad_s = (
                    attention * (grad_att - jnp.sum(grad_att * attention, 1, keepdims=True))
                ).astype(bf16)
                grad_q.append(dot(grad_s, key))
                grad_k.append(dot_tn(grad_s, query))
                grad_v.append(dot_tn(attention.astype(bf16), grad))
            for k, (parts, scale) in enumerate(((grad_q, 0.125), (grad_k, 1.0), (grad_v, 1.0))):
                grad_proj[dest, k * D + at : k * D + at + 128] = (
                    jnp.where(first, parts[0], parts[1]) * scale
                ).astype(bf16)
        return carry

    lax.fori_loop(0, blocks, one_block, 0)


def attention_backward(lens, qkv, grad_mixed, start, rows):
    return pl.pallas_call(
        functools.partial(attention_kernel, start=start),
        out_shape=jax.ShapeDtypeStruct((rows, 3 * D), bf16),
        in_specs=[SM] + [VM] * 2,
        out_specs=VM,
        compiler_params=PARAMS,
        cost_estimate=pl.CostEstimate(
            flops=2 * rows * 3 * D * D, bytes_accessed=16 * 1024 * 1024, transcendentals=0
        ),
        name="attention_backward",
    )(lens, qkv, grad_mixed)


def proj_kernel(
    place_ref, mine_ref, proj_low, proj_high, after_ref, mixed_ref, x_ref, vec_ref,
    gain_ref, bup_ref, wqkv_ref,
    caption_grad, own, other, grad_proj, sums, lhs_t, grad_out,
):
    half_rows = proj_low.shape[0]
    chunk_rows = D // CHUNKS
    mine = mine_ref[0]
    gain_a = vec_ref[:, 0:D]
    grad_proj[0:half_rows, :] = proj_low[...]
    grad_proj[half_rows:, :] = proj_high[...]
    normed_one, inverse_one = normalize(x_ref[...].astype(f32))
    lhs_t[...] = (normed_one * gain_a).astype(bf16).T
    half_out, half_qkv = D // 2, 3 * D // 2
    for which, dest in ((1 - mine, other), (mine, own)):
        for col in range(0, half_qkv, 384):
            lanes = pl.ds(pl.multiple_of(which * half_qkv + col, 128), 384)
            put_chunks(dest, dot(lhs_t[...], grad_proj[:, lanes]), place_ref, col // 768, col)
    lhs_t[...] = mixed_ref[...].T
    grad_out[...] = after_ref[...].astype(bf16)
    for which, dest in ((1 - mine, other), (mine, own)):
        lanes = pl.ds(pl.multiple_of(which * half_out, 128), half_out)
        put_chunks(dest, dot(lhs_t[...], grad_out[:, lanes]), place_ref, 1, half_qkv)
    grad_in = dot_nt(grad_proj[...], wqkv_ref[...])
    sums[:, 0:D] = jnp.sum(grad_in * normed_one, 0, keepdims=True)
    sums[:, D : 2 * D] = jnp.sum(grad_proj[:, 0:D].astype(f32), 0, keepdims=True)
    sums[:, 2 * D : 3 * D] = jnp.sum(grad_proj[:, 2 * D :].astype(f32), 0, keepdims=True)
    sums[:, 3 * D : 4 * D] = gain_ref[...]
    sums[:, 4 * D :] = bup_ref[...]
    caption_grad[...] = after_ref[...] + norm_back(grad_in * gain_a, normed_one, inverse_one)
    for which, dest in ((1 - mine, other), (mine, own)):
        dest[:, BW - 128 :] = jnp.zeros((D, 128), dest.dtype)
        pieces = []
        for start, size in ((0, D), (D, 2 * D), (3 * D, D), (4 * D, FF)):
            for k in range(0, size // 2, 128):
                at = pl.multiple_of(start + which * (size // 2) + k, 128)
                pieces.append(sums[:, pl.ds(at, 128)])
        pieces += [jnp.zeros_like(pieces[0])] * (32 - len(pieces))
        at = pl.multiple_of(place_ref[1, 0] * chunk_rows, 16)
        dest[pl.ds(at, 32), BW - 128 :] = jnp.concatenate(pieces, 0).astype(dest.dtype)


def proj_backward(
    place, mine, proj_low, proj_high, grad_after, mixed, captions, vec, grad_gain, grad_bup, w_qkv
):
    rows = captions.shape[0]
    shape = jax.ShapeDtypeStruct
    return pl.pallas_call(
        proj_kernel,
        out_shape=[shape((rows, D), f32), shape((D, BW), f32), shape((D, BW), bf16)],
        in_specs=[SM, SM] + [VM] * 9,
        out_specs=[VM] * 3,
        scratch_shapes=[
            pltpu.VMEM((rows, 3 * D), bf16),
            pltpu.VMEM((1, 4 * D + FF), f32),
            pltpu.VMEM((D, rows), bf16),
            pltpu.VMEM((rows, D), bf16),
        ],
        compiler_params=PARAMS,
        cost_estimate=pl.CostEstimate(
            flops=2 * rows * 7 * D * D, bytes_accessed=20 * 1024 * 1024, transcendentals=0
        ),
        name="proj_backward",
    )(place, mine, proj_low, proj_high, grad_after, mixed, captions, vec, grad_gain, grad_bup, w_qkv)


def dp_bits():
    bits, bit = [], 1
    while bit < lax.axis_size("dp"):
        bits.append(bit)
        bit *= 2
    return bits


def swap(values, axis, bit):
    size = lax.axis_size(axis)
    return lax.ppermute(values, axis, [(place, place ^ bit) for place in range(size)])


def gather_relative(values):
    bits = dp_bits()
    while bits:
        pair = bits[-2:]
        bits = bits[:-2]
        offsets = [0]
        for bit in pair:
            offsets += [entry + bit for entry in offsets]
        values = jnp.concatenate([swap(values, "dp", k) if k else values for k in offsets], 0)
    return jnp.concatenate([values, swap(values, "rep", 1)], 0)


def relative_chips():
    bits, table = dp_bits(), [0]
    while bits:
        pair = bits[-2:]
        bits = bits[:-2]
        offsets = [0]
        for bit in pair:
            offsets += [entry + bit for entry in offsets]
        table = [entry ^ k for k in offsets for entry in table]
    return table


def chunk_places():
    away = jnp.arange(CHUNKS, dtype=jnp.int32) ^ (lax.axis_index("dp") % CHUNKS)
    one, two, rest = away % 2, away // 2 % 2, away // 4
    return jnp.stack([one * 8 + two * 4 + rest, two * 8 + one * 4 + rest]).astype(jnp.int32)


def reduce_chunks(own, arrived, first_width):
    half, quarter, last = (own.shape[0] // k for k in (2, 4, CHUNKS))
    streams = ((slice(0, first_width), 1, 2), (slice(first_width, None), 2, 1))

    def both(rows, lanes):
        return own[rows, lanes] + arrived[rows, lanes].astype(f32)

    came = [
        swap(both(slice(half, None), lanes).astype(bf16), "dp", bit) for lanes, bit, _ in streams
    ]
    kept = [
        both(slice(0, half), lanes) + got.astype(f32)
        for (lanes, _, _), got in zip(streams, came, strict=True)
    ]
    came = [
        swap(total[quarter:].astype(bf16), "dp", bit)
        for total, (_, _, bit) in zip(kept, streams, strict=True)
    ]
    total = jnp.concatenate(
        [kept[k][:quarter] + came[k].astype(f32) for k in range(2)], 1
    )
    parts = [
        swap(total[k * last : (k + 1) * last].astype(bf16), "dp", 4 * k) for k in (1, 2, 3)
    ]
    total = total[:last] + sum(part.astype(f32) for part in parts)
    for bit in dp_bits()[4:]:
        total = total + swap(total.astype(bf16), "dp", bit).astype(f32)
    return total.astype(bf16)


def spread_chunks(chunk, first_width):
    column = [swap(chunk, "dp", 4 * k) if k else chunk for k in range(4)]
    quarters = []
    for lanes, one, two in ((slice(0, first_width), 1, 2), (slice(first_width, None), 2, 1)):
        mine = jnp.concatenate([piece[:, lanes] for piece in column], 0)
        near = swap(mine, "dp", two)
        quarters += [mine, near, swap(mine, "dp", one), swap(near, "dp", one)]
    return quarters


def unpack_kernel(place_ref, *refs):
    parts = refs[:16]
    g_up, g_qkv, g_out = refs[16:19]
    vectors = refs[19:]
    rows = D // CHUNKS
    place = place_ref[0, 0]
    me = place // 8 + 2 * (place // 4 % 2) + 4 * (place % 4)
    for stream in range(2):
        for quarter in range(4):
            for k in range(4):
                high, low = quarter // 2, quarter % 2
                away = (high + 2 * low if stream == 0 else low + 2 * high) + 4 * k
                chunk = me ^ away
                at = pl.ds(pl.multiple_of(chunk * rows, 16), rows)
                span = slice(k * rows, (k + 1) * rows)
                lanes = slice(stream * FF // 4, (stream + 1) * FF // 4)
                g_up[at, lanes] = parts[stream * 4 + quarter][span, :].astype(f32)
                rest = parts[8 + stream * 4 + quarter][span, :].astype(f32)
                if stream == 0:
                    g_qkv[at, 0:D] = rest
                    continue
                g_qkv[at, D:] = rest[:, : D // 2]
                g_out[at, :] = rest[:, D // 2 : D]

                @pl.when(chunk == 0)
                def _():
                    row = 0
                    for dest in vectors:
                        for lane in range(0, dest.shape[0], 128):
                            dest[lane : lane + 128] = rest[row, D:]
                            row += 1


def unpack(place, ups, rests):
    shape = jax.ShapeDtypeStruct
    return pl.pallas_call(
        unpack_kernel,
        out_shape=[
            shape((D, FF // 2), f32),
            shape((D, 3 * D // 2), f32),
            shape((D, D // 2), f32),
            shape((D // 2,), f32),
            shape((D,), f32),
            shape((D // 2,), f32),
            shape((FF // 2,), f32),
        ],
        in_specs=[SM] + [VM] * 16,
        out_specs=[VM] * 7,
        compiler_params=PARAMS,
        name="unpack",
    )(place, *ups, *rests)


def softmax_parts(scores, axis):
    maxima = jnp.max(scores, axis, keepdims=True)
    powers = jnp.exp(scores - maxima)
    totals = jnp.sum(powers, axis, keepdims=True)
    return powers / totals, maxima + jnp.log(totals)


def text_unit(pooled_low, text_proj):
    proj_out = dot(pooled_low, text_proj)
    inverse_z = lax.rsqrt(jnp.sum(proj_out * proj_out, -1, keepdims=True) + EPS)
    return proj_out * inverse_z, inverse_z


def branch_grad(grad_unit, unit_text, inverse_z, text_proj, lengths):
    grad_projout = (
        inverse_z * (grad_unit - unit_text * jnp.sum(unit_text * grad_unit, -1, keepdims=True))
    ).astype(bf16)
    return dot_nt(grad_projout, text_proj) / lengths


def loss_whole(pooled_all, image_all, text_proj, lengths_all, same, first_row, local_pairs):
    unit_text, inverse_z = text_unit(pooled_all, text_proj)
    scores = dot_nt(unit_text.astype(bf16), image_all) * SCALE
    by_text, text_total = softmax_parts(scores, 1)
    by_image, image_total = softmax_parts(scores, 0)

    def own_rows(values):
        return lax.dynamic_slice_in_dim(values, first_row, local_pairs, 0)

    own = jnp.sum(own_rows(scores * same), -1)
    pair_loss = 0.5 * (own_rows(text_total)[:, 0] - own) + 0.5 * (
        image_total[0, :local_pairs] - own
    )
    sgrad = (0.5 * (by_text - same) + 0.5 * (by_image - same)).astype(bf16)
    grad_unit = dot(sgrad, image_all) * SCALE
    grads = branch_grad(grad_unit, unit_text, inverse_z, text_proj, lengths_all)
    return pair_loss, own_rows(grads), grads.astype(bf16)


def loss_rows(pooled_all, image_all, text_proj, lengths_all, same, first_row, local_pairs):
    unit_all, inverse_all = text_unit(pooled_all, text_proj)

    def own_rows(values):
        return lax.dynamic_slice_in_dim(values, first_row, local_pairs, 0)

    unit_text, inverse_z = own_rows(unit_all), own_rows(inverse_all)
    text_scores = dot_nt(unit_text.astype(bf16), image_all) * SCALE
    image_scores = dot_nt(image_all[:local_pairs], unit_all.astype(bf16)) * SCALE
    by_text, text_total = softmax_parts(text_scores, 1)
    image_total = softmax_parts(image_scores, 1)[1]
    every_total = gather_relative(image_total)
    own_same = own_rows(same)
    own = jnp.sum(text_scores * own_same, -1)
    pair_loss = 0.5 * (text_total[:, 0] - own) + 0.5 * (image_total[:, 0] - own)
    by_image = jnp.exp(text_scores - every_total[:, 0][None, :])
    sgrad = (0.5 * (by_text - own_same) + 0.5 * (by_image - own_same)).astype(bf16)
    grad_unit = dot(sgrad, image_all) * SCALE
    grads = branch_grad(grad_unit, unit_text, inverse_z, text_proj, own_rows(lengths_all))
    return pair_loss, grads, grads.astype(bf16)


def local(
    images,
    groups,
    captions,
    cap_lengths,
    img_gain_a,
    img_w_qkv,
    img_b_qv,
    img_w_out,
    img_gain_m,
    img_w_up,
    img_b_up,
    img_w_down,
    gain_attn,
    w_qkv,
    b_qv,
    w_out,
    gain_mlp,
    w_up,
    b_up,
    w_down,
    text_proj,
):
    local_pairs = images.shape[0]
    rows_total = local_pairs * CAP
    mine = lax.axis_index("rep").astype(jnp.int32)
    mine_one = mine[None]
    total_pairs = local_pairs * lax.axis_size("dp") * lax.axis_size("rep")
    whole = total_pairs <= MOST_PAIRS

    image_vec = jnp.concatenate([img_gain_a, img_b_qv, img_gain_m, img_b_up])[None]
    image_vec_other = swap(image_vec, "rep", 1)
    weights = []
    for weight in (img_w_qkv, img_w_out, img_w_up, img_w_down):
        weights += [weight, swap(weight, "rep", 1)]

    text_vec = jnp.concatenate([gain_attn, b_qv, gain_mlp, b_up]).astype(f32)[None]
    flat = captions.reshape(rows_total, D)
    qkv, mixed, after, mlp, slope, early, hidden_low = text_forward(
        flat, cap_lengths, text_vec, w_qkv, w_out, w_up, w_down
    )
    early_all = lax.all_gather(early, ("dp", "rep"), axis=0, tiled=True)
    if whole:
        hidden_all = lax.all_gather(hidden_low, ("dp", "rep"), axis=0, tiled=True)
    image_emb = image_tower(jnp.transpose(images, (1, 0, 2)), groups, mine_one, image_vec, image_vec_other, weights)
    image_all = gather_relative(image_emb)

    first_row = lax.axis_index(("dp", "rep")) * local_pairs
    chips = lax.axis_index("dp") ^ jnp.array(relative_chips(), jnp.int32)
    devices = jnp.concatenate([2 * chips + mine, 2 * chips + 1 - mine])
    image_ids = (
        devices[:, None] * local_pairs + jnp.arange(local_pairs, dtype=jnp.int32)[None, :]
    ).reshape(1, total_pairs)
    same = (jnp.arange(total_pairs, dtype=jnp.int32)[:, None] == image_ids).astype(f32)
    loss_of = loss_whole if whole else loss_rows
    pair_loss, grads, branch_all = loss_of(
        early_all[:, :D],
        image_all,
        text_proj,
        early_all[:, D : D + 1].astype(f32),
        same,
        first_row,
        local_pairs,
    )
    place = chunk_places()
    branch = grads.astype(bf16)
    grad_pre, up_own, up_other, grad_bup = up_backward(
        place, mine_one, cap_lengths, branch, slope, mlp, w_down
    )
    half = D // 2
    own_columns = lax.dynamic_slice_in_dim(branch_all, mine * half, half, 1)
    if whole:
        grad_w_down = dot_tn(hidden_all, own_columns)
    else:
        other_columns = lax.dynamic_slice_in_dim(branch_all, (1 - mine) * half, half, 1)
        grad_w_down = dot_tn(hidden_low, own_columns) + swap(
            dot_tn(hidden_low, other_columns).astype(bf16), "rep", 1
        ).astype(f32)
        grad_w_down = lax.psum(grad_w_down, "dp")
    up_chunk = reduce_chunks(up_own, swap(up_other, "rep", 1), FF // 4)
    grad_after, grad_mixed, grad_gain = mlp_backward(
        cap_lengths, grad_pre, grads, after, text_vec, w_up, w_out
    )
    low, high = (
        attention_backward(cap_lengths, qkv, grad_mixed, start, rows_total // 2)
        for start in (0, rows_total // 2)
    )
    caption_grad, rest_own, rest_other = proj_backward(
        place, mine_one, low, high, grad_after, mixed, flat, text_vec, grad_gain, grad_bup, w_qkv
    )
    rest_chunk = reduce_chunks(rest_own, swap(rest_other, "rep", 1), D)
    place, grad_w_down = lax.optimization_barrier((place, grad_w_down))
    grad_w_up, grad_w_qkv, grad_w_out, *small = unpack(
        place, spread_chunks(up_chunk, FF // 4), spread_chunks(rest_chunk, D)
    )
    return (
        pair_loss,
        caption_grad.reshape(local_pairs, CAP, D),
        small[0],
        grad_w_qkv,
        small[1],
        grad_w_out,
        small[2],
        grad_w_up,
        small[3],
        grad_w_down,
    )


def solution(mesh):
    in_specs = (
        P(("dp", "rep"), None, None),
        P(("dp", "rep")),
        P(("dp", "rep"), None, None),
        P(("dp", "rep")),
        P("rep"),
        P("rep", None),
        P("rep"),
        P("rep", None),
        P("rep"),
        P("rep", None),
        P("rep"),
        P("rep", None),
        P(),
        P(),
        P(),
        P(),
        P(),
        P(),
        P(),
        P(),
        P(),
    )
    out_specs = (
        P(("dp", "rep")),
        P(("dp", "rep"), None, None),
        P("rep"),
        P(None, "rep"),
        P("rep"),
        P(None, "rep"),
        P("rep"),
        P(None, "rep"),
        P("rep"),
        P(None, "rep"),
    )
    return jax.shard_map(local, mesh=mesh, in_specs=in_specs, out_specs=out_specs, check_vma=False)
```

```python
import functools
import math

import jax
import jax.numpy as jnp
from jax import lax
from jax.experimental import pallas as pl
from jax.experimental.pallas import tpu as pltpu
from jax.sharding import PartitionSpec as P

D = 768
HEADS = 12
FF = 3072
ILEN = 145
LOWLEN = 50
CAP = 16

SCALE = 100.0
EPS = 1e-06
NEGATIVE = -1e30
LOG2E = math.log2(math.e)
MOST_PAIRS = 2048
VMEM_BYTES = 58 * 1024 * 1024

UNIT = 160
UNITS = 2
PART = 48
SPAN = 29
QB = 128
BW = 3 * D // 2 + D // 2 + 128
EARLY = D + 128
CHUNKS = 16

f32 = jnp.float32
bf16 = jnp.bfloat16


def dot(left_side, right_side):
    return jnp.dot(left_side, right_side, preferred_element_type=f32)


def dot_nt(left_side, right_side):
    return lax.dot_general(
        left_side, right_side, (((1,), (1,)), ((), ())), preferred_element_type=f32
    )


def dot_tn(left_side, right_side):
    return lax.dot_general(
        left_side, right_side, (((0,), (0,)), ((), ())), preferred_element_type=f32
    )


def normalize(values):
    center = values - jnp.mean(values, -1, keepdims=True)
    inverse = lax.rsqrt(jnp.mean(center * center, -1, keepdims=True) + EPS)
    return center * inverse, inverse


def norm_back(grad, normed, inverse):
    return inverse * (
        grad
        - jnp.mean(grad, -1, keepdims=True)
        - normed * jnp.mean(grad * normed, -1, keepdims=True)
    )


def normal_cdf(values):
    return 0.5 + 0.5 * lax.erf(values * (1.0 / math.sqrt(2.0)))


def split_low(values):
    big = values.astype(bf16)
    return big, (values - big.astype(f32)).astype(bf16)


def tower_kernel(
    groups_ref,
    mine_ref,
    x_hbm,
    vec_own_ref,
    vec_other_ref,
    qkv_own,
    qkv_other,
    out_own,
    out_other,
    up_own,
    up_other,
    down_own,
    down_other,
    emb_ref,
    order,
    x_ref,
    x_wide,
    wqkv,
    wout,
    wup,
    wdown,
    gain_a,
    bqkv,
    gain_m,
    bup,
    xs,
    qkv,
    mixed,
    asum,
    hsum,
    aparts,
    hparts,
    sems,
):
    total = x_ref.shape[1]
    pitch = total + 8
    mine = mine_ref[0]
    copies = []
    for k in range(ILEN // SPAN):
        span = pl.ds(k * SPAN, SPAN)
        copies.append(pltpu.make_async_copy(x_hbm.at[span], x_ref.at[span], sems.at[8 + k]))
    for k, (own, other, whole) in enumerate(
        (
            (qkv_own, qkv_other, wqkv),
            (out_own, out_other, wout),
            (up_own, up_other, wup),
            (down_own, down_other, wdown),
        )
    ):
        half = own.shape[0]
        copies.append(
            pltpu.make_async_copy(own, whole.at[pl.ds(mine * half, half)], sems.at[2 * k])
        )
        copies.append(
            pltpu.make_async_copy(
                other, whole.at[pl.ds((1 - mine) * half, half)], sems.at[2 * k + 1]
            )
        )
    for copy in copies:
        copy.start()

    vec_own = vec_own_ref[...].astype(f32)
    vec_other = vec_other_ref[...].astype(f32)
    low = jnp.where(mine == 0, vec_own, vec_other)
    high = jnp.where(mine == 0, vec_other, vec_own)
    start = 0
    for dest, size, at in (
        (gain_a, D // 2, (0, D // 2)),
        (bqkv, D, (0, 2 * D)),
        (gain_m, D // 2, (0, D // 2)),
        (bup, FF // 2, (0, FF // 2)),
    ):
        dest[:, at[0] : at[0] + size] = low[:, start : start + size]
        dest[:, at[1] : at[1] + size] = high[:, start : start + size]
        start += size
    bqkv[:, D : 2 * D] = jnp.zeros((1, D), f32)

    def count(i, found):
        return found + groups_ref[i]

    n_hi = lax.fori_loop(0, total, count, 0)

    def place_one(i, state):
        hi, lo = state
        group = groups_ref[i]
        order[jnp.where(group == 1, hi, lo)] = i
        return hi + group, lo + 1 - group

    lax.fori_loop(0, total, place_one, (0, n_hi))
    n_units = n_hi + (total - n_hi + 2) // 3

    xs[...] = jnp.zeros_like(xs)
    first = lax.broadcasted_iota(jnp.int32, (1, 128), 1) < 64
    key_at = lax.broadcasted_iota(jnp.int32, (UNIT, UNIT), 1)
    row_at = lax.broadcasted_iota(jnp.int32, (UNIT, UNIT), 0)
    sub = lax.broadcasted_iota(jnp.int32, (8, 1), 0)

    def place(unit, k):
        last = jnp.minimum(unit, n_units - 1)
        is_hi = last < n_hi
        where = jnp.where(is_hi, last, n_hi + 3 * (last - n_hi) + k)
        return order[jnp.minimum(where, total - 1)], is_hi

    def keep_parts(values, j, dest, col, width):
        rows = values.reshape(UNIT // 8, 8, width)
        parts = [
            jnp.sum(rows[0:6], 0),
            rows[6],
            jnp.sum(rows[7:12], 0),
            rows[12],
            jnp.sum(rows[13:18], 0),
            rows[18],
        ]
        for k, part in enumerate(parts):
            dest[j * PART + k * 8 : j * PART + k * 8 + 8, col : col + width] = part

    loads = copies[: ILEN // SPAN]
    copies = copies[ILEN // SPAN :]

    def widen(t, carry):
        for panel in range(D // 128):
            x_wide[panel, pl.ds(pl.multiple_of(t * pitch, 8), total), :] = x_ref[
                t, :, panel * 128 : (panel + 1) * 128
            ].astype(f32)
        return carry

    for k, load in enumerate(loads):
        load.wait()
        lax.fori_loop(k * SPAN, (k + 1) * SPAN, widen, 0)
    for copy in copies[:2]:
        copy.wait()

    def body(step, carry):
        for j in range(UNITS):
            unit = step * UNITS + j
            one, is_hi = place(unit, 0)
            two, three = place(unit, 1)[0], place(unit, 2)[0]
            base = j * UNIT

            @pl.when(is_hi)
            def _():
                for panel in range(D // 128):
                    xs[base : base + ILEN, panel * 128 : (panel + 1) * 128] = x_wide[
                        panel, pl.ds(one, ILEN, stride=pitch), :
                    ]

            @pl.when(jnp.logical_not(is_hi))
            def _():
                for k, index in enumerate((one, two, three)):
                    for panel in range(D // 128):
                        xs[
                            base + LOWLEN * k : base + LOWLEN * (k + 1),
                            panel * 128 : (panel + 1) * 128,
                        ] = x_wide[panel, pl.ds(index, LOWLEN, stride=pitch), :]

        low_rows = (normalize(xs[...])[0] * gain_a[...]).astype(bf16)
        for col in range(0, 3 * D, 256):
            values = dot(low_rows, wqkv[:, col : col + 256]) + bqkv[:, col : col + 256]
            if col < D:
                values = values * (LOG2E / 8.0)
            qkv[:, col : col + 256] = values.astype(bf16)

        @pl.when(step == 0)
        def _():
            for copy in copies[2:6]:
                copy.wait()

        for j in range(UNITS):
            is_hi = place(step * UNITS + j, 0)[1]
            base = j * UNIT
            key_seg = jnp.where(key_at < LOWLEN, 0, jnp.where(key_at < 2 * LOWLEN, 1, 2))
            row_seg = jnp.where(row_at < LOWLEN, 0, jnp.where(row_at < 2 * LOWLEN, 1, 2))
            short_ok = jnp.logical_and(key_seg == row_seg, key_at < 3 * LOWLEN)
            allowed = jnp.where(
                is_hi, (key_at < ILEN).astype(jnp.int32), short_ok.astype(jnp.int32)
            )
            bias = jnp.where(allowed > 0, 0.0, NEGATIVE)
            for p in range(HEADS // 2):
                lanes = slice(p * 128, (p + 1) * 128)
                query = qkv[base : base + UNIT, lanes]
                key = qkv[base : base + UNIT, D + p * 128 : D + (p + 1) * 128]
                value = qkv[base : base + UNIT, 2 * D + p * 128 : 2 * D + (p + 1) * 128]
                value_one = jnp.concatenate([value, jnp.ones_like(value)], 1)
                outs = []
                for h in range(2):
                    head = first if h == 0 else jnp.logical_not(first)
                    scores = dot_nt(jnp.where(head, query, jnp.zeros_like(query)), key) + bias
                    powers = jnp.exp2(scores - jnp.max(scores, 1, keepdims=True)).astype(bf16)
                    summed = dot(powers, value_one)
                    outs.append(summed[:, :128] / summed[:, 128:])
                mixed[base : base + UNIT, lanes] = jnp.where(first, outs[0], outs[1]).astype(bf16)
        for col in range(0, D, 256):
            xs[:, col : col + 256] += dot(mixed[...], wout[:, col : col + 256])
        for j in range(UNITS):
            keep_parts(xs[j * UNIT : (j + 1) * UNIT, :], j, aparts, 0, D)
        low_two = (normalize(xs[...])[0] * gain_m[...]).astype(bf16)
        width = 1024
        for col in range(0, FF, width):
            pre_act = dot(low_two, wup[:, col : col + width]) + bup[:, col : col + width]
            hidden = pre_act * normal_cdf(pre_act)
            for j in range(UNITS):
                keep_parts(hidden[j * UNIT : (j + 1) * UNIT], j, hparts, col, width)
        for j in range(UNITS):
            unit = step * UNITS + j
            one, is_hi = place(unit, 0)
            two, three = place(unit, 1)[0], place(unit, 2)[0]

            def rows_of(index):
                return pl.ds(pl.multiple_of(index * 8, 8), 8)

            @pl.when(is_hi)
            def _():
                for src, dest in ((aparts, asum), (hparts, hsum)):
                    part = [src[j * PART + k * 8 : j * PART + k * 8 + 8, :] for k in range(6)]
                    dest[rows_of(one), :] = (
                        (part[0] + part[1])
                        + (part[2] + part[3])
                        + (part[4] + jnp.where(sub < 1, part[5], 0.0))
                    )

            @pl.when(jnp.logical_not(is_hi))
            def _():
                for src, dest in ((aparts, asum), (hparts, hsum)):
                    part = [src[j * PART + k * 8 : j * PART + k * 8 + 8, :] for k in range(6)]
                    dest[rows_of(three), :] = (
                        jnp.where(sub < 4, 0.0, part[3])
                        + part[4]
                        + jnp.where(sub < 6, part[5], 0.0)
                    )
                    dest[rows_of(two), :] = (
                        jnp.where(sub < 2, 0.0, part[1])
                        + part[2]
                        + jnp.where(sub < 4, part[3], 0.0)
                    )
                    dest[rows_of(one), :] = part[0] + jnp.where(sub < 2, part[1], 0.0)

        return carry

    lax.fori_loop(0, (n_units + UNITS - 1) // UNITS, body, 0)
    for copy in copies[6:]:
        copy.wait()
    which = lax.broadcasted_iota(jnp.int32, (total, 128), 0)
    scale = jnp.zeros((total, 128), f32)
    for i in range(total):
        scale = jnp.where(
            which == i, jnp.where(groups_ref[i] == 1, 1.0 / ILEN, 1.0 / LOWLEN), scale
        )
    scale = scale[:, 0:1]
    big, rest = split_low(jnp.sum(hsum[...].reshape(total, 8, FF), 1) * scale)
    product = dot(jnp.concatenate([big, rest], 0), wdown[...])
    pooled = jnp.sum(asum[...].reshape(total, 8, D), 1) * scale + product[:total] + product[total:]
    emb_ref[...] = (
        pooled * lax.rsqrt(jnp.sum(pooled * pooled, -1, keepdims=True) + EPS)
    ).astype(bf16)


VM = pl.BlockSpec(memory_space=pltpu.VMEM)
SM = pl.BlockSpec(memory_space=pltpu.SMEM)
ANY = pl.BlockSpec(memory_space=pl.ANY)
PARAMS = pltpu.CompilerParams(vmem_limit_bytes=VMEM_BYTES)


def image_tower(images, groups, mine, vec_own, vec_other, weights):
    number = images.shape[1]
    rows = UNITS * UNIT
    flops = number * 100 * 2 * (4 * D * D + D * FF)
    return pl.pallas_call(
        tower_kernel,
        out_shape=jax.ShapeDtypeStruct((number, D), bf16),
        in_specs=[SM, SM, ANY, VM, VM] + [ANY] * 8,
        out_specs=VM,
        scratch_shapes=[
            pltpu.SMEM((number,), jnp.int32),
            pltpu.VMEM(images.shape, bf16),
            pltpu.VMEM((D // 128, ILEN * (number + 8), 128), f32),
            pltpu.VMEM((D, 3 * D), bf16),
            pltpu.VMEM((D, D), bf16),
            pltpu.VMEM((D, FF), bf16),
            pltpu.VMEM((FF, D), bf16),
            pltpu.VMEM((1, D), f32),
            pltpu.VMEM((1, 3 * D), f32),
            pltpu.VMEM((1, D), f32),
            pltpu.VMEM((1, FF), f32),
            pltpu.VMEM((rows, D), f32),
            pltpu.VMEM((rows, 3 * D), bf16),
            pltpu.VMEM((rows, D), bf16),
            pltpu.VMEM((number * 8, D), f32),
            pltpu.VMEM((number * 8, FF), f32),
            pltpu.VMEM((UNITS * PART, D), f32),
            pltpu.VMEM((UNITS * PART, FF), f32),
            pltpu.SemaphoreType.DMA((8 + ILEN // SPAN,)),
        ],
        compiler_params=PARAMS,
        cost_estimate=pl.CostEstimate(
            flops=flops, bytes_accessed=24 * 1024 * 1024, transcendentals=0
        ),
        name="image_tower",
    )(groups, mine, images, vec_own, vec_other, *weights)


def lens_along(lens_ref, start, number):
    owner = lax.broadcasted_iota(jnp.int32, (1, number * CAP), 1) // CAP
    lens = jnp.zeros((1, number * CAP), jnp.int32)
    for c in range(number):
        lens = jnp.where(owner == c, lens_ref[start + c], lens)
    return lens


def score_bias(lens_ref, block):
    per = QB // CAP
    position = lax.broadcasted_iota(jnp.int32, (1, QB), 1) % CAP
    valid = position < lens_along(lens_ref, block * per, per)
    rows = lax.broadcasted_iota(jnp.int32, (QB, QB), 0) // CAP
    columns = lax.broadcasted_iota(jnp.int32, (QB, QB), 1) // CAP
    return jnp.where(jnp.logical_and(rows == columns, valid), 0.0, NEGATIVE)


def forward_kernel(
    lens_ref,
    x_ref,
    vec_ref,
    wqkv_ref,
    wout_ref,
    wup_ref,
    wdown_ref,
    qkv,
    mixed,
    after,
    mlp,
    slope,
    attention,
    early,
    hidden_low,
    hidden,
):
    rows = x_ref.shape[0]
    number = rows // CAP
    first = lax.broadcasted_iota(jnp.int32, (1, 128), 1) < 64
    normed, _ = normalize(x_ref[...].astype(f32))
    low = (normed * vec_ref[:, 0:D]).astype(bf16)
    for col in range(0, 3 * D, 256):
        values = dot(low, wqkv_ref[:, col : col + 256])
        if col < D:
            values = values + vec_ref[:, D + col : D + col + 256]
        if col >= 2 * D:
            values = values + vec_ref[:, col : col + 256]
        values = values.astype(bf16)
        if col < D:
            values = values * jnp.asarray(0.125, bf16)
        qkv[:, col : col + 256] = values
    for block in range(rows // QB):
        bias = score_bias(lens_ref, block)
        span = slice(block * QB, (block + 1) * QB)
        for p in range(HEADS // 2):
            query = qkv[span, p * 128 : (p + 1) * 128]
            key = qkv[span, D + p * 128 : D + (p + 1) * 128]
            value = qkv[span, 2 * D + p * 128 : 2 * D + (p + 1) * 128]
            outs = []
            for h in range(2):
                head = first if h == 0 else jnp.logical_not(first)
                scores = dot_nt(jnp.where(head, query, jnp.zeros_like(query)), key) * LOG2E + bias
                powers = jnp.exp2(scores - jnp.max(scores, 1, keepdims=True))
                low_att = (powers * (1.0 / jnp.sum(powers, 1, keepdims=True))).astype(bf16)
                outs.append(dot(low_att, value))
                attention[span, (2 * p + h) * QB : (2 * p + h + 1) * QB] = low_att
            mixed[span, p * 128 : (p + 1) * 128] = jnp.where(first, outs[0], outs[1]).astype(bf16)
    for col in range(0, D, 256):
        after[:, col : col + 256] = x_ref[:, col : col + 256].astype(f32) + dot(
            mixed[...], wout_ref[:, col : col + 256]
        )
    mlp[...] = (normalize(after[...])[0] * vec_ref[:, 3 * D : 4 * D]).astype(bf16)
    lens = lens_along(lens_ref, 0, number)
    position = lax.broadcasted_iota(jnp.int32, (1, rows), 1)
    owner = (
        lax.broadcasted_iota(jnp.int32, (number, rows), 0)
        == lax.broadcasted_iota(jnp.int32, (number, rows), 1) // CAP
    )
    members = jnp.where(jnp.logical_and(owner, position % CAP < lens), 1.0, 0.0)
    pool = members.astype(bf16)
    count = jnp.sum(members, 1, keepdims=True)
    width = 512
    for col in range(0, FF, width):
        span = slice(col, col + width)
        pre_act = dot(mlp[...], wup_ref[:, span]) + vec_ref[:, 4 * D + col : 4 * D + col + width]
        phi = normal_cdf(pre_act)
        hidden[:, span] = (pre_act * phi).astype(bf16)
        density = jnp.exp2(pre_act * pre_act * (-0.5 * LOG2E)) * (1.0 / math.sqrt(2.0 * math.pi))
        slope[:, span] = (phi + pre_act * density).astype(bf16)
    big, rest = split_low(dot(pool, hidden[...]))
    after_big, after_rest = split_low(after[...])
    pooled = (
        dot(pool, after_big)
        + dot(pool, after_rest)
        + dot(big, wdown_ref[...])
        + dot(rest, wdown_ref[...])
    )
    early[:, 0:D] = (pooled / count).astype(bf16)
    early[:, D:EARLY] = jnp.broadcast_to(count, (number, EARLY - D)).astype(bf16)
    hidden_low[...] = big


def text_forward(captions, lens, vec, w_qkv, w_out, w_up, w_down):
    rows = captions.shape[0]
    shape = jax.ShapeDtypeStruct
    return pl.pallas_call(
        forward_kernel,
        out_shape=[
            shape((rows, 3 * D), bf16),
            shape((rows, D), bf16),
            shape((rows, D), f32),
            shape((rows, D), bf16),
            shape((rows, FF), bf16),
            shape((rows, HEADS * QB), bf16),
            shape((rows // CAP, EARLY), bf16),
            shape((rows // CAP, FF), bf16),
        ],
        in_specs=[SM] + [VM] * 6,
        out_specs=[VM] * 8,
        scratch_shapes=[pltpu.VMEM((rows, FF), bf16)],
        compiler_params=PARAMS,
        cost_estimate=pl.CostEstimate(
            flops=2 * rows * (4 * D * D + 2 * D * FF),
            bytes_accessed=24 * 1024 * 1024,
            transcendentals=0,
        ),
        name="text_forward",
    )(lens, captions, vec, w_qkv, w_out, w_up, w_down)


def put_chunks(dest, values, place_ref, stream, col):
    rows = values.shape[0] // CHUNKS
    for chunk in range(CHUNKS):
        at = pl.multiple_of(place_ref[stream, chunk] * rows, 16)
        dest[pl.ds(at, rows), col : col + values.shape[1]] = values[
            chunk * rows : (chunk + 1) * rows
        ].astype(dest.dtype)


def up_kernel(
    place_ref, mine_ref, lens_ref, branch_ref, slope_ref, mlp_ref, wdown_ref,
    grad_pre, own, other, grad_bup, grad_hidden, mlp_t,
):
    number = slope_ref.shape[0] // CAP
    half = FF // 2
    mine = mine_ref[0]
    for col in range(0, FF, 512):
        grad_hidden[:, col : col + 512] = dot_nt(branch_ref[...], wdown_ref[col : col + 512, :])
    position = lax.broadcasted_iota(jnp.int32, (CAP, 1), 0)
    for c in range(number):
        span = slice(c * CAP, (c + 1) * CAP)
        keep = jnp.where(position < lens_ref[c], 1.0, 0.0)
        grad_pre[span, :] = (
            grad_hidden[c : c + 1, :] * slope_ref[span, :].astype(f32) * keep
        ).astype(bf16)
    mlp_t[...] = mlp_ref[...].T
    for which, dest in ((1 - mine, other), (mine, own)):
        for col in range(0, half, 384):
            lanes = pl.ds(pl.multiple_of(which * half + col, 128), 384)
            put_chunks(dest, dot(mlp_t[...], grad_pre[:, lanes]), place_ref, 2 * col // half, col)
    for col in range(0, FF, 512):
        grad_bup[:, col : col + 512] = jnp.sum(
            grad_pre[:, col : col + 512].astype(f32), 0, keepdims=True
        )


def up_backward(place, mine, lens, branch, slope, mlp, w_down):
    rows = slope.shape[0]
    shape = jax.ShapeDtypeStruct
    return pl.pallas_call(
        up_kernel,
        out_shape=[
            shape((rows, FF), bf16),
            shape((D, FF // 2), f32),
            shape((D, FF // 2), bf16),
            shape((1, FF), f32),
        ],
        in_specs=[SM, SM, SM] + [VM] * 4,
        out_specs=[VM] * 4,
        scratch_shapes=[pltpu.VMEM((rows // CAP, FF), f32), pltpu.VMEM((D, rows), bf16)],
        compiler_params=PARAMS,
        cost_estimate=pl.CostEstimate(
            flops=2 * rows * D * FF, bytes_accessed=20 * 1024 * 1024, transcendentals=0
        ),
        name="up_backward",
    )(place, mine, lens, branch, slope, mlp, w_down)


def mlp_kernel(
    lens_ref, pre_ref, grad_ref, after_ref, vec_ref, wup_ref, wout_ref,
    grad_after, grad_mixed, grad_gain, grad_out,
):
    number = after_ref.shape[0] // CAP
    grad_mlp = dot_nt(pre_ref[...], wup_ref[...])
    normed_two, inverse_two = normalize(after_ref[...])
    grad_gain[...] = jnp.sum(grad_mlp * normed_two, 0, keepdims=True)
    grad_after[...] = norm_back(grad_mlp * vec_ref[:, 3 * D : 4 * D], normed_two, inverse_two)
    position = lax.broadcasted_iota(jnp.int32, (CAP, 1), 0)
    for c in range(number):
        keep = jnp.where(position < lens_ref[c], 1.0, 0.0)
        grad_after[c * CAP : (c + 1) * CAP, :] += grad_ref[c : c + 1, :] * keep
    grad_out[...] = grad_after[...].astype(bf16)
    for col in range(0, D, 256):
        grad_mixed[:, col : col + 256] = dot_nt(
            grad_out[...], wout_ref[col : col + 256, :]
        ).astype(bf16)


def mlp_backward(lens, grad_pre, grads, after, vec, w_up, w_out):
    rows = after.shape[0]
    shape = jax.ShapeDtypeStruct
    return pl.pallas_call(
        mlp_kernel,
        out_shape=[shape((rows, D), f32), shape((rows, D), bf16), shape((1, D), f32)],
        in_specs=[SM] + [VM] * 6,
        out_specs=[VM] * 3,
        scratch_shapes=[pltpu.VMEM((rows, D), bf16)],
        compiler_params=PARAMS,
        cost_estimate=pl.CostEstimate(
            flops=2 * rows * (D * D + D * FF), bytes_accessed=20 * 1024 * 1024, transcendentals=0
        ),
        name="mlp_backward",
    )(lens, grad_pre, grads, after, vec, w_up, w_out)


def attention_kernel(qkv_ref, att_ref, mixed_ref, grad_ref, grad_proj, *, start):
    first = lax.broadcasted_iota(jnp.int32, (1, 128), 1) < 64
    ones = jnp.ones((128, QB), bf16)
    for block in range(grad_proj.shape[0] // QB):
        span = slice(start + block * QB, start + (block + 1) * QB)
        dest = slice(block * QB, (block + 1) * QB)
        for p in range(HEADS // 2):
            at = p * 128
            query = qkv_ref[span, at : at + 128]
            key = qkv_ref[span, D + at : D + at + 128]
            value = qkv_ref[span, 2 * D + at : 2 * D + at + 128]
            grad = grad_ref[span, at : at + 128]
            product = (grad.astype(f32) * mixed_ref[span, at : at + 128].astype(f32)).astype(bf16)
            grad_q, grad_k, grad_v = [], [], []
            for h in range(2):
                head = first if h == 0 else jnp.logical_not(first)
                low = att_ref[span, (2 * p + h) * QB : (2 * p + h + 1) * QB]
                grad_att = dot_nt(jnp.where(head, grad, jnp.zeros_like(grad)), value)
                mean = dot(jnp.where(head, product, jnp.zeros_like(product)), ones)
                grad_s = (low.astype(f32) * (grad_att - mean)).astype(bf16)
                grad_q.append(dot(grad_s, key))
                grad_k.append(dot_tn(grad_s, query))
                grad_v.append(dot_tn(low, grad))
            for k, (parts, scale) in enumerate(((grad_q, 0.125), (grad_k, 1.0), (grad_v, 1.0))):
                grad_proj[dest, k * D + at : k * D + at + 128] = (
                    jnp.where(first, parts[0], parts[1]) * scale
                ).astype(bf16)


def attention_backward(qkv, attention, mixed, grad_mixed, start, rows):
    return pl.pallas_call(
        functools.partial(attention_kernel, start=start),
        out_shape=jax.ShapeDtypeStruct((rows, 3 * D), bf16),
        in_specs=[VM] * 4,
        out_specs=VM,
        compiler_params=PARAMS,
        cost_estimate=pl.CostEstimate(
            flops=2 * rows * 24 * D * D, bytes_accessed=40 * 1024 * 1024, transcendentals=0
        ),
        name="attention_backward",
    )(qkv, attention, mixed, grad_mixed)


def proj_kernel(
    place_ref, mine_ref, proj_low, proj_high, after_ref, mixed_ref, x_ref, vec_ref,
    gain_ref, bup_ref, wqkv_ref,
    caption_grad, own, other, grad_proj, sums, lhs_t, grad_out,
):
    half_rows = proj_low.shape[0]
    chunk_rows = D // CHUNKS
    mine = mine_ref[0]
    gain_a = vec_ref[:, 0:D]
    grad_proj[0:half_rows, :] = proj_low[...]
    grad_proj[half_rows:, :] = proj_high[...]
    normed_one, inverse_one = normalize(x_ref[...].astype(f32))
    lhs_t[...] = (normed_one * gain_a).astype(bf16).T
    half_out, half_qkv = D // 2, 3 * D // 2
    for which, dest in ((1 - mine, other), (mine, own)):
        for col in range(0, half_qkv, 384):
            lanes = pl.ds(pl.multiple_of(which * half_qkv + col, 128), 384)
            put_chunks(dest, dot(lhs_t[...], grad_proj[:, lanes]), place_ref, col // 768, col)
    lhs_t[...] = mixed_ref[...].T
    grad_out[...] = after_ref[...].astype(bf16)
    for which, dest in ((1 - mine, other), (mine, own)):
        lanes = pl.ds(pl.multiple_of(which * half_out, 128), half_out)
        put_chunks(dest, dot(lhs_t[...], grad_out[:, lanes]), place_ref, 1, half_qkv)
    grad_in = dot_nt(grad_proj[...], wqkv_ref[...])
    sums[:, 0:D] = jnp.sum(grad_in * normed_one, 0, keepdims=True)
    sums[:, D : 2 * D] = jnp.sum(grad_proj[:, 0:D].astype(f32), 0, keepdims=True)
    sums[:, 2 * D : 3 * D] = jnp.sum(grad_proj[:, 2 * D :].astype(f32), 0, keepdims=True)
    sums[:, 3 * D : 4 * D] = gain_ref[...]
    sums[:, 4 * D :] = bup_ref[...]
    caption_grad[...] = after_ref[...] + norm_back(grad_in * gain_a, normed_one, inverse_one)
    for which, dest in ((1 - mine, other), (mine, own)):
        dest[:, BW - 128 :] = jnp.zeros((D, 128), dest.dtype)
        pieces = []
        for start, size in ((0, D), (D, 2 * D), (3 * D, D), (4 * D, FF)):
            for k in range(0, size // 2, 128):
                at = pl.multiple_of(start + which * (size // 2) + k, 128)
                pieces.append(sums[:, pl.ds(at, 128)])
        pieces += [jnp.zeros_like(pieces[0])] * (32 - len(pieces))
        at = pl.multiple_of(place_ref[1, 0] * chunk_rows, 16)
        dest[pl.ds(at, 32), BW - 128 :] = jnp.concatenate(pieces, 0).astype(dest.dtype)


def proj_backward(
    place, mine, proj_low, proj_high, grad_after, mixed, captions, vec, grad_gain, grad_bup, w_qkv
):
    rows = captions.shape[0]
    shape = jax.ShapeDtypeStruct
    return pl.pallas_call(
        proj_kernel,
        out_shape=[shape((rows, D), f32), shape((D, BW), f32), shape((D, BW), bf16)],
        in_specs=[SM, SM] + [VM] * 9,
        out_specs=[VM] * 3,
        scratch_shapes=[
            pltpu.VMEM((rows, 3 * D), bf16),
            pltpu.VMEM((1, 4 * D + FF), f32),
            pltpu.VMEM((D, rows), bf16),
            pltpu.VMEM((rows, D), bf16),
        ],
        compiler_params=PARAMS,
        cost_estimate=pl.CostEstimate(
            flops=2 * rows * 7 * D * D, bytes_accessed=20 * 1024 * 1024, transcendentals=0
        ),
        name="proj_backward",
    )(place, mine, proj_low, proj_high, grad_after, mixed, captions, vec, grad_gain, grad_bup, w_qkv)


def dp_bits():
    bits, bit = [], 1
    while bit < lax.axis_size("dp"):
        bits.append(bit)
        bit *= 2
    return bits


def swap(values, axis, bit):
    size = lax.axis_size(axis)
    return lax.ppermute(values, axis, [(place, place ^ bit) for place in range(size)])


def gather_relative(values):
    bits = dp_bits()
    while bits:
        pair = bits[-2:]
        bits = bits[:-2]
        offsets = [0]
        for bit in pair:
            offsets += [entry + bit for entry in offsets]
        values = jnp.concatenate([swap(values, "dp", k) if k else values for k in offsets], 0)
    return jnp.concatenate([values, swap(values, "rep", 1)], 0)


def relative_chips():
    bits, table = dp_bits(), [0]
    while bits:
        pair = bits[-2:]
        bits = bits[:-2]
        offsets = [0]
        for bit in pair:
            offsets += [entry + bit for entry in offsets]
        table = [entry ^ k for k in offsets for entry in table]
    return table


def chunk_places():
    away = jnp.arange(CHUNKS, dtype=jnp.int32) ^ (lax.axis_index("dp") % CHUNKS)
    one, two, rest = away % 2, away // 2 % 2, away // 4
    return jnp.stack([one * 8 + two * 4 + rest, two * 8 + one * 4 + rest]).astype(jnp.int32)


def streams_of(width):
    return ((slice(0, width), 1, 2), (slice(width, None), 2, 1))


def reduce_first(own, arrived, streams):
    half = own.shape[0] // 2

    def both(rows, lanes):
        return own[rows, lanes] + arrived[rows, lanes].astype(f32)

    sent = [both(slice(half, None), lanes).astype(bf16) for lanes, _, _ in streams]
    return sent, [both(slice(0, half), lanes) for lanes, _, _ in streams]


def reduce_swaps(sent, streams, stage):
    return [swap(piece, "dp", stream[stage]) for piece, stream in zip(sent, streams)]


def reduce_add(came, kept):
    half = kept[0].shape[0] // 2
    totals = [total + got.astype(f32) for total, got in zip(kept, came)]
    return [total[half:].astype(bf16) for total in totals], [total[:half] for total in totals]


def reduce_join(came, kept):
    total = jnp.concatenate([total + got.astype(f32) for total, got in zip(kept, came)], 1)
    rows = total.shape[0] // 4
    return [total[k * rows : (k + 1) * rows].astype(bf16) for k in (1, 2, 3)], total[:rows]


def reduce_last(parts, total):
    total = total + sum(part.astype(f32) for part in parts)
    for bit in dp_bits()[4:]:
        total = total + swap(total.astype(bf16), "dp", bit).astype(f32)
    return total.astype(bf16)


def spread_first(chunk):
    return [swap(chunk, "dp", 4 * k) if k else chunk for k in range(4)]


def spread_second(column, streams):
    return [jnp.concatenate([piece[:, lanes] for piece in column], 0) for lanes, _, _ in streams]


def spread_third(mine, near, streams):
    quarters = []
    for own, next_to, (_, one, _) in zip(mine, near, streams):
        quarters += [own, next_to, swap(own, "dp", one), swap(next_to, "dp", one)]
    return quarters


def unpack_kernel(place_ref, *refs):
    parts = refs[:16]
    g_up, g_qkv, g_out = refs[16:19]
    vectors = refs[19:]
    rows = D // CHUNKS
    place = place_ref[0, 0]
    me = place // 8 + 2 * (place // 4 % 2) + 4 * (place % 4)
    for stream in range(2):
        for quarter in range(4):
            for k in range(4):
                high, low = quarter // 2, quarter % 2
                away = (high + 2 * low if stream == 0 else low + 2 * high) + 4 * k
                chunk = me ^ away
                at = pl.ds(pl.multiple_of(chunk * rows, 16), rows)
                span = slice(k * rows, (k + 1) * rows)
                lanes = slice(stream * FF // 4, (stream + 1) * FF // 4)
                g_up[at, lanes] = parts[stream * 4 + quarter][span, :].astype(f32)
                rest = parts[8 + stream * 4 + quarter][span, :].astype(f32)
                if stream == 0:
                    g_qkv[at, 0:D] = rest
                    continue
                g_qkv[at, D:] = rest[:, : D // 2]
                g_out[at, :] = rest[:, D // 2 : D]

                @pl.when(chunk == 0)
                def _():
                    row = 0
                    for dest in vectors:
                        for lane in range(0, dest.shape[0], 128):
                            dest[lane : lane + 128] = rest[row, D:]
                            row += 1


def unpack(place, ups, rests):
    shape = jax.ShapeDtypeStruct
    return pl.pallas_call(
        unpack_kernel,
        out_shape=[
            shape((D, FF // 2), f32),
            shape((D, 3 * D // 2), f32),
            shape((D, D // 2), f32),
            shape((D // 2,), f32),
            shape((D,), f32),
            shape((D // 2,), f32),
            shape((FF // 2,), f32),
        ],
        in_specs=[SM] + [VM] * 16,
        out_specs=[VM] * 7,
        compiler_params=PARAMS,
        name="unpack",
    )(place, *ups, *rests)


def softmax_parts(scores, axis):
    maxima = jnp.max(scores, axis, keepdims=True)
    powers = jnp.exp(scores - maxima)
    totals = jnp.sum(powers, axis, keepdims=True)
    return powers / totals, maxima + jnp.log(totals)


def text_unit(pooled_low, text_proj):
    proj_out = dot(pooled_low, text_proj)
    inverse_z = lax.rsqrt(jnp.sum(proj_out * proj_out, -1, keepdims=True) + EPS)
    return proj_out * inverse_z, inverse_z


def branch_grad(grad_unit, unit_text, inverse_z, text_proj, lengths):
    grad_projout = (
        inverse_z * (grad_unit - unit_text * jnp.sum(unit_text * grad_unit, -1, keepdims=True))
    ).astype(bf16)
    return dot_nt(grad_projout, text_proj) / lengths


def loss_kernel(
    where_ref, early_ref, image_ref, proj_ref, pair_loss, own_grads, branch,
    unit, inverse, scores, sgrad,
):
    total = image_ref.shape[0]
    number = own_grads.shape[0]
    chip, mine = where_ref[0], where_ref[1]
    block = 256
    for row in range(0, total, block):
        span = slice(row, row + block)
        proj_out = dot(early_ref[span, 0:D], proj_ref[...])
        inverse_z = lax.rsqrt(jnp.sum(proj_out * proj_out, -1, keepdims=True) + EPS)
        inverse[span, :] = jnp.broadcast_to(inverse_z, (block, 128))
        unit[span, :] = proj_out * inverse_z
        scores[span, :] = dot_nt(unit[span, :].astype(bf16), image_ref[...]) * SCALE
    place = lax.broadcasted_iota(jnp.int32, (1, total), 1) // number
    chips = total // (2 * number)
    away = place % chips
    other = place // chips
    from_chip = chip ^ (away // 4 + 4 * (away % 4)) if chips == 16 else None
    image_id = (from_chip * 2 + (mine ^ other)) * number + (
        lax.broadcasted_iota(jnp.int32, (1, total), 1) % number
    )
    column_max = jnp.max(scores[...], 0, keepdims=True)
    column_sum = jnp.zeros((1, total), f32)
    for row in range(0, total, block):
        column_sum += jnp.sum(
            jnp.exp(scores[row : row + block, :] - column_max), 0, keepdims=True
        )
    column_total = column_max + jnp.log(column_sum)
    for row in range(0, total, block):
        span = slice(row, row + block)
        values = scores[span, :]
        row_max = jnp.max(values, 1, keepdims=True)
        powers = jnp.exp(values - row_max)
        by_text = powers * (0.5 / jnp.sum(powers, 1, keepdims=True))
        by_image = jnp.exp(values - column_max) * (0.5 / column_sum)
        text_id = lax.broadcasted_iota(jnp.int32, (block, 1), 0) + row
        same = jnp.where(text_id == image_id, 1.0, 0.0)
        sgrad[span, :] = (by_text + by_image - same).astype(bf16)
        grad_unit = dot(sgrad[span, :], image_ref[...]) * SCALE
        unit_text = unit[span, :]
        grad_proj = (
            inverse[span, 0:1]
            * (grad_unit - unit_text * jnp.sum(unit_text * grad_unit, -1, keepdims=True))
        ).astype(bf16)
        unit[span, :] = dot_nt(grad_proj, proj_ref[...]) / early_ref[span, D : D + 1].astype(f32)
        branch[span, :] = unit[span, :].astype(bf16)
    first = pl.multiple_of((chip * 2 + mine) * number, 32)
    own_grads[...] = unit[pl.ds(first, number), :]
    values = scores[pl.ds(first, number), :]
    row_max = jnp.max(values, 1, keepdims=True)
    row_total = row_max + jnp.log(jnp.sum(jnp.exp(values - row_max), 1, keepdims=True))
    text_id = lax.broadcasted_iota(jnp.int32, (number, 1), 0) + first
    same = jnp.where(text_id == image_id, 1.0, 0.0)
    both = 0.5 * (row_total + column_total) - values
    pair_loss[...] = jnp.broadcast_to(jnp.sum(both * same, 1, keepdims=True), (number, 128))


def loss_whole(early_all, image_all, text_proj, chip, mine, number):
    total = image_all.shape[0]
    shape = jax.ShapeDtypeStruct
    pair_loss, grads, branch = pl.pallas_call(
        loss_kernel,
        out_shape=[shape((number, 128), f32), shape((number, D), f32), shape((total, D), bf16)],
        in_specs=[SM] + [VM] * 3,
        out_specs=[VM] * 3,
        scratch_shapes=[
            pltpu.VMEM((total, D), f32),
            pltpu.VMEM((total, 128), f32),
            pltpu.VMEM((total, total), f32),
            pltpu.VMEM((total, total), bf16),
        ],
        compiler_params=PARAMS,
        name="pair_loss",
    )(jnp.stack([chip, mine]), early_all, image_all, text_proj)
    return pair_loss[:, 0], grads, branch


def loss_rows(pooled_all, image_all, text_proj, lengths_all, image_ids, first_row, local_pairs):
    unit_all, inverse_all = text_unit(pooled_all, text_proj)

    def own_rows(values):
        return lax.dynamic_slice_in_dim(values, first_row, local_pairs, 0)

    unit_text, inverse_z = own_rows(unit_all), own_rows(inverse_all)
    text_scores = dot_nt(unit_text.astype(bf16), image_all) * SCALE
    image_scores = dot_nt(image_all[:local_pairs], unit_all.astype(bf16)) * SCALE
    by_text, text_total = softmax_parts(text_scores, 1)
    image_total = softmax_parts(image_scores, 1)[1]
    every_total = gather_relative(image_total)
    text_ids = first_row + jnp.arange(local_pairs, dtype=jnp.int32)
    own_same = (text_ids[:, None] == image_ids).astype(f32)
    own = jnp.sum(text_scores * own_same, -1)
    pair_loss = 0.5 * (text_total[:, 0] - own) + 0.5 * (image_total[:, 0] - own)
    by_image = jnp.exp(text_scores - every_total[:, 0][None, :])
    sgrad = (0.5 * (by_text - own_same) + 0.5 * (by_image - own_same)).astype(bf16)
    grad_unit = dot(sgrad, image_all) * SCALE
    grads = branch_grad(grad_unit, unit_text, inverse_z, text_proj, own_rows(lengths_all))
    return pair_loss, grads, grads.astype(bf16)


def local(
    images,
    groups,
    captions,
    cap_lengths,
    img_gain_a,
    img_w_qkv,
    img_b_qv,
    img_w_out,
    img_gain_m,
    img_w_up,
    img_b_up,
    img_w_down,
    gain_attn,
    w_qkv,
    b_qv,
    w_out,
    gain_mlp,
    w_up,
    b_up,
    w_down,
    text_proj,
):
    local_pairs = images.shape[0]
    rows_total = local_pairs * CAP
    mine = lax.axis_index("rep").astype(jnp.int32)
    mine_one = mine[None]
    total_pairs = local_pairs * lax.axis_size("dp") * lax.axis_size("rep")
    whole = total_pairs <= MOST_PAIRS

    image_vec = jnp.concatenate([img_gain_a, img_b_qv, img_gain_m, img_b_up])[None]
    image_vec_other = swap(image_vec, "rep", 1)
    weights = []
    for weight in (img_w_qkv, img_w_out, img_w_up, img_w_down):
        weights += [weight, swap(weight, "rep", 1)]

    text_vec = jnp.concatenate([gain_attn, b_qv, gain_mlp, b_up]).astype(f32)[None]
    flat = captions.reshape(rows_total, D)
    qkv, mixed, after, mlp, slope, attention, early, hidden_low = text_forward(
        flat, cap_lengths, text_vec, w_qkv, w_out, w_up, w_down
    )
    sent = jnp.concatenate([early, hidden_low], 1) if whole else early
    early_all = lax.all_gather(sent, ("dp", "rep"), axis=0, tiled=True)
    image_emb = image_tower(
        jnp.transpose(images, (1, 0, 2)), groups, mine_one, image_vec, image_vec_other, weights
    )
    image_all = gather_relative(image_emb)
    chip = lax.axis_index("dp").astype(jnp.int32)
    if whole:
        pair_loss, grads, branch_all = loss_whole(
            early_all, image_all, text_proj, chip, mine, local_pairs
        )
    else:
        chips = chip ^ jnp.array(relative_chips(), jnp.int32)
        devices = jnp.concatenate([2 * chips + mine, 2 * chips + 1 - mine])
        image_ids = (
            devices[:, None] * local_pairs + jnp.arange(local_pairs, dtype=jnp.int32)[None, :]
        ).reshape(1, total_pairs)
        pair_loss, grads, branch_all = loss_rows(
            early_all[:, :D],
            image_all,
            text_proj,
            early_all[:, D : D + 1].astype(f32),
            image_ids,
            (2 * chip + mine) * local_pairs,
            local_pairs,
        )
    place = chunk_places()
    branch = grads.astype(bf16)
    grad_pre, up_own, up_other, grad_bup = up_backward(
        place, mine_one, cap_lengths, branch, slope, mlp, w_down
    )
    arrived = swap(up_other, "rep", 1)
    grad_after, grad_mixed, grad_gain = mlp_backward(
        cap_lengths, grad_pre, grads, after, text_vec, w_up, w_out
    )
    up_streams = streams_of(FF // 4)
    up_sent, up_kept = reduce_first(up_own, arrived, up_streams)
    grad_mixed, *up_sent = lax.optimization_barrier((grad_mixed, *up_sent))
    half_rows = rows_total // 2
    low = attention_backward(qkv, attention, mixed, grad_mixed, 0, half_rows)
    up_came = reduce_swaps(up_sent, up_streams, 1)
    low, *up_came = lax.optimization_barrier((low, *up_came))
    up_sent, up_kept = reduce_add(up_came, up_kept)
    grad_mixed, *up_sent = lax.optimization_barrier((grad_mixed, *up_sent))
    high = attention_backward(qkv, attention, mixed, grad_mixed, half_rows, half_rows)
    up_came = reduce_swaps(up_sent, up_streams, 2)
    high, *up_came = lax.optimization_barrier((high, *up_came))
    up_sent, up_kept = reduce_join(up_came, up_kept)
    low, high, *up_sent = lax.optimization_barrier((low, high, *up_sent))
    up_came = [swap(piece, "dp", 4 * (k + 1)) for k, piece in enumerate(up_sent)]
    caption_grad, rest_own, rest_other = proj_backward(
        place, mine_one, low, high, grad_after, mixed, flat, text_vec, grad_gain, grad_bup, w_qkv
    )
    rest_other, *up_came = lax.optimization_barrier((rest_other, *up_came))
    up_chunk = reduce_last(up_came, up_kept)
    rest_streams = streams_of(D)
    arrived = swap(rest_other, "rep", 1)
    up_column = spread_first(up_chunk)
    rest_sent, rest_kept = reduce_first(rest_own, arrived, rest_streams)
    half = D // 2
    own_columns = lax.dynamic_slice_in_dim(branch_all, mine * half, half, 1)
    if whole:
        grad_w_down = dot_tn(early_all[:, EARLY:], own_columns)
    else:
        other_columns = lax.dynamic_slice_in_dim(branch_all, (1 - mine) * half, half, 1)
        grad_w_down = dot_tn(hidden_low, own_columns) + swap(
            dot_tn(hidden_low, other_columns).astype(bf16), "rep", 1
        ).astype(f32)
        grad_w_down = lax.psum(grad_w_down, "dp")
    rest_came = reduce_swaps(rest_sent, rest_streams, 1)
    up_mine = spread_second(up_column, up_streams)
    grad_w_down, *rest_came = lax.optimization_barrier((grad_w_down, *rest_came))
    rest_sent, rest_kept = reduce_add(rest_came, rest_kept)
    up_near = [swap(piece, "dp", two) for piece, (_, _, two) in zip(up_mine, up_streams)]
    rest_sent, rest_kept = reduce_join(reduce_swaps(rest_sent, rest_streams, 2), rest_kept)
    rest_came = [swap(piece, "dp", 4 * (k + 1)) for k, piece in enumerate(rest_sent)]
    rest_chunk = reduce_last(rest_came, rest_kept)
    rest_column = spread_first(rest_chunk)
    up_parts = spread_third(up_mine, up_near, up_streams)
    rest_mine = spread_second(rest_column, rest_streams)
    rest_near = [swap(piece, "dp", two) for piece, (_, _, two) in zip(rest_mine, rest_streams)]
    rest_parts = spread_third(rest_mine, rest_near, rest_streams)
    grad_w_up, grad_w_qkv, grad_w_out, *small = unpack(place, up_parts, rest_parts)
    return (
        pair_loss,
        caption_grad.reshape(local_pairs, CAP, D),
        small[0],
        grad_w_qkv,
        small[1],
        grad_w_out,
        small[2],
        grad_w_up,
        small[3],
        grad_w_down,
    )


def solution(mesh):
    in_specs = (
        P(("dp", "rep"), None, None),
        P(("dp", "rep")),
        P(("dp", "rep"), None, None),
        P(("dp", "rep")),
        P("rep"),
        P("rep", None),
        P("rep"),
        P("rep", None),
        P("rep"),
        P("rep", None),
        P("rep"),
        P("rep", None),
        P(),
        P(),
        P(),
        P(),
        P(),
        P(),
        P(),
        P(),
        P(),
    )
    out_specs = (
        P(("dp", "rep")),
        P(("dp", "rep"), None, None),
        P("rep"),
        P(None, "rep"),
        P("rep"),
        P(None, "rep"),
        P("rep"),
        P(None, "rep"),
        P("rep"),
        P(None, "rep"),
    )
    return jax.shard_map(local, mesh=mesh, in_specs=in_specs, out_specs=out_specs, check_vma=False)
```

```python
import functools
import math

import jax
import jax.numpy as jnp
from jax import lax
from jax.experimental import pallas as pl
from jax.experimental.pallas import tpu as pltpu
from jax.sharding import PartitionSpec as P

D = 768
HEADS = 12
FF = 3072
ILEN = 145
LOWLEN = 50
CAP = 16

SCALE = 100.0
EPS = 1e-06
NEGATIVE = -1e30
LOG2E = math.log2(math.e)
MOST_PAIRS = 2048

UNIT = 160
UNITS = 2
PART = 48
SPAN = 29
QB = 128
BW = 3 * D // 2 + D // 2 + 128
EARLY = D + 128
CHUNKS = 16

f32 = jnp.float32
bf16 = jnp.bfloat16


def dot(left_side, right_side):
    return jnp.dot(left_side, right_side, preferred_element_type=f32)


def dot_nt(left_side, right_side):
    return lax.dot_general(
        left_side, right_side, (((1,), (1,)), ((), ())), preferred_element_type=f32
    )


def dot_tn(left_side, right_side):
    return lax.dot_general(
        left_side, right_side, (((0,), (0,)), ((), ())), preferred_element_type=f32
    )


def normalize(values):
    center = values - jnp.mean(values, -1, keepdims=True)
    inverse = lax.rsqrt(jnp.mean(center * center, -1, keepdims=True) + EPS)
    return center * inverse, inverse


def norm_back(grad, normed, inverse):
    return inverse * (
        grad
        - jnp.mean(grad, -1, keepdims=True)
        - normed * jnp.mean(grad * normed, -1, keepdims=True)
    )


def normal_cdf(values):
    return 0.5 + 0.5 * lax.erf(values * (1.0 / math.sqrt(2.0)))


def split_low(values):
    big = values.astype(bf16)
    return big, (values - big.astype(f32)).astype(bf16)


def tower_kernel(
    groups_ref,
    mine_ref,
    x_hbm,
    vec_own_ref,
    vec_other_ref,
    qkv_own,
    qkv_other,
    out_own,
    out_other,
    up_own,
    up_other,
    down_own,
    down_other,
    emb_ref,
    order,
    x_ref,
    x_wide,
    wqkv,
    wout,
    wup,
    wdown,
    gain_a,
    bqkv,
    gain_m,
    bup,
    xs,
    qkv,
    mixed,
    asum,
    hsum,
    aparts,
    hparts,
    scores,
    attention,
    sems,
):
    total = x_ref.shape[1]
    pitch = total + 8
    mine = mine_ref[0]
    copies = []
    for k in range(ILEN // SPAN):
        span = pl.ds(k * SPAN, SPAN)
        copies.append(pltpu.make_async_copy(x_hbm.at[span], x_ref.at[span], sems.at[8 + k]))
    for k, (own, other, whole) in enumerate(
        (
            (qkv_own, qkv_other, wqkv),
            (out_own, out_other, wout),
            (up_own, up_other, wup),
            (down_own, down_other, wdown),
        )
    ):
        half = own.shape[0]
        copies.append(
            pltpu.make_async_copy(own, whole.at[pl.ds(mine * half, half)], sems.at[2 * k])
        )
        copies.append(
            pltpu.make_async_copy(
                other, whole.at[pl.ds((1 - mine) * half, half)], sems.at[2 * k + 1]
            )
        )
    for copy in copies:
        copy.start()

    vec_own = vec_own_ref[...].astype(f32)
    vec_other = vec_other_ref[...].astype(f32)
    low = jnp.where(mine == 0, vec_own, vec_other)
    high = jnp.where(mine == 0, vec_other, vec_own)
    start = 0
    for dest, size, at in (
        (gain_a, D // 2, (0, D // 2)),
        (bqkv, D, (0, 2 * D)),
        (gain_m, D // 2, (0, D // 2)),
        (bup, FF // 2, (0, FF // 2)),
    ):
        dest[:, at[0] : at[0] + size] = low[:, start : start + size]
        dest[:, at[1] : at[1] + size] = high[:, start : start + size]
        start += size
    bqkv[:, D : 2 * D] = jnp.zeros((1, D), f32)

    def count(i, found):
        return found + groups_ref[i]

    n_hi = lax.fori_loop(0, total, count, 0)

    def place_one(i, state):
        hi, lo = state
        group = groups_ref[i]
        order[jnp.where(group == 1, hi, lo)] = i
        return hi + group, lo + 1 - group

    lax.fori_loop(0, total, place_one, (0, n_hi))
    n_units = n_hi + (total - n_hi + 2) // 3

    xs[...] = jnp.zeros_like(xs)
    first = lax.broadcasted_iota(jnp.int32, (1, 128), 1) < 64
    key_at = lax.broadcasted_iota(jnp.int32, (UNIT, UNIT), 1)
    row_at = lax.broadcasted_iota(jnp.int32, (UNIT, UNIT), 0)
    sub = lax.broadcasted_iota(jnp.int32, (8, 1), 0)

    def place(unit, k):
        last = jnp.minimum(unit, n_units - 1)
        is_hi = last < n_hi
        where = jnp.where(is_hi, last, n_hi + 3 * (last - n_hi) + k)
        return order[jnp.minimum(where, total - 1)], is_hi

    def keep_parts(values, j, dest, col, width):
        rows = values.reshape(UNIT // 8, 8, width)
        parts = [
            jnp.sum(rows[0:6], 0),
            rows[6],
            jnp.sum(rows[7:12], 0),
            rows[12],
            jnp.sum(rows[13:18], 0),
            rows[18],
        ]
        for k, part in enumerate(parts):
            dest[j * PART + k * 8 : j * PART + k * 8 + 8, col : col + width] = part

    loads = copies[: ILEN // SPAN]
    copies = copies[ILEN // SPAN :]

    def widen(t, carry):
        for panel in range(D // 128):
            x_wide[panel, pl.ds(pl.multiple_of(t * pitch, 8), total), :] = x_ref[
                t, :, panel * 128 : (panel + 1) * 128
            ].astype(f32)
        return carry

    for k, load in enumerate(loads):
        load.wait()
        lax.fori_loop(k * SPAN, (k + 1) * SPAN, widen, 0)
    for copy in copies[:2]:
        copy.wait()

    def body(step, carry):
        for j in range(UNITS):
            unit = step * UNITS + j
            one, is_hi = place(unit, 0)
            two, three = place(unit, 1)[0], place(unit, 2)[0]
            base = j * UNIT

            @pl.when(is_hi)
            def _():
                for panel in range(D // 128):
                    xs[base : base + ILEN, panel * 128 : (panel + 1) * 128] = x_wide[
                        panel, pl.ds(one, ILEN, stride=pitch), :
                    ]

            @pl.when(jnp.logical_not(is_hi))
            def _():
                for k, index in enumerate((one, two, three)):
                    for panel in range(D // 128):
                        xs[
                            base + LOWLEN * k : base + LOWLEN * (k + 1),
                            panel * 128 : (panel + 1) * 128,
                        ] = x_wide[panel, pl.ds(index, LOWLEN, stride=pitch), :]

        low_rows = (normalize(xs[...])[0] * gain_a[...]).astype(bf16)
        for col in range(0, 3 * D, 256):
            values = dot(low_rows, wqkv[:, col : col + 256]) + bqkv[:, col : col + 256]
            if col < D:
                values = values * (LOG2E / 8.0)
            qkv[:, col : col + 256] = values.astype(bf16)

        @pl.when(step == 0)
        def _():
            for copy in copies[2:6]:
                copy.wait()

        for j in range(UNITS):
            is_hi = place(step * UNITS + j, 0)[1]
            base = j * UNIT
            key_seg = jnp.where(key_at < LOWLEN, 0, jnp.where(key_at < 2 * LOWLEN, 1, 2))
            row_seg = jnp.where(row_at < LOWLEN, 0, jnp.where(row_at < 2 * LOWLEN, 1, 2))
            short_ok = jnp.logical_and(key_seg == row_seg, key_at < 3 * LOWLEN)
            allowed = jnp.where(
                is_hi, (key_at < ILEN).astype(jnp.int32), short_ok.astype(jnp.int32)
            )
            bias = jnp.where(allowed > 0, 0.0, NEGATIVE)
            for p in range(HEADS // 2):
                query = qkv[base : base + UNIT, p * 128 : (p + 1) * 128]
                key = qkv[base : base + UNIT, D + p * 128 : D + (p + 1) * 128]
                for h in range(2):
                    head = first if h == 0 else jnp.logical_not(first)
                    at = (j * HEADS + 2 * p + h) * UNIT
                    scores[at : at + UNIT, :] = (
                        dot_nt(jnp.where(head, query, jnp.zeros_like(query)), key) + bias
                    )
        for j in range(UNITS):
            part = slice(j * HEADS * UNIT, (j + 1) * HEADS * UNIT)
            values = scores[part, :]
            powers = jnp.exp2(values - jnp.max(values, 1, keepdims=True))
            attention[part, :] = powers.astype(bf16)
        for j in range(UNITS):
            base = j * UNIT
            for p in range(HEADS // 2):
                lanes = slice(p * 128, (p + 1) * 128)
                value = qkv[base : base + UNIT, 2 * D + p * 128 : 2 * D + (p + 1) * 128]
                outs = []
                at = (j * HEADS + 2 * p) * UNIT
                value_one = jnp.concatenate([value, jnp.ones_like(value)], 1)
                for h in range(2):
                    summed = dot(attention[at + h * UNIT : at + (h + 1) * UNIT, :], value_one)
                    outs.append(summed[:, :128] / summed[:, 128:])
                mixed[base : base + UNIT, lanes] = jnp.where(first, outs[0], outs[1]).astype(bf16)
        for col in range(0, D, 256):
            xs[:, col : col + 256] += dot(mixed[...], wout[:, col : col + 256])
        for j in range(UNITS):
            keep_parts(xs[j * UNIT : (j + 1) * UNIT, :], j, aparts, 0, D)
        low_two = (normalize(xs[...])[0] * gain_m[...]).astype(bf16)
        width = 1024
        for col in range(0, FF, width):
            pre_act = dot(low_two, wup[:, col : col + width]) + bup[:, col : col + width]
            hidden = pre_act * normal_cdf(pre_act)
            for j in range(UNITS):
                keep_parts(hidden[j * UNIT : (j + 1) * UNIT], j, hparts, col, width)
        for j in range(UNITS):
            unit = step * UNITS + j
            one, is_hi = place(unit, 0)
            two, three = place(unit, 1)[0], place(unit, 2)[0]

            def rows_of(index):
                return pl.ds(pl.multiple_of(index * 8, 8), 8)

            @pl.when(is_hi)
            def _():
                for src, dest in ((aparts, asum), (hparts, hsum)):
                    part = [src[j * PART + k * 8 : j * PART + k * 8 + 8, :] for k in range(6)]
                    dest[rows_of(one), :] = (
                        (part[0] + part[1])
                        + (part[2] + part[3])
                        + (part[4] + jnp.where(sub < 1, part[5], 0.0))
                    )

            @pl.when(jnp.logical_not(is_hi))
            def _():
                for src, dest in ((aparts, asum), (hparts, hsum)):
                    part = [src[j * PART + k * 8 : j * PART + k * 8 + 8, :] for k in range(6)]
                    dest[rows_of(three), :] = (
                        jnp.where(sub < 4, 0.0, part[3])
                        + part[4]
                        + jnp.where(sub < 6, part[5], 0.0)
                    )
                    dest[rows_of(two), :] = (
                        jnp.where(sub < 2, 0.0, part[1])
                        + part[2]
                        + jnp.where(sub < 4, part[3], 0.0)
                    )
                    dest[rows_of(one), :] = part[0] + jnp.where(sub < 2, part[1], 0.0)

        return carry

    lax.fori_loop(0, (n_units + UNITS - 1) // UNITS, body, 0)
    for copy in copies[6:]:
        copy.wait()
    which = lax.broadcasted_iota(jnp.int32, (total, 128), 0)
    scale = jnp.zeros((total, 128), f32)
    for i in range(total):
        scale = jnp.where(
            which == i, jnp.where(groups_ref[i] == 1, 1.0 / ILEN, 1.0 / LOWLEN), scale
        )
    scale = scale[:, 0:1]
    big, rest = split_low(jnp.sum(hsum[...].reshape(total, 8, FF), 1) * scale)
    product = dot(jnp.concatenate([big, rest], 0), wdown[...])
    pooled = jnp.sum(asum[...].reshape(total, 8, D), 1) * scale + product[:total] + product[total:]
    emb_ref[...] = (
        pooled * lax.rsqrt(jnp.sum(pooled * pooled, -1, keepdims=True) + EPS)
    ).astype(bf16)


VM = pl.BlockSpec(memory_space=pltpu.VMEM)
SM = pl.BlockSpec(memory_space=pltpu.SMEM)
ANY = pl.BlockSpec(memory_space=pltpu.HBM)


def limit(mebibytes):
    return pltpu.CompilerParams(vmem_limit_bytes=mebibytes * 1024 * 1024)


def image_tower(images, groups, mine, vec_own, vec_other, weights):
    number = images.shape[1]
    rows = UNITS * UNIT
    flops = number * 100 * 2 * (4 * D * D + D * FF)
    return pl.pallas_call(
        tower_kernel,
        out_shape=jax.ShapeDtypeStruct((number, D), bf16),
        in_specs=[SM, SM, ANY, VM, VM] + [ANY] * 8,
        out_specs=VM,
        scratch_shapes=[
            pltpu.SMEM((number,), jnp.int32),
            pltpu.VMEM(images.shape, bf16),
            pltpu.VMEM((D // 128, ILEN * (number + 8), 128), f32),
            pltpu.VMEM((D, 3 * D), bf16),
            pltpu.VMEM((D, D), bf16),
            pltpu.VMEM((D, FF), bf16),
            pltpu.VMEM((FF, D), bf16),
            pltpu.VMEM((1, D), f32),
            pltpu.VMEM((1, 3 * D), f32),
            pltpu.VMEM((1, D), f32),
            pltpu.VMEM((1, FF), f32),
            pltpu.VMEM((rows, D), f32),
            pltpu.VMEM((rows, 3 * D), bf16),
            pltpu.VMEM((rows, D), bf16),
            pltpu.VMEM((number * 8, D), f32),
            pltpu.VMEM((number * 8, FF), f32),
            pltpu.VMEM((UNITS * PART, D), f32),
            pltpu.VMEM((UNITS * PART, FF), f32),
            pltpu.VMEM((UNITS * HEADS * UNIT, UNIT), f32),
            pltpu.VMEM((UNITS * HEADS * UNIT, UNIT), bf16),
            pltpu.SemaphoreType.DMA((8 + ILEN // SPAN,)),
        ],
        compiler_params=limit(58),
        cost_estimate=pl.CostEstimate(
            flops=flops, bytes_accessed=24 * 1024 * 1024, transcendentals=0
        ),
        name="image_tower",
    )(groups, mine, images, vec_own, vec_other, *weights)


def lens_along(lens_ref, start, number):
    owner = lax.broadcasted_iota(jnp.int32, (1, number * CAP), 1) // CAP
    lens = jnp.zeros((1, number * CAP), jnp.int32)
    for c in range(number):
        lens = jnp.where(owner == c, lens_ref[start + c], lens)
    return lens


def score_bias(lens_ref, block):
    per = QB // CAP
    position = lax.broadcasted_iota(jnp.int32, (1, QB), 1) % CAP
    valid = position < lens_along(lens_ref, block * per, per)
    rows = lax.broadcasted_iota(jnp.int32, (QB, QB), 0) // CAP
    columns = lax.broadcasted_iota(jnp.int32, (QB, QB), 1) // CAP
    return jnp.where(jnp.logical_and(rows == columns, valid), 0.0, NEGATIVE)


def forward_kernel(
    lens_ref,
    x_ref,
    vec_ref,
    wqkv_ref,
    wout_ref,
    wup_ref,
    wdown_ref,
    qkv,
    mixed,
    after,
    mlp,
    slope,
    attention,
    early,
    hidden,
    scores,
):
    rows = x_ref.shape[0]
    number = rows // CAP
    first = lax.broadcasted_iota(jnp.int32, (1, 128), 1) < 64
    normed, _ = normalize(x_ref[...].astype(f32))
    low = (normed * vec_ref[:, 0:D]).astype(bf16)
    for col in range(0, 3 * D, 256):
        values = dot(low, wqkv_ref[:, col : col + 256])
        if col < D:
            values = values + vec_ref[:, D + col : D + col + 256]
        if col >= 2 * D:
            values = values + vec_ref[:, col : col + 256]
        values = values.astype(bf16)
        if col < D:
            values = values * jnp.asarray(0.125, bf16)
        qkv[:, col : col + 256] = values
    for block in range(rows // QB):
        bias = score_bias(lens_ref, block)
        span = slice(block * QB, (block + 1) * QB)
        for p in range(HEADS // 2):
            query = qkv[span, p * 128 : (p + 1) * 128]
            key = qkv[span, D + p * 128 : D + (p + 1) * 128]
            for h in range(2):
                head = first if h == 0 else jnp.logical_not(first)
                at = (block * HEADS + 2 * p + h) * QB
                scores[at : at + QB, :] = (
                    dot_nt(jnp.where(head, query, jnp.zeros_like(query)), key) * LOG2E + bias
                )
    for block in range(rows // QB):
        part = slice(block * HEADS * QB, (block + 1) * HEADS * QB)
        values = scores[part, :]
        powers = jnp.exp2(values - jnp.max(values, 1, keepdims=True))
        attention[part, :] = (powers * (1.0 / jnp.sum(powers, 1, keepdims=True))).astype(bf16)
    for block in range(rows // QB):
        span = slice(block * QB, (block + 1) * QB)
        for p in range(HEADS // 2):
            value = qkv[span, 2 * D + p * 128 : 2 * D + (p + 1) * 128]
            at = (block * HEADS + 2 * p) * QB
            outs = [dot(attention[at + h * QB : at + (h + 1) * QB, :], value) for h in range(2)]
            mixed[span, p * 128 : (p + 1) * 128] = jnp.where(first, outs[0], outs[1]).astype(bf16)
    for col in range(0, D, 256):
        after[:, col : col + 256] = x_ref[:, col : col + 256].astype(f32) + dot(
            mixed[...], wout_ref[:, col : col + 256]
        )
    mlp[...] = (normalize(after[...])[0] * vec_ref[:, 3 * D : 4 * D]).astype(bf16)
    lens = lens_along(lens_ref, 0, number)
    position = lax.broadcasted_iota(jnp.int32, (1, rows), 1)
    owner = (
        lax.broadcasted_iota(jnp.int32, (number, rows), 0)
        == lax.broadcasted_iota(jnp.int32, (number, rows), 1) // CAP
    )
    members = jnp.where(jnp.logical_and(owner, position % CAP < lens), 1.0, 0.0)
    pool = members.astype(bf16)
    count = jnp.sum(members, 1, keepdims=True)
    width = 512
    for col in range(0, FF, width):
        span = slice(col, col + width)
        pre_act = dot(mlp[...], wup_ref[:, span]) + vec_ref[:, 4 * D + col : 4 * D + col + width]
        phi = normal_cdf(pre_act)
        hidden[:, span] = (pre_act * phi).astype(bf16)
        density = jnp.exp2(pre_act * pre_act * (-0.5 * LOG2E)) * (1.0 / math.sqrt(2.0 * math.pi))
        slope[:, span] = (phi + pre_act * density).astype(bf16)
    big, rest = split_low(dot(pool, hidden[...]))
    after_big, after_rest = split_low(after[...])
    pooled = (
        dot(pool, after_big)
        + dot(pool, after_rest)
        + dot(big, wdown_ref[...])
        + dot(rest, wdown_ref[...])
    )
    early[:, 0:D] = (pooled / count).astype(bf16)
    early[:, D:EARLY] = jnp.broadcast_to(count, (number, EARLY - D)).astype(bf16)
    early[:, EARLY:] = big


def text_forward(captions, lens, vec, w_qkv, w_out, w_up, w_down):
    rows = captions.shape[0]
    shape = jax.ShapeDtypeStruct
    return pl.pallas_call(
        forward_kernel,
        out_shape=[
            shape((rows, 3 * D), bf16),
            shape((rows, D), bf16),
            shape((rows, D), f32),
            shape((rows, D), bf16),
            shape((rows, FF), bf16),
            shape((rows * HEADS, QB), bf16),
            shape((rows // CAP, EARLY + FF), bf16),
        ],
        in_specs=[SM] + [VM] * 6,
        out_specs=[VM] * 7,
        scratch_shapes=[pltpu.VMEM((rows, FF), bf16), pltpu.VMEM((rows * HEADS, QB), f32)],
        compiler_params=limit(50),
        cost_estimate=pl.CostEstimate(
            flops=2 * rows * (4 * D * D + 2 * D * FF),
            bytes_accessed=24 * 1024 * 1024,
            transcendentals=0,
        ),
        name="text_forward",
    )(lens, captions, vec, w_qkv, w_out, w_up, w_down)


def put_chunks(dest, values, place_ref, stream, col):
    rows = values.shape[0] // CHUNKS
    for chunk in range(CHUNKS):
        at = pl.multiple_of(place_ref[stream, chunk] * rows, 16)
        dest[pl.ds(at, rows), col : col + values.shape[1]] = values[
            chunk * rows : (chunk + 1) * rows
        ].astype(dest.dtype)


def up_kernel(
    place_ref, mine_ref, lens_ref, branch_ref, slope_ref, mlp_ref, wdown_ref,
    grad_pre, own, other, grad_bup, grad_hidden, mlp_t,
):
    number = slope_ref.shape[0] // CAP
    half = FF // 2
    mine = mine_ref[0]
    for col in range(0, FF, 512):
        grad_hidden[:, col : col + 512] = dot_nt(branch_ref[...], wdown_ref[col : col + 512, :])
    position = lax.broadcasted_iota(jnp.int32, (CAP, 1), 0)
    for c in range(number):
        span = slice(c * CAP, (c + 1) * CAP)
        keep = jnp.where(position < lens_ref[c], 1.0, 0.0)
        grad_pre[span, :] = (
            grad_hidden[c : c + 1, :] * slope_ref[span, :].astype(f32) * keep
        ).astype(bf16)
    mlp_t[...] = mlp_ref[...].T
    for which, dest in ((1 - mine, other), (mine, own)):
        for col in range(0, half, 384):
            lanes = pl.ds(pl.multiple_of(which * half + col, 128), 384)
            put_chunks(dest, dot(mlp_t[...], grad_pre[:, lanes]), place_ref, 2 * col // half, col)
    for col in range(0, FF, 512):
        grad_bup[:, col : col + 512] = jnp.sum(
            grad_pre[:, col : col + 512].astype(f32), 0, keepdims=True
        )


def up_backward(place, mine, lens, branch, slope, mlp, w_down):
    rows = slope.shape[0]
    shape = jax.ShapeDtypeStruct
    return pl.pallas_call(
        up_kernel,
        out_shape=[
            shape((rows, FF), bf16),
            shape((D, FF // 2), f32),
            shape((D, FF // 2), bf16),
            shape((1, FF), f32),
        ],
        in_specs=[SM, SM, SM] + [VM] * 4,
        out_specs=[VM] * 4,
        scratch_shapes=[pltpu.VMEM((rows // CAP, FF), f32), pltpu.VMEM((D, rows), bf16)],
        compiler_params=limit(32),
        cost_estimate=pl.CostEstimate(
            flops=2 * rows * D * FF, bytes_accessed=20 * 1024 * 1024, transcendentals=0
        ),
        name="up_backward",
    )(place, mine, lens, branch, slope, mlp, w_down)


def mlp_kernel(
    lens_ref, pre_ref, grad_ref, after_ref, vec_ref, wup_ref, wout_ref,
    grad_after, grad_mixed, grad_gain, grad_out,
):
    number = after_ref.shape[0] // CAP
    grad_mlp = dot_nt(pre_ref[...], wup_ref[...])
    normed_two, inverse_two = normalize(after_ref[...])
    grad_gain[...] = jnp.sum(grad_mlp * normed_two, 0, keepdims=True)
    grad_after[...] = norm_back(grad_mlp * vec_ref[:, 3 * D : 4 * D], normed_two, inverse_two)
    position = lax.broadcasted_iota(jnp.int32, (CAP, 1), 0)
    for c in range(number):
        keep = jnp.where(position < lens_ref[c], 1.0, 0.0)
        grad_after[c * CAP : (c + 1) * CAP, :] += grad_ref[c : c + 1, :] * keep
    grad_out[...] = grad_after[...].astype(bf16)
    for col in range(0, D, 256):
        grad_mixed[:, col : col + 256] = dot_nt(
            grad_out[...], wout_ref[col : col + 256, :]
        ).astype(bf16)


def mlp_backward(lens, grad_pre, grads, after, vec, w_up, w_out):
    rows = after.shape[0]
    shape = jax.ShapeDtypeStruct
    return pl.pallas_call(
        mlp_kernel,
        out_shape=[shape((rows, D), f32), shape((rows, D), bf16), shape((1, D), f32)],
        in_specs=[SM] + [VM] * 6,
        out_specs=[VM] * 3,
        scratch_shapes=[pltpu.VMEM((rows, D), bf16)],
        compiler_params=limit(36),
        cost_estimate=pl.CostEstimate(
            flops=2 * rows * (D * D + D * FF), bytes_accessed=20 * 1024 * 1024, transcendentals=0
        ),
        name="mlp_backward",
    )(lens, grad_pre, grads, after, vec, w_up, w_out)


def attention_kernel(
    qkv_ref, att_ref, mixed_ref, grad_ref, grad_proj, grad_att, means, grad_s, *, start
):
    first = lax.broadcasted_iota(jnp.int32, (1, 128), 1) < 64
    ones = jnp.ones((128, QB), bf16)
    heads = (first, jnp.logical_not(first))
    blocks = grad_proj.shape[0] // QB
    for block in range(blocks):
        span = slice(start + block * QB, start + (block + 1) * QB)
        for p in range(HEADS // 2):
            at = p * 128
            value = qkv_ref[span, 2 * D + at : 2 * D + at + 128]
            grad = grad_ref[span, at : at + 128]
            product = (grad.astype(f32) * mixed_ref[span, at : at + 128].astype(f32)).astype(bf16)
            for h, head in enumerate(heads):
                to = (block * HEADS + 2 * p + h) * QB
                grad_att[to : to + QB, :] = dot_nt(
                    jnp.where(head, grad, jnp.zeros_like(grad)), value
                )
                means[to : to + QB, :] = dot(
                    jnp.where(head, product, jnp.zeros_like(product)), ones
                )
    for block in range(blocks):
        part = slice(block * HEADS * QB, (block + 1) * HEADS * QB)
        place = (start // QB + block) * HEADS * QB
        low = att_ref[place : place + HEADS * QB, :].astype(f32)
        grad_s[part, :] = (low * (grad_att[part, :] - means[part, :])).astype(bf16)
    for block in range(blocks):
        span = slice(start + block * QB, start + (block + 1) * QB)
        dest = slice(block * QB, (block + 1) * QB)
        for p in range(HEADS // 2):
            at = p * 128
            query = qkv_ref[span, at : at + 128]
            key = qkv_ref[span, D + at : D + at + 128]
            grad = grad_ref[span, at : at + 128]
            grad_q, grad_k, grad_v = [], [], []
            for h in range(2):
                to = (block * HEADS + 2 * p + h) * QB
                place = ((start // QB + block) * HEADS + 2 * p + h) * QB
                sgrad = grad_s[to : to + QB, :]
                grad_q.append(dot(sgrad, key))
                grad_k.append(dot_tn(sgrad, query))
                grad_v.append(dot_tn(att_ref[place : place + QB, :], grad))
            for k, (parts, scale) in enumerate(((grad_q, 0.125), (grad_k, 1.0), (grad_v, 1.0))):
                grad_proj[dest, k * D + at : k * D + at + 128] = (
                    jnp.where(first, parts[0], parts[1]) * scale
                ).astype(bf16)


def attention_backward(qkv, attention, mixed, grad_mixed, start, rows):
    return pl.pallas_call(
        functools.partial(attention_kernel, start=start),
        out_shape=jax.ShapeDtypeStruct((rows, 3 * D), bf16),
        in_specs=[VM] * 4,
        out_specs=VM,
        scratch_shapes=[
            pltpu.VMEM((rows * HEADS, QB), f32),
            pltpu.VMEM((rows * HEADS, QB), f32),
            pltpu.VMEM((rows * HEADS, QB), bf16),
        ],
        compiler_params=limit(28),
        cost_estimate=pl.CostEstimate(
            flops=2 * rows * 24 * D * D, bytes_accessed=40 * 1024 * 1024, transcendentals=0
        ),
        name="attention_backward",
    )(qkv, attention, mixed, grad_mixed)


def input_kernel(
    proj_ref, after_ref, x_ref, vec_ref, gain_ref, bup_ref, wqkv_ref, caption_grad, sums, input_low
):
    gain_a = vec_ref[:, 0:D]
    normed_one, inverse_one = normalize(x_ref[...].astype(f32))
    input_low[...] = (normed_one * gain_a).astype(bf16)
    grad_in = dot_nt(proj_ref[...], wqkv_ref[...])
    sums[:, 0:D] = jnp.sum(grad_in * normed_one, 0, keepdims=True)
    sums[:, D : 2 * D] = jnp.sum(proj_ref[:, 0:D].astype(f32), 0, keepdims=True)
    sums[:, 2 * D : 3 * D] = jnp.sum(proj_ref[:, 2 * D :].astype(f32), 0, keepdims=True)
    sums[:, 3 * D : 4 * D] = gain_ref[...]
    sums[:, 4 * D :] = bup_ref[...]
    caption_grad[...] = after_ref[...] + norm_back(grad_in * gain_a, normed_one, inverse_one)


def input_backward(grad_proj, grad_after, captions, vec, grad_gain, grad_bup, w_qkv):
    rows = captions.shape[0]
    shape = jax.ShapeDtypeStruct
    return pl.pallas_call(
        input_kernel,
        out_shape=[shape((rows, D), f32), shape((1, 4 * D + FF), f32), shape((rows, D), bf16)],
        in_specs=[VM] * 7,
        out_specs=[VM] * 3,
        compiler_params=limit(32),
        cost_estimate=pl.CostEstimate(
            flops=2 * rows * 12 * D * D, bytes_accessed=24 * 1024 * 1024, transcendentals=0
        ),
        name="input_backward",
    )(grad_proj, grad_after, captions, vec, grad_gain, grad_bup, w_qkv)


def proj_kernel(
    place_ref, mine_ref, proj_ref, after_ref, mixed_ref, input_ref, sums, own, other, lhs_t, grad_out
):
    chunk_rows = D // CHUNKS
    mine = mine_ref[0]
    lhs_t[...] = input_ref[...].T
    half_out, half_qkv = D // 2, 3 * D // 2
    for which, dest in ((1 - mine, other), (mine, own)):
        for col in range(0, half_qkv, 384):
            lanes = pl.ds(pl.multiple_of(which * half_qkv + col, 128), 384)
            put_chunks(dest, dot(lhs_t[...], proj_ref[:, lanes]), place_ref, col // 768, col)
    lhs_t[...] = mixed_ref[...].T
    grad_out[...] = after_ref[...].astype(bf16)
    for which, dest in ((1 - mine, other), (mine, own)):
        lanes = pl.ds(pl.multiple_of(which * half_out, 128), half_out)
        put_chunks(dest, dot(lhs_t[...], grad_out[:, lanes]), place_ref, 1, half_qkv)
    for which, dest in ((1 - mine, other), (mine, own)):
        dest[:, BW - 128 :] = jnp.zeros((D, 128), dest.dtype)
        pieces = []
        for start, size in ((0, D), (D, 2 * D), (3 * D, D), (4 * D, FF)):
            for k in range(0, size // 2, 128):
                at = pl.multiple_of(start + which * (size // 2) + k, 128)
                pieces.append(sums[:, pl.ds(at, 128)])
        pieces += [jnp.zeros_like(pieces[0])] * (32 - len(pieces))
        at = pl.multiple_of(place_ref[1, 0] * chunk_rows, 16)
        dest[pl.ds(at, 32), BW - 128 :] = jnp.concatenate(pieces, 0).astype(dest.dtype)


def proj_backward(place, mine, grad_proj, grad_after, mixed, input_low, sums):
    rows = mixed.shape[0]
    shape = jax.ShapeDtypeStruct
    return pl.pallas_call(
        proj_kernel,
        out_shape=[shape((D, BW), f32), shape((D, BW), bf16)],
        in_specs=[SM, SM] + [VM] * 5,
        out_specs=[VM] * 2,
        scratch_shapes=[pltpu.VMEM((D, rows), bf16), pltpu.VMEM((rows, D), bf16)],
        compiler_params=limit(30),
        cost_estimate=pl.CostEstimate(
            flops=2 * rows * 12 * D * D, bytes_accessed=30 * 1024 * 1024, transcendentals=0
        ),
        name="proj_backward",
    )(place, mine, grad_proj, grad_after, mixed, input_low, sums)


def dp_bits():
    bits, bit = [], 1
    while bit < lax.axis_size("dp"):
        bits.append(bit)
        bit *= 2
    return bits


def swap(values, axis, bit):
    size = lax.axis_size(axis)
    return lax.ppermute(values, axis, [(place, place ^ bit) for place in range(size)])


def gather_relative(values):
    bits = dp_bits()
    while bits:
        pair = bits[-2:]
        bits = bits[:-2]
        offsets = [0]
        for bit in pair:
            offsets += [entry + bit for entry in offsets]
        values = jnp.concatenate([swap(values, "dp", k) if k else values for k in offsets], 0)
    return jnp.concatenate([values, swap(values, "rep", 1)], 0)


def relative_chips():
    bits, table = dp_bits(), [0]
    while bits:
        pair = bits[-2:]
        bits = bits[:-2]
        offsets = [0]
        for bit in pair:
            offsets += [entry + bit for entry in offsets]
        table = [entry ^ k for k in offsets for entry in table]
    return table


def chunk_places():
    away = jnp.arange(CHUNKS, dtype=jnp.int32) ^ (lax.axis_index("dp") % CHUNKS)
    one, two, rest = away % 2, away // 2 % 2, away // 4
    return jnp.stack([one * 8 + two * 4 + rest, two * 8 + one * 4 + rest]).astype(jnp.int32)


def streams_of(width):
    return ((slice(0, width), 1, 2), (slice(width, None), 2, 1))


def reduce_first(own, arrived, streams):
    half = own.shape[0] // 2

    def both(rows, lanes):
        return own[rows, lanes] + arrived[rows, lanes].astype(f32)

    sent = [both(slice(half, None), lanes).astype(bf16) for lanes, _, _ in streams]
    return sent, [both(slice(0, half), lanes) for lanes, _, _ in streams]


def reduce_swaps(sent, streams, stage):
    return [swap(piece, "dp", stream[stage]) for piece, stream in zip(sent, streams)]


def reduce_add(came, kept):
    half = kept[0].shape[0] // 2
    totals = [total + got.astype(f32) for total, got in zip(kept, came)]
    return [total[half:].astype(bf16) for total in totals], [total[:half] for total in totals]


def reduce_join(came, kept):
    total = jnp.concatenate([total + got.astype(f32) for total, got in zip(kept, came)], 1)
    rows = total.shape[0] // 4
    return [total[k * rows : (k + 1) * rows].astype(bf16) for k in (1, 2, 3)], total[:rows]


def reduce_last(parts, total):
    total = total + sum(part.astype(f32) for part in parts)
    for bit in dp_bits()[4:]:
        total = total + swap(total.astype(bf16), "dp", bit).astype(f32)
    return total.astype(bf16)


def spread_first(chunk):
    return [swap(chunk, "dp", 4 * k) if k else chunk for k in range(4)]


def spread_second(column, streams):
    return [jnp.concatenate([piece[:, lanes] for piece in column], 0) for lanes, _, _ in streams]


def spread_third(mine, near, streams):
    quarters = []
    for own, next_to, (_, one, _) in zip(mine, near, streams):
        quarters += [own, next_to, swap(own, "dp", one), swap(next_to, "dp", one)]
    return quarters


def unpack_kernel(place_ref, *refs):
    parts = refs[:16]
    g_up, g_qkv, g_out = refs[16:19]
    vectors = refs[19:]
    rows = D // CHUNKS
    place = place_ref[0, 0]
    me = place // 8 + 2 * (place // 4 % 2) + 4 * (place % 4)
    for stream in range(2):
        for quarter in range(4):
            for k in range(4):
                high, low = quarter // 2, quarter % 2
                away = (high + 2 * low if stream == 0 else low + 2 * high) + 4 * k
                chunk = me ^ away
                at = pl.ds(pl.multiple_of(chunk * rows, 16), rows)
                span = slice(k * rows, (k + 1) * rows)
                lanes = slice(stream * FF // 4, (stream + 1) * FF // 4)
                g_up[at, lanes] = parts[stream * 4 + quarter][span, :].astype(f32)
                rest = parts[8 + stream * 4 + quarter][span, :].astype(f32)
                if stream == 0:
                    g_qkv[at, 0:D] = rest
                    continue
                g_qkv[at, D:] = rest[:, : D // 2]
                g_out[at, :] = rest[:, D // 2 : D]

                @pl.when(chunk == 0)
                def _():
                    row = 0
                    for dest in vectors:
                        for lane in range(0, dest.shape[0], 128):
                            dest[lane : lane + 128] = rest[row, D:]
                            row += 1


def unpack(place, ups, rests):
    shape = jax.ShapeDtypeStruct
    return pl.pallas_call(
        unpack_kernel,
        out_shape=[
            shape((D, FF // 2), f32),
            shape((D, 3 * D // 2), f32),
            shape((D, D // 2), f32),
            shape((D // 2,), f32),
            shape((D,), f32),
            shape((D // 2,), f32),
            shape((FF // 2,), f32),
        ],
        in_specs=[SM] + [VM] * 16,
        out_specs=[VM] * 7,
        compiler_params=limit(26),
        name="unpack",
    )(place, *ups, *rests)


def softmax_parts(scores, axis):
    maxima = jnp.max(scores, axis, keepdims=True)
    powers = jnp.exp(scores - maxima)
    totals = jnp.sum(powers, axis, keepdims=True)
    return powers / totals, maxima + jnp.log(totals)


def text_unit(pooled_low, text_proj):
    proj_out = dot(pooled_low, text_proj)
    inverse_z = lax.rsqrt(jnp.sum(proj_out * proj_out, -1, keepdims=True) + EPS)
    return proj_out * inverse_z, inverse_z


def branch_grad(grad_unit, unit_text, inverse_z, text_proj, lengths):
    grad_projout = (
        inverse_z * (grad_unit - unit_text * jnp.sum(unit_text * grad_unit, -1, keepdims=True))
    ).astype(bf16)
    return dot_nt(grad_projout, text_proj) / lengths


def loss_kernel(
    where_ref, early_hbm, image_ref, proj_ref, pair_loss, own_grads, own_branch, branch,
    unit, inverse, scores, sgrad, early_ref, sem,
):
    copy = pltpu.make_async_copy(early_hbm.at[:, pl.ds(0, EARLY)], early_ref, sem)
    copy.start()
    copy.wait()
    total = image_ref.shape[0]
    number = own_grads.shape[0]
    chip, mine = where_ref[0], where_ref[1]
    block = 256
    for row in range(0, total, block):
        span = slice(row, row + block)
        proj_out = dot(early_ref[span, 0:D], proj_ref[...])
        inverse_z = lax.rsqrt(jnp.sum(proj_out * proj_out, -1, keepdims=True) + EPS)
        inverse[span, :] = jnp.broadcast_to(inverse_z, (block, 128))
        unit[span, :] = proj_out * inverse_z
        scores[span, :] = dot_nt(unit[span, :].astype(bf16), image_ref[...]) * SCALE
    place = lax.broadcasted_iota(jnp.int32, (1, total), 1) // number
    chips = total // (2 * number)
    away = place % chips
    other = place // chips
    from_chip = chip ^ (away // 4 + 4 * (away % 4)) if chips == 16 else None
    image_id = (from_chip * 2 + (mine ^ other)) * number + (
        lax.broadcasted_iota(jnp.int32, (1, total), 1) % number
    )
    column_max = jnp.max(scores[...], 0, keepdims=True)
    column_sum = jnp.zeros((1, total), f32)
    for row in range(0, total, block):
        column_sum += jnp.sum(
            jnp.exp(scores[row : row + block, :] - column_max), 0, keepdims=True
        )
    column_total = column_max + jnp.log(column_sum)
    for row in range(0, total, block):
        span = slice(row, row + block)
        values = scores[span, :]
        row_max = jnp.max(values, 1, keepdims=True)
        powers = jnp.exp(values - row_max)
        by_text = powers * (0.5 / jnp.sum(powers, 1, keepdims=True))
        by_image = jnp.exp(values - column_max) * (0.5 / column_sum)
        text_id = lax.broadcasted_iota(jnp.int32, (block, 1), 0) + row
        same = jnp.where(text_id == image_id, 1.0, 0.0)
        sgrad[span, :] = (by_text + by_image - same).astype(bf16)
        grad_unit = dot(sgrad[span, :], image_ref[...]) * SCALE
        unit_text = unit[span, :]
        grad_proj = (
            inverse[span, 0:1]
            * (grad_unit - unit_text * jnp.sum(unit_text * grad_unit, -1, keepdims=True))
        ).astype(bf16)
        unit[span, :] = dot_nt(grad_proj, proj_ref[...]) / early_ref[span, D : D + 1].astype(f32)
        branch[span, :] = unit[span, :].astype(bf16)
    first = pl.multiple_of((chip * 2 + mine) * number, 32)
    own_grads[...] = unit[pl.ds(first, number), :]
    own_branch[...] = unit[pl.ds(first, number), :].astype(bf16)
    values = scores[pl.ds(first, number), :]
    row_max = jnp.max(values, 1, keepdims=True)
    row_total = row_max + jnp.log(jnp.sum(jnp.exp(values - row_max), 1, keepdims=True))
    text_id = lax.broadcasted_iota(jnp.int32, (number, 1), 0) + first
    same = jnp.where(text_id == image_id, 1.0, 0.0)
    both = 0.5 * (row_total + column_total) - values
    pair_loss[...] = jnp.broadcast_to(jnp.sum(both * same, 1, keepdims=True), (number, 128))


def loss_whole(early_all, image_all, text_proj, chip, mine, number):
    total = image_all.shape[0]
    shape = jax.ShapeDtypeStruct
    pair_loss, grads, own_branch, branch = pl.pallas_call(
        loss_kernel,
        out_shape=[
            shape((number, 128), f32),
            shape((number, D), f32),
            shape((number, D), bf16),
            shape((total, D), bf16),
        ],
        in_specs=[SM, ANY, VM, VM],
        out_specs=[VM] * 4,
        scratch_shapes=[
            pltpu.VMEM((total, D), f32),
            pltpu.VMEM((total, 128), f32),
            pltpu.VMEM((total, total), f32),
            pltpu.VMEM((total, total), bf16),
            pltpu.VMEM((total, EARLY), bf16),
            pltpu.SemaphoreType.DMA,
        ],
        compiler_params=limit(30),
        name="pair_loss",
    )(jnp.stack([chip, mine]), early_all, image_all, text_proj)
    return pair_loss[:, 0], grads, own_branch, branch


def loss_rows(pooled_all, image_all, text_proj, lengths_all, image_ids, first_row, local_pairs):
    unit_all, inverse_all = text_unit(pooled_all, text_proj)

    def own_rows(values):
        return lax.dynamic_slice_in_dim(values, first_row, local_pairs, 0)

    unit_text, inverse_z = own_rows(unit_all), own_rows(inverse_all)
    text_scores = dot_nt(unit_text.astype(bf16), image_all) * SCALE
    image_scores = dot_nt(image_all[:local_pairs], unit_all.astype(bf16)) * SCALE
    by_text, text_total = softmax_parts(text_scores, 1)
    image_total = softmax_parts(image_scores, 1)[1]
    every_total = gather_relative(image_total)
    text_ids = first_row + jnp.arange(local_pairs, dtype=jnp.int32)
    own_same = (text_ids[:, None] == image_ids).astype(f32)
    own = jnp.sum(text_scores * own_same, -1)
    pair_loss = 0.5 * (text_total[:, 0] - own) + 0.5 * (image_total[:, 0] - own)
    by_image = jnp.exp(text_scores - every_total[:, 0][None, :])
    sgrad = (0.5 * (by_text - own_same) + 0.5 * (by_image - own_same)).astype(bf16)
    grad_unit = dot(sgrad, image_all) * SCALE
    grads = branch_grad(grad_unit, unit_text, inverse_z, text_proj, own_rows(lengths_all))
    return pair_loss, grads, grads.astype(bf16), grads.astype(bf16)


def local(
    images,
    groups,
    captions,
    cap_lengths,
    img_gain_a,
    img_w_qkv,
    img_b_qv,
    img_w_out,
    img_gain_m,
    img_w_up,
    img_b_up,
    img_w_down,
    gain_attn,
    w_qkv,
    b_qv,
    w_out,
    gain_mlp,
    w_up,
    b_up,
    w_down,
    text_proj,
):
    local_pairs = images.shape[0]
    rows_total = local_pairs * CAP
    mine = lax.axis_index("rep").astype(jnp.int32)
    mine_one = mine[None]
    total_pairs = local_pairs * lax.axis_size("dp") * lax.axis_size("rep")
    whole = total_pairs <= MOST_PAIRS

    image_vec = jnp.concatenate([img_gain_a, img_b_qv, img_gain_m, img_b_up])[None]
    image_vec_other = swap(image_vec, "rep", 1)
    weights = []
    for weight in (img_w_qkv, img_w_out, img_w_up, img_w_down):
        weights += [weight, swap(weight, "rep", 1)]

    text_vec = lax.optimization_barrier(jnp.concatenate([gain_attn, b_qv, gain_mlp, b_up]))
    text_vec = text_vec.astype(f32)[None]
    flat = captions.reshape(rows_total, D)
    qkv, mixed, after, mlp, slope, attention, early = text_forward(
        flat, cap_lengths, text_vec, w_qkv, w_out, w_up, w_down
    )
    early, image_vec_other, *weights = lax.optimization_barrier((early, image_vec_other, *weights))
    early_all = lax.all_gather(
        early if whole else early[:, :EARLY], ("dp", "rep"), axis=0, tiled=True
    )
    image_emb = image_tower(
        jnp.transpose(images, (1, 0, 2)), groups, mine_one, image_vec, image_vec_other, weights
    )
    image_all = gather_relative(image_emb)
    chip = lax.axis_index("dp").astype(jnp.int32)
    if whole:
        pair_loss, grads, branch, branch_all = loss_whole(
            early_all, image_all, text_proj, chip, mine, local_pairs
        )
    else:
        chips = chip ^ jnp.array(relative_chips(), jnp.int32)
        devices = jnp.concatenate([2 * chips + mine, 2 * chips + 1 - mine])
        image_ids = (
            devices[:, None] * local_pairs + jnp.arange(local_pairs, dtype=jnp.int32)[None, :]
        ).reshape(1, total_pairs)
        pair_loss, grads, branch, branch_all = loss_rows(
            early_all[:, :D],
            image_all,
            text_proj,
            early_all[:, D : D + 1].astype(f32),
            image_ids,
            (2 * chip + mine) * local_pairs,
            local_pairs,
        )
    place = chunk_places()
    grad_pre, up_own, up_other, grad_bup = up_backward(
        place, mine_one, cap_lengths, branch, slope, mlp, w_down
    )
    arrived = swap(up_other, "rep", 1)
    grad_after, grad_mixed, grad_gain = mlp_backward(
        cap_lengths, grad_pre, grads, after, text_vec, w_up, w_out
    )
    up_streams = streams_of(FF // 4)
    up_sent, up_kept = reduce_first(up_own, arrived, up_streams)
    grad_mixed, *up_sent = lax.optimization_barrier((grad_mixed, *up_sent))
    grad_proj = attention_backward(qkv, attention, mixed, grad_mixed, 0, rows_total)
    up_came = reduce_swaps(up_sent, up_streams, 1)
    grad_proj, *up_came = lax.optimization_barrier((grad_proj, *up_came))
    up_sent, up_kept = reduce_add(up_came, up_kept)
    grad_proj, *up_sent = lax.optimization_barrier((grad_proj, *up_sent))
    caption_grad, sums, input_low = input_backward(
        grad_proj, grad_after, flat, text_vec, grad_gain, grad_bup, w_qkv
    )
    up_came = reduce_swaps(up_sent, up_streams, 2)
    input_low, *up_came = lax.optimization_barrier((input_low, *up_came))
    up_sent, up_kept = reduce_join(up_came, up_kept)
    input_low, *up_sent = lax.optimization_barrier((input_low, *up_sent))
    up_came = [swap(piece, "dp", 4 * (k + 1)) for k, piece in enumerate(up_sent)]
    rest_own, rest_other = proj_backward(
        place, mine_one, grad_proj, grad_after, mixed, input_low, sums
    )
    rest_other, *up_came = lax.optimization_barrier((rest_other, *up_came))
    up_chunk = reduce_last(up_came, up_kept)
    rest_streams = streams_of(D)
    arrived = swap(rest_other, "rep", 1)
    up_column = spread_first(up_chunk)
    rest_sent, rest_kept = reduce_first(rest_own, arrived, rest_streams)
    half = D // 2
    own_columns = lax.dynamic_slice_in_dim(branch_all, mine * half, half, 1)
    if whole:
        grad_w_down = dot_tn(early_all[:, EARLY:], own_columns)
    else:
        other_columns = lax.dynamic_slice_in_dim(branch_all, (1 - mine) * half, half, 1)
        grad_w_down = dot_tn(early[:, EARLY:], own_columns) + swap(
            dot_tn(early[:, EARLY:], other_columns).astype(bf16), "rep", 1
        ).astype(f32)
        grad_w_down = lax.psum(grad_w_down, "dp")
    rest_came = reduce_swaps(rest_sent, rest_streams, 1)
    up_mine = spread_second(up_column, up_streams)
    grad_w_down, *rest_came = lax.optimization_barrier((grad_w_down, *rest_came))
    rest_sent, rest_kept = reduce_add(rest_came, rest_kept)
    up_near = [swap(piece, "dp", two) for piece, (_, _, two) in zip(up_mine, up_streams)]
    rest_sent, rest_kept = reduce_join(reduce_swaps(rest_sent, rest_streams, 2), rest_kept)
    rest_came = [swap(piece, "dp", 4 * (k + 1)) for k, piece in enumerate(rest_sent)]
    rest_chunk = reduce_last(rest_came, rest_kept)
    rest_column = spread_first(rest_chunk)
    up_parts = spread_third(up_mine, up_near, up_streams)
    rest_mine = spread_second(rest_column, rest_streams)
    rest_near = [swap(piece, "dp", two) for piece, (_, _, two) in zip(rest_mine, rest_streams)]
    rest_parts = spread_third(rest_mine, rest_near, rest_streams)
    grad_w_up, grad_w_qkv, grad_w_out, *small = unpack(place, up_parts, rest_parts)
    return (
        pair_loss,
        caption_grad.reshape(local_pairs, CAP, D),
        small[0],
        grad_w_qkv,
        small[1],
        grad_w_out,
        small[2],
        grad_w_up,
        small[3],
        grad_w_down,
    )


def solution(mesh):
    in_specs = (
        P(("dp", "rep"), None, None),
        P(("dp", "rep")),
        P(("dp", "rep"), None, None),
        P(("dp", "rep")),
        P("rep"),
        P("rep", None),
        P("rep"),
        P("rep", None),
        P("rep"),
        P("rep", None),
        P("rep"),
        P("rep", None),
        P(),
        P(),
        P(),
        P(),
        P(),
        P(),
        P(),
        P(),
        P(),
    )
    out_specs = (
        P(("dp", "rep")),
        P(("dp", "rep"), None, None),
        P("rep"),
        P(None, "rep"),
        P("rep"),
        P(None, "rep"),
        P("rep"),
        P(None, "rep"),
        P("rep"),
        P(None, "rep"),
    )
    return jax.shard_map(local, mesh=mesh, in_specs=in_specs, out_specs=out_specs, check_vma=False)
```

```python
import functools
import math

import jax
import jax.numpy as jnp
from jax import lax
from jax.experimental import pallas as pl
from jax.experimental.pallas import tpu as pltpu
from jax.sharding import PartitionSpec as P

D = 768
HEADS = 12
FF = 3072
ILEN = 145
LOWLEN = 50
CAP = 16

SCALE = 100.0
EPS = 1e-06
NEGATIVE = -1e30
LOG2E = math.log2(math.e)
MOST_PAIRS = 2048

UNIT = 160
UNITS = 2
PART = 48
SPAN = 29
QB = 128
BW = 3 * D // 2 + D // 2 + 128
EARLY = D + 128
CHUNKS = 16

f32 = jnp.float32
bf16 = jnp.bfloat16


def dot(left_side, right_side):
    return jnp.dot(left_side, right_side, preferred_element_type=f32)


def dot_nt(left_side, right_side):
    return lax.dot_general(
        left_side, right_side, (((1,), (1,)), ((), ())), preferred_element_type=f32
    )


def dot_tn(left_side, right_side):
    return lax.dot_general(
        left_side, right_side, (((0,), (0,)), ((), ())), preferred_element_type=f32
    )


def normalize(values):
    center = values - jnp.mean(values, -1, keepdims=True)
    inverse = lax.rsqrt(jnp.mean(center * center, -1, keepdims=True) + EPS)
    return center * inverse, inverse


def norm_back(grad, normed, inverse):
    return inverse * (
        grad
        - jnp.mean(grad, -1, keepdims=True)
        - normed * jnp.mean(grad * normed, -1, keepdims=True)
    )


def normal_cdf(values):
    return 0.5 + 0.5 * lax.erf(values * (1.0 / math.sqrt(2.0)))


def split_low(values):
    big = values.astype(bf16)
    return big, (values - big.astype(f32)).astype(bf16)


def tower_kernel(
    groups_ref,
    mine_ref,
    x_hbm,
    vec_own_ref,
    vec_other_ref,
    qkv_own,
    qkv_other,
    out_own,
    out_other,
    up_own,
    up_other,
    down_own,
    down_other,
    emb_ref,
    order,
    x_ref,
    x_wide,
    wqkv,
    wout,
    wup,
    wdown,
    gain_a,
    bqkv,
    gain_m,
    bup,
    xs,
    qkv,
    mixed,
    asum,
    hsum,
    aparts,
    hparts,
    scores,
    attention,
    sems,
):
    total = x_ref.shape[1]
    pitch = total + 8
    mine = mine_ref[0]
    copies = []
    for k in range(ILEN // SPAN):
        span = pl.ds(k * SPAN, SPAN)
        copies.append(pltpu.make_async_copy(x_hbm.at[span], x_ref.at[span], sems.at[8 + k]))
    for k, (own, other, whole) in enumerate(
        (
            (qkv_own, qkv_other, wqkv),
            (out_own, out_other, wout),
            (up_own, up_other, wup),
            (down_own, down_other, wdown),
        )
    ):
        half = own.shape[0]
        copies.append(
            pltpu.make_async_copy(own, whole.at[pl.ds(mine * half, half)], sems.at[2 * k])
        )
        copies.append(
            pltpu.make_async_copy(
                other, whole.at[pl.ds((1 - mine) * half, half)], sems.at[2 * k + 1]
            )
        )
    for copy in copies:
        copy.start()

    vec_own = vec_own_ref[...].astype(f32)
    vec_other = vec_other_ref[...].astype(f32)
    low = jnp.where(mine == 0, vec_own, vec_other)
    high = jnp.where(mine == 0, vec_other, vec_own)
    start = 0
    for dest, size, at in (
        (gain_a, D // 2, (0, D // 2)),
        (bqkv, D, (0, 2 * D)),
        (gain_m, D // 2, (0, D // 2)),
        (bup, FF // 2, (0, FF // 2)),
    ):
        dest[:, at[0] : at[0] + size] = low[:, start : start + size]
        dest[:, at[1] : at[1] + size] = high[:, start : start + size]
        start += size
    bqkv[:, D : 2 * D] = jnp.zeros((1, D), f32)

    def count(i, found):
        return found + groups_ref[i]

    n_hi = lax.fori_loop(0, total, count, 0)

    def place_one(i, state):
        hi, lo = state
        group = groups_ref[i]
        order[jnp.where(group == 1, hi, lo)] = i
        return hi + group, lo + 1 - group

    lax.fori_loop(0, total, place_one, (0, n_hi))
    n_units = n_hi + (total - n_hi + 2) // 3

    xs[...] = jnp.zeros_like(xs)
    first = lax.broadcasted_iota(jnp.int32, (1, 128), 1) < 64
    key_at = lax.broadcasted_iota(jnp.int32, (UNIT, UNIT), 1)
    row_at = lax.broadcasted_iota(jnp.int32, (UNIT, UNIT), 0)
    sub = lax.broadcasted_iota(jnp.int32, (8, 1), 0)

    def place(unit, k):
        last = jnp.minimum(unit, n_units - 1)
        is_hi = last < n_hi
        where = jnp.where(is_hi, last, n_hi + 3 * (last - n_hi) + k)
        return order[jnp.minimum(where, total - 1)], is_hi

    def keep_parts(values, j, dest, col, width):
        rows = values.reshape(UNIT // 8, 8, width)
        parts = [
            jnp.sum(rows[0:6], 0),
            rows[6],
            jnp.sum(rows[7:12], 0),
            rows[12],
            jnp.sum(rows[13:18], 0),
            rows[18],
        ]
        for k, part in enumerate(parts):
            dest[j * PART + k * 8 : j * PART + k * 8 + 8, col : col + width] = part

    loads = copies[: ILEN // SPAN]
    copies = copies[ILEN // SPAN :]

    def widen(t, carry):
        for panel in range(D // 128):
            x_wide[panel, pl.ds(pl.multiple_of(t * pitch, 8), total), :] = x_ref[
                t, :, panel * 128 : (panel + 1) * 128
            ].astype(f32)
        return carry

    for k, load in enumerate(loads):
        load.wait()
        lax.fori_loop(k * SPAN, (k + 1) * SPAN, widen, 0)
    for copy in copies[:2]:
        copy.wait()

    def body(step, carry):
        for j in range(UNITS):
            unit = step * UNITS + j
            one, is_hi = place(unit, 0)
            two, three = place(unit, 1)[0], place(unit, 2)[0]
            base = j * UNIT

            @pl.when(is_hi)
            def _():
                for panel in range(D // 128):
                    xs[base : base + ILEN, panel * 128 : (panel + 1) * 128] = x_wide[
                        panel, pl.ds(one, ILEN, stride=pitch), :
                    ]

            @pl.when(jnp.logical_not(is_hi))
            def _():
                for k, index in enumerate((one, two, three)):
                    for panel in range(D // 128):
                        xs[
                            base + LOWLEN * k : base + LOWLEN * (k + 1),
                            panel * 128 : (panel + 1) * 128,
                        ] = x_wide[panel, pl.ds(index, LOWLEN, stride=pitch), :]

        low_rows = (normalize(xs[...])[0] * gain_a[...]).astype(bf16)
        for col in range(0, 3 * D, 256):
            values = dot(low_rows, wqkv[:, col : col + 256]) + bqkv[:, col : col + 256]
            if col < D:
                values = values * (LOG2E / 8.0)
            qkv[:, col : col + 256] = values.astype(bf16)

        @pl.when(step == 0)
        def _():
            for copy in copies[2:6]:
                copy.wait()

        for j in range(UNITS):
            is_hi = place(step * UNITS + j, 0)[1]
            base = j * UNIT
            key_seg = jnp.where(key_at < LOWLEN, 0, jnp.where(key_at < 2 * LOWLEN, 1, 2))
            row_seg = jnp.where(row_at < LOWLEN, 0, jnp.where(row_at < 2 * LOWLEN, 1, 2))
            short_ok = jnp.logical_and(key_seg == row_seg, key_at < 3 * LOWLEN)
            allowed = jnp.where(
                is_hi, (key_at < ILEN).astype(jnp.int32), short_ok.astype(jnp.int32)
            )
            bias = jnp.where(allowed > 0, 0.0, NEGATIVE)
            for p in range(HEADS // 2):
                query = qkv[base : base + UNIT, p * 128 : (p + 1) * 128]
                key = qkv[base : base + UNIT, D + p * 128 : D + (p + 1) * 128]
                for h in range(2):
                    head = first if h == 0 else jnp.logical_not(first)
                    at = (j * HEADS + 2 * p + h) * UNIT
                    scores[at : at + UNIT, :] = (
                        dot_nt(jnp.where(head, query, jnp.zeros_like(query)), key) + bias
                    )
        for j in range(UNITS):
            part = slice(j * HEADS * UNIT, (j + 1) * HEADS * UNIT)
            values = scores[part, :]
            powers = jnp.exp2(values - jnp.max(values, 1, keepdims=True))
            attention[part, :] = powers.astype(bf16)
        for j in range(UNITS):
            base = j * UNIT
            for p in range(HEADS // 2):
                lanes = slice(p * 128, (p + 1) * 128)
                value = qkv[base : base + UNIT, 2 * D + p * 128 : 2 * D + (p + 1) * 128]
                outs = []
                at = (j * HEADS + 2 * p) * UNIT
                value_one = jnp.concatenate([value, jnp.ones_like(value)], 1)
                for h in range(2):
                    summed = dot(attention[at + h * UNIT : at + (h + 1) * UNIT, :], value_one)
                    outs.append(summed[:, :128] / summed[:, 128:])
                mixed[base : base + UNIT, lanes] = jnp.where(first, outs[0], outs[1]).astype(bf16)
        for col in range(0, D, 256):
            xs[:, col : col + 256] += dot(mixed[...], wout[:, col : col + 256])
        for j in range(UNITS):
            keep_parts(xs[j * UNIT : (j + 1) * UNIT, :], j, aparts, 0, D)
        low_two = (normalize(xs[...])[0] * gain_m[...]).astype(bf16)
        width = 1024
        for col in range(0, FF, width):
            pre_act = dot(low_two, wup[:, col : col + width]) + bup[:, col : col + width]
            hidden = pre_act * normal_cdf(pre_act)
            for j in range(UNITS):
                keep_parts(hidden[j * UNIT : (j + 1) * UNIT], j, hparts, col, width)
        for j in range(UNITS):
            unit = step * UNITS + j
            one, is_hi = place(unit, 0)
            two, three = place(unit, 1)[0], place(unit, 2)[0]

            def rows_of(index):
                return pl.ds(pl.multiple_of(index * 8, 8), 8)

            @pl.when(is_hi)
            def _():
                for src, dest in ((aparts, asum), (hparts, hsum)):
                    part = [src[j * PART + k * 8 : j * PART + k * 8 + 8, :] for k in range(6)]
                    dest[rows_of(one), :] = (
                        (part[0] + part[1])
                        + (part[2] + part[3])
                        + (part[4] + jnp.where(sub < 1, part[5], 0.0))
                    )

            @pl.when(jnp.logical_not(is_hi))
            def _():
                for src, dest in ((aparts, asum), (hparts, hsum)):
                    part = [src[j * PART + k * 8 : j * PART + k * 8 + 8, :] for k in range(6)]
                    dest[rows_of(three), :] = (
                        jnp.where(sub < 4, 0.0, part[3])
                        + part[4]
                        + jnp.where(sub < 6, part[5], 0.0)
                    )
                    dest[rows_of(two), :] = (
                        jnp.where(sub < 2, 0.0, part[1])
                        + part[2]
                        + jnp.where(sub < 4, part[3], 0.0)
                    )
                    dest[rows_of(one), :] = part[0] + jnp.where(sub < 2, part[1], 0.0)

        return carry

    lax.fori_loop(0, (n_units + UNITS - 1) // UNITS, body, 0)
    for copy in copies[6:]:
        copy.wait()
    which = lax.broadcasted_iota(jnp.int32, (total, 128), 0)
    scale = jnp.zeros((total, 128), f32)
    for i in range(total):
        scale = jnp.where(
            which == i, jnp.where(groups_ref[i] == 1, 1.0 / ILEN, 1.0 / LOWLEN), scale
        )
    scale = scale[:, 0:1]
    big, rest = split_low(jnp.sum(hsum[...].reshape(total, 8, FF), 1) * scale)
    product = dot(jnp.concatenate([big, rest], 0), wdown[...])
    pooled = jnp.sum(asum[...].reshape(total, 8, D), 1) * scale + product[:total] + product[total:]
    emb_ref[...] = (
        pooled * lax.rsqrt(jnp.sum(pooled * pooled, -1, keepdims=True) + EPS)
    ).astype(bf16)


VM = pl.BlockSpec(memory_space=pltpu.VMEM)
SM = pl.BlockSpec(memory_space=pltpu.SMEM)
ANY = pl.BlockSpec(memory_space=pltpu.HBM)


def limit(mebibytes):
    return pltpu.CompilerParams(vmem_limit_bytes=mebibytes * 1024 * 1024)


def image_tower(images, groups, mine, vec_own, vec_other, weights):
    number = images.shape[1]
    rows = UNITS * UNIT
    flops = number * 100 * 2 * (4 * D * D + D * FF)
    return pl.pallas_call(
        tower_kernel,
        out_shape=jax.ShapeDtypeStruct((number, D), bf16),
        in_specs=[SM, SM, ANY, VM, VM] + [ANY] * 8,
        out_specs=VM,
        scratch_shapes=[
            pltpu.SMEM((number,), jnp.int32),
            pltpu.VMEM(images.shape, bf16),
            pltpu.VMEM((D // 128, ILEN * (number + 8), 128), f32),
            pltpu.VMEM((D, 3 * D), bf16),
            pltpu.VMEM((D, D), bf16),
            pltpu.VMEM((D, FF), bf16),
            pltpu.VMEM((FF, D), bf16),
            pltpu.VMEM((1, D), f32),
            pltpu.VMEM((1, 3 * D), f32),
            pltpu.VMEM((1, D), f32),
            pltpu.VMEM((1, FF), f32),
            pltpu.VMEM((rows, D), f32),
            pltpu.VMEM((rows, 3 * D), bf16),
            pltpu.VMEM((rows, D), bf16),
            pltpu.VMEM((number * 8, D), f32),
            pltpu.VMEM((number * 8, FF), f32),
            pltpu.VMEM((UNITS * PART, D), f32),
            pltpu.VMEM((UNITS * PART, FF), f32),
            pltpu.VMEM((UNITS * HEADS * UNIT, UNIT), f32),
            pltpu.VMEM((UNITS * HEADS * UNIT, UNIT), bf16),
            pltpu.SemaphoreType.DMA((8 + ILEN // SPAN,)),
        ],
        compiler_params=limit(62),
        cost_estimate=pl.CostEstimate(
            flops=flops, bytes_accessed=24 * 1024 * 1024, transcendentals=0
        ),
        name="image_tower",
    )(groups, mine, images, vec_own, vec_other, *weights)


def lens_along(lens_ref, start, number):
    owner = lax.broadcasted_iota(jnp.int32, (1, number * CAP), 1) // CAP
    lens = jnp.zeros((1, number * CAP), jnp.int32)
    for c in range(number):
        lens = jnp.where(owner == c, lens_ref[start + c], lens)
    return lens


def score_bias(lens_ref, block):
    per = QB // CAP
    position = lax.broadcasted_iota(jnp.int32, (1, QB), 1) % CAP
    valid = position < lens_along(lens_ref, block * per, per)
    rows = lax.broadcasted_iota(jnp.int32, (QB, QB), 0) // CAP
    columns = lax.broadcasted_iota(jnp.int32, (QB, QB), 1) // CAP
    return jnp.where(jnp.logical_and(rows == columns, valid), 0.0, NEGATIVE)


def forward_kernel(
    lens_ref,
    x_ref,
    vec_ref,
    wqkv_ref,
    wout_ref,
    wup_ref,
    wdown_ref,
    qkv,
    mixed,
    after,
    mlp,
    slope,
    attention,
    early,
    hidden,
    scores,
):
    rows = x_ref.shape[0]
    number = rows // CAP
    first = lax.broadcasted_iota(jnp.int32, (1, 128), 1) < 64
    normed, _ = normalize(x_ref[...].astype(f32))
    low = (normed * vec_ref[:, 0:D]).astype(bf16)
    for col in range(0, 3 * D, 256):
        values = dot(low, wqkv_ref[:, col : col + 256])
        if col < D:
            values = values + vec_ref[:, D + col : D + col + 256]
        if col >= 2 * D:
            values = values + vec_ref[:, col : col + 256]
        values = values.astype(bf16)
        if col < D:
            values = values * jnp.asarray(0.125, bf16)
        qkv[:, col : col + 256] = values
    for block in range(rows // QB):
        bias = score_bias(lens_ref, block)
        span = slice(block * QB, (block + 1) * QB)
        for p in range(HEADS // 2):
            query = qkv[span, p * 128 : (p + 1) * 128]
            key = qkv[span, D + p * 128 : D + (p + 1) * 128]
            for h in range(2):
                head = first if h == 0 else jnp.logical_not(first)
                at = (block * HEADS + 2 * p + h) * QB
                scores[at : at + QB, :] = (
                    dot_nt(jnp.where(head, query, jnp.zeros_like(query)), key) * LOG2E + bias
                )
    for block in range(rows // QB):
        part = slice(block * HEADS * QB, (block + 1) * HEADS * QB)
        values = scores[part, :]
        powers = jnp.exp2(values - jnp.max(values, 1, keepdims=True))
        attention[part, :] = (powers * (1.0 / jnp.sum(powers, 1, keepdims=True))).astype(bf16)
    for block in range(rows // QB):
        span = slice(block * QB, (block + 1) * QB)
        for p in range(HEADS // 2):
            value = qkv[span, 2 * D + p * 128 : 2 * D + (p + 1) * 128]
            at = (block * HEADS + 2 * p) * QB
            outs = [dot(attention[at + h * QB : at + (h + 1) * QB, :], value) for h in range(2)]
            mixed[span, p * 128 : (p + 1) * 128] = jnp.where(first, outs[0], outs[1]).astype(bf16)
    for col in range(0, D, 256):
        after[:, col : col + 256] = x_ref[:, col : col + 256].astype(f32) + dot(
            mixed[...], wout_ref[:, col : col + 256]
        )
    mlp[...] = (normalize(after[...])[0] * vec_ref[:, 3 * D : 4 * D]).astype(bf16)
    lens = lens_along(lens_ref, 0, number)
    position = lax.broadcasted_iota(jnp.int32, (1, rows), 1)
    owner = (
        lax.broadcasted_iota(jnp.int32, (number, rows), 0)
        == lax.broadcasted_iota(jnp.int32, (number, rows), 1) // CAP
    )
    members = jnp.where(jnp.logical_and(owner, position % CAP < lens), 1.0, 0.0)
    pool = members.astype(bf16)
    count = jnp.sum(members, 1, keepdims=True)
    width = 512
    for col in range(0, FF, width):
        span = slice(col, col + width)
        pre_act = dot(mlp[...], wup_ref[:, span]) + vec_ref[:, 4 * D + col : 4 * D + col + width]
        phi = normal_cdf(pre_act)
        hidden[:, span] = (pre_act * phi).astype(bf16)
        density = jnp.exp2(pre_act * pre_act * (-0.5 * LOG2E)) * (1.0 / math.sqrt(2.0 * math.pi))
        slope[:, span] = (phi + pre_act * density).astype(bf16)
    big, rest = split_low(dot(pool, hidden[...]))
    after_big, after_rest = split_low(after[...])
    pooled = (
        dot(pool, after_big)
        + dot(pool, after_rest)
        + dot(big, wdown_ref[...])
        + dot(rest, wdown_ref[...])
    )
    early[:, 0:D] = (pooled / count).astype(bf16)
    early[:, D:EARLY] = jnp.broadcast_to(count, (number, EARLY - D)).astype(bf16)
    early[:, EARLY:] = big


def text_forward(captions, lens, vec, w_qkv, w_out, w_up, w_down):
    rows = captions.shape[0]
    shape = jax.ShapeDtypeStruct
    return pl.pallas_call(
        forward_kernel,
        out_shape=[
            shape((rows, 3 * D), bf16),
            shape((rows, D), bf16),
            shape((rows, D), f32),
            shape((rows, D), bf16),
            shape((rows, FF), bf16),
            shape((rows * HEADS, QB), bf16),
            shape((rows // CAP, EARLY + FF), bf16),
        ],
        in_specs=[SM] + [VM] * 6,
        out_specs=[VM] * 7,
        scratch_shapes=[pltpu.VMEM((rows, FF), bf16), pltpu.VMEM((rows * HEADS, QB), f32)],
        compiler_params=limit(60),
        cost_estimate=pl.CostEstimate(
            flops=2 * rows * (4 * D * D + 2 * D * FF),
            bytes_accessed=24 * 1024 * 1024,
            transcendentals=0,
        ),
        name="text_forward",
    )(lens, captions, vec, w_qkv, w_out, w_up, w_down)


def put_chunks(dest, values, place_ref, stream, col):
    rows = values.shape[0] // CHUNKS
    for chunk in range(CHUNKS):
        at = pl.multiple_of(place_ref[stream, chunk] * rows, 16)
        dest[pl.ds(at, rows), col : col + values.shape[1]] = values[
            chunk * rows : (chunk + 1) * rows
        ].astype(dest.dtype)


def up_kernel(
    place_ref, mine_ref, lens_ref, branch_ref, slope_ref, mlp_ref, wdown_ref,
    grad_pre, own, other, grad_bup, grad_hidden, mlp_t,
):
    number = slope_ref.shape[0] // CAP
    half = FF // 2
    mine = mine_ref[0]
    for col in range(0, FF, 512):
        grad_hidden[:, col : col + 512] = dot_nt(branch_ref[...], wdown_ref[col : col + 512, :])
    position = lax.broadcasted_iota(jnp.int32, (CAP, 1), 0)
    for c in range(number):
        span = slice(c * CAP, (c + 1) * CAP)
        keep = jnp.where(position < lens_ref[c], 1.0, 0.0)
        grad_pre[span, :] = (
            grad_hidden[c : c + 1, :] * slope_ref[span, :].astype(f32) * keep
        ).astype(bf16)
    mlp_t[...] = mlp_ref[...].T
    for which, dest in ((1 - mine, other), (mine, own)):
        for col in range(0, half, 384):
            lanes = pl.ds(pl.multiple_of(which * half + col, 128), 384)
            put_chunks(dest, dot(mlp_t[...], grad_pre[:, lanes]), place_ref, 2 * col // half, col)
    for col in range(0, FF, 512):
        grad_bup[:, col : col + 512] = jnp.sum(
            grad_pre[:, col : col + 512].astype(f32), 0, keepdims=True
        )


def up_backward(place, mine, lens, branch, slope, mlp, w_down):
    rows = slope.shape[0]
    shape = jax.ShapeDtypeStruct
    return pl.pallas_call(
        up_kernel,
        out_shape=[
            shape((rows, FF), bf16),
            shape((D, FF // 2), f32),
            shape((D, FF // 2), bf16),
            shape((1, FF), f32),
        ],
        in_specs=[SM, SM, SM] + [VM] * 4,
        out_specs=[VM] * 4,
        scratch_shapes=[pltpu.VMEM((rows // CAP, FF), f32), pltpu.VMEM((D, rows), bf16)],
        compiler_params=limit(32),
        cost_estimate=pl.CostEstimate(
            flops=2 * rows * D * FF, bytes_accessed=20 * 1024 * 1024, transcendentals=0
        ),
        name="up_backward",
    )(place, mine, lens, branch, slope, mlp, w_down)


def mlp_kernel(
    lens_ref, pre_ref, grad_ref, after_ref, vec_ref, wup_ref, wout_ref,
    grad_after, grad_mixed, grad_gain, grad_out,
):
    number = after_ref.shape[0] // CAP
    grad_mlp = dot_nt(pre_ref[...], wup_ref[...])
    normed_two, inverse_two = normalize(after_ref[...])
    grad_gain[...] = jnp.sum(grad_mlp * normed_two, 0, keepdims=True)
    grad_after[...] = norm_back(grad_mlp * vec_ref[:, 3 * D : 4 * D], normed_two, inverse_two)
    position = lax.broadcasted_iota(jnp.int32, (CAP, 1), 0)
    for c in range(number):
        keep = jnp.where(position < lens_ref[c], 1.0, 0.0)
        grad_after[c * CAP : (c + 1) * CAP, :] += grad_ref[c : c + 1, :] * keep
    grad_out[...] = grad_after[...].astype(bf16)
    for col in range(0, D, 256):
        grad_mixed[:, col : col + 256] = dot_nt(
            grad_out[...], wout_ref[col : col + 256, :]
        ).astype(bf16)


def mlp_backward(lens, grad_pre, grads, after, vec, w_up, w_out):
    rows = after.shape[0]
    shape = jax.ShapeDtypeStruct
    return pl.pallas_call(
        mlp_kernel,
        out_shape=[shape((rows, D), f32), shape((rows, D), bf16), shape((1, D), f32)],
        in_specs=[SM] + [VM] * 6,
        out_specs=[VM] * 3,
        scratch_shapes=[pltpu.VMEM((rows, D), bf16)],
        compiler_params=limit(36),
        cost_estimate=pl.CostEstimate(
            flops=2 * rows * (D * D + D * FF), bytes_accessed=20 * 1024 * 1024, transcendentals=0
        ),
        name="mlp_backward",
    )(lens, grad_pre, grads, after, vec, w_up, w_out)


def attention_kernel(
    qkv_ref, att_ref, mixed_ref, grad_ref, grad_proj, grad_att, means, grad_s, *, start
):
    first = lax.broadcasted_iota(jnp.int32, (1, 128), 1) < 64
    ones = jnp.ones((128, QB), bf16)
    heads = (first, jnp.logical_not(first))
    blocks = grad_proj.shape[0] // QB
    for block in range(blocks):
        span = slice(start + block * QB, start + (block + 1) * QB)
        for p in range(HEADS // 2):
            at = p * 128
            value = qkv_ref[span, 2 * D + at : 2 * D + at + 128]
            grad = grad_ref[span, at : at + 128]
            product = (grad.astype(f32) * mixed_ref[span, at : at + 128].astype(f32)).astype(bf16)
            for h, head in enumerate(heads):
                to = (block * HEADS + 2 * p + h) * QB
                grad_att[to : to + QB, :] = dot_nt(
                    jnp.where(head, grad, jnp.zeros_like(grad)), value
                )
                means[to : to + QB, :] = dot(
                    jnp.where(head, product, jnp.zeros_like(product)), ones
                )
    for block in range(blocks):
        part = slice(block * HEADS * QB, (block + 1) * HEADS * QB)
        place = (start // QB + block) * HEADS * QB
        low = att_ref[place : place + HEADS * QB, :].astype(f32)
        grad_s[part, :] = (low * (grad_att[part, :] - means[part, :])).astype(bf16)
    for block in range(blocks):
        span = slice(start + block * QB, start + (block + 1) * QB)
        dest = slice(block * QB, (block + 1) * QB)
        for p in range(HEADS // 2):
            at = p * 128
            query = qkv_ref[span, at : at + 128]
            key = qkv_ref[span, D + at : D + at + 128]
            grad = grad_ref[span, at : at + 128]
            grad_q, grad_k, grad_v = [], [], []
            for h in range(2):
                to = (block * HEADS + 2 * p + h) * QB
                place = ((start // QB + block) * HEADS + 2 * p + h) * QB
                sgrad = grad_s[to : to + QB, :]
                grad_q.append(dot(sgrad, key))
                grad_k.append(dot_tn(sgrad, query))
                grad_v.append(dot_tn(att_ref[place : place + QB, :], grad))
            for k, (parts, scale) in enumerate(((grad_q, 0.125), (grad_k, 1.0), (grad_v, 1.0))):
                grad_proj[dest, k * D + at : k * D + at + 128] = (
                    jnp.where(first, parts[0], parts[1]) * scale
                ).astype(bf16)


def input_kernel(
    proj_ref, after_ref, x_ref, vec_ref, gain_ref, bup_ref, wqkv_ref, caption_grad, sums, input_low
):
    gain_a = vec_ref[:, 0:D]
    normed_one, inverse_one = normalize(x_ref[...].astype(f32))
    input_low[...] = (normed_one * gain_a).astype(bf16)
    grad_in = dot_nt(proj_ref[...], wqkv_ref[...])
    sums[:, 0:D] = jnp.sum(grad_in * normed_one, 0, keepdims=True)
    sums[:, D : 2 * D] = jnp.sum(proj_ref[:, 0:D].astype(f32), 0, keepdims=True)
    sums[:, 2 * D : 3 * D] = jnp.sum(proj_ref[:, 2 * D :].astype(f32), 0, keepdims=True)
    sums[:, 3 * D : 4 * D] = gain_ref[...]
    sums[:, 4 * D :] = bup_ref[...]
    caption_grad[...] = after_ref[...] + norm_back(grad_in * gain_a, normed_one, inverse_one)


def proj_kernel(
    place_ref, mine_ref, proj_ref, after_ref, mixed_ref, input_ref, sums, own, other, lhs_t, grad_out
):
    chunk_rows = D // CHUNKS
    mine = mine_ref[0]
    lhs_t[...] = input_ref[...].T
    half_out, half_qkv = D // 2, 3 * D // 2
    for which, dest in ((1 - mine, other), (mine, own)):
        for col in range(0, half_qkv, 384):
            lanes = pl.ds(pl.multiple_of(which * half_qkv + col, 128), 384)
            put_chunks(dest, dot(lhs_t[...], proj_ref[:, lanes]), place_ref, col // 768, col)
    lhs_t[...] = mixed_ref[...].T
    grad_out[...] = after_ref[...].astype(bf16)
    for which, dest in ((1 - mine, other), (mine, own)):
        lanes = pl.ds(pl.multiple_of(which * half_out, 128), half_out)
        put_chunks(dest, dot(lhs_t[...], grad_out[:, lanes]), place_ref, 1, half_qkv)
    for which, dest in ((1 - mine, other), (mine, own)):
        dest[:, BW - 128 :] = jnp.zeros((D, 128), dest.dtype)
        pieces = []
        for start, size in ((0, D), (D, 2 * D), (3 * D, D), (4 * D, FF)):
            for k in range(0, size // 2, 128):
                at = pl.multiple_of(start + which * (size // 2) + k, 128)
                pieces.append(sums[:, pl.ds(at, 128)])
        pieces += [jnp.zeros_like(pieces[0])] * (32 - len(pieces))
        at = pl.multiple_of(place_ref[1, 0] * chunk_rows, 16)
        dest[pl.ds(at, 32), BW - 128 :] = jnp.concatenate(pieces, 0).astype(dest.dtype)


def rest_kernel(
    place_ref, mine_ref, qkv_ref, att_ref, mixed_ref, grad_ref, after_ref, x_ref, vec_ref,
    gain_ref, bup_ref, wqkv_ref, caption_grad, own, other,
    grad_proj, sums, input_low, grad_att, means, grad_s, lhs_t, grad_out,
):
    attention_kernel(
        qkv_ref, att_ref, mixed_ref, grad_ref, grad_proj, grad_att, means, grad_s, start=0
    )
    input_kernel(
        grad_proj, after_ref, x_ref, vec_ref, gain_ref, bup_ref, wqkv_ref,
        caption_grad, sums, input_low,
    )
    proj_kernel(
        place_ref, mine_ref, grad_proj, after_ref, mixed_ref, input_low, sums,
        own, other, lhs_t, grad_out,
    )


def rest_backward(
    place, mine, qkv, attention, mixed, grad_mixed, grad_after, captions, vec, grad_gain, grad_bup, w_qkv
):
    rows = captions.shape[0]
    shape = jax.ShapeDtypeStruct
    return pl.pallas_call(
        rest_kernel,
        out_shape=[shape((rows, D), f32), shape((D, BW), f32), shape((D, BW), bf16)],
        in_specs=[SM, SM] + [VM] * 10,
        out_specs=[VM] * 3,
        scratch_shapes=[
            pltpu.VMEM((rows, 3 * D), bf16),
            pltpu.VMEM((1, 4 * D + FF), f32),
            pltpu.VMEM((rows, D), bf16),
            pltpu.VMEM((rows * HEADS, QB), f32),
            pltpu.VMEM((rows * HEADS, QB), f32),
            pltpu.VMEM((rows * HEADS, QB), bf16),
            pltpu.VMEM((D, rows), bf16),
            pltpu.VMEM((rows, D), bf16),
        ],
        compiler_params=limit(48),
        cost_estimate=pl.CostEstimate(
            flops=2 * rows * 48 * D * D, bytes_accessed=60 * 1024 * 1024, transcendentals=0
        ),
        name="rest_backward",
    )(
        place, mine, qkv, attention, mixed, grad_mixed, grad_after, captions, vec,
        grad_gain, grad_bup, w_qkv,
    )


def dp_bits():
    bits, bit = [], 1
    while bit < lax.axis_size("dp"):
        bits.append(bit)
        bit *= 2
    return bits


def swap(values, axis, bit):
    size = lax.axis_size(axis)
    return lax.ppermute(values, axis, [(place, place ^ bit) for place in range(size)])


def gather_relative(values):
    bits = dp_bits()
    while bits:
        pair = bits[-2:]
        bits = bits[:-2]
        offsets = [0]
        for bit in pair:
            offsets += [entry + bit for entry in offsets]
        values = jnp.concatenate([swap(values, "dp", k) if k else values for k in offsets], 0)
    return jnp.concatenate([values, swap(values, "rep", 1)], 0)


def relative_chips():
    bits, table = dp_bits(), [0]
    while bits:
        pair = bits[-2:]
        bits = bits[:-2]
        offsets = [0]
        for bit in pair:
            offsets += [entry + bit for entry in offsets]
        table = [entry ^ k for k in offsets for entry in table]
    return table


def chunk_places():
    away = jnp.arange(CHUNKS, dtype=jnp.int32) ^ (lax.axis_index("dp") % CHUNKS)
    one, two, rest = away % 2, away // 2 % 2, away // 4
    return jnp.stack([one * 8 + two * 4 + rest, two * 8 + one * 4 + rest]).astype(jnp.int32)


def streams_of(width):
    return ((slice(0, width), 1, 2), (slice(width, None), 2, 1))


def reduce_first(own, arrived, streams):
    half = own.shape[0] // 2

    def both(rows, lanes):
        return own[rows, lanes] + arrived[rows, lanes].astype(f32)

    sent = [both(slice(half, None), lanes).astype(bf16) for lanes, _, _ in streams]
    return sent, [both(slice(0, half), lanes) for lanes, _, _ in streams]


def reduce_swaps(sent, streams, stage):
    return [swap(piece, "dp", stream[stage]) for piece, stream in zip(sent, streams)]


def reduce_add(came, kept):
    half = kept[0].shape[0] // 2
    totals = [total + got.astype(f32) for total, got in zip(kept, came)]
    return [total[half:].astype(bf16) for total in totals], [total[:half] for total in totals]


def reduce_join(came, kept):
    total = jnp.concatenate([total + got.astype(f32) for total, got in zip(kept, came)], 1)
    rows = total.shape[0] // 4
    return [total[k * rows : (k + 1) * rows].astype(bf16) for k in (1, 2, 3)], total[:rows]


def reduce_last(parts, total):
    total = total + sum(part.astype(f32) for part in parts)
    for bit in dp_bits()[4:]:
        total = total + swap(total.astype(bf16), "dp", bit).astype(f32)
    return total.astype(bf16)


def spread_first(chunk):
    return [swap(chunk, "dp", 4 * k) if k else chunk for k in range(4)]


def spread_second(column, streams):
    return [jnp.concatenate([piece[:, lanes] for piece in column], 0) for lanes, _, _ in streams]


def spread_swaps(pieces, streams, stage):
    return [swap(piece, "dp", stream[stage]) for piece, stream in zip(pieces, streams)]


def reduce_swaps_far(sent):
    return [swap(piece, "dp", 4 * (k + 1)) for k, piece in enumerate(sent)]


def in_quarters(*quarters):
    return [quarter[stream] for stream in range(2) for quarter in quarters]


def behind(values, others):
    return list(lax.optimization_barrier((*values, *others))[: len(values)])


def each_chunk(place_ref):
    rows = D // CHUNKS
    place = place_ref[0, 0]
    me = place // 8 + 2 * (place // 4 % 2) + 4 * (place % 4)
    for stream in range(2):
        for quarter in range(4):
            for k in range(4):
                high, low = quarter // 2, quarter % 2
                away = (high + 2 * low if stream == 0 else low + 2 * high) + 4 * k
                chunk = me ^ away
                at = pl.ds(pl.multiple_of(chunk * rows, 16), rows)
                yield stream, stream * 4 + quarter, slice(k * rows, (k + 1) * rows), chunk, at


def unpack_up_kernel(place_ref, *refs):
    parts, g_up = refs[:8], refs[8]
    for stream, part, span, _, at in each_chunk(place_ref):
        lanes = slice(stream * FF // 4, (stream + 1) * FF // 4)
        g_up[at, lanes] = parts[part][span, :].astype(f32)


def unpack_rest_kernel(place_ref, *refs):
    parts, (g_qkv, g_out), vectors = refs[:8], refs[8:10], refs[10:]
    for stream, part, span, chunk, at in each_chunk(place_ref):
        rest = parts[part][span, :].astype(f32)
        if stream == 0:
            g_qkv[at, 0:D] = rest
            continue
        g_qkv[at, D:] = rest[:, : D // 2]
        g_out[at, :] = rest[:, D // 2 : D]

        @pl.when(chunk == 0)
        def _():
            row = 0
            for dest in vectors:
                for lane in range(0, dest.shape[0], 128):
                    dest[lane : lane + 128] = rest[row, D:]
                    row += 1


def unpack_up(place, parts):
    return pl.pallas_call(
        unpack_up_kernel,
        out_shape=jax.ShapeDtypeStruct((D, FF // 2), f32),
        in_specs=[SM] + [VM] * 8,
        out_specs=VM,
        compiler_params=limit(20),
        name="unpack_up",
    )(place, *parts)


def unpack_rest(place, parts):
    shape = jax.ShapeDtypeStruct
    return pl.pallas_call(
        unpack_rest_kernel,
        out_shape=[
            shape((D, 3 * D // 2), f32),
            shape((D, D // 2), f32),
            shape((D // 2,), f32),
            shape((D,), f32),
            shape((D // 2,), f32),
            shape((FF // 2,), f32),
        ],
        in_specs=[SM] + [VM] * 8,
        out_specs=[VM] * 6,
        compiler_params=limit(20),
        name="unpack_rest",
    )(place, *parts)


def softmax_parts(scores, axis):
    maxima = jnp.max(scores, axis, keepdims=True)
    powers = jnp.exp(scores - maxima)
    totals = jnp.sum(powers, axis, keepdims=True)
    return powers / totals, maxima + jnp.log(totals)


def text_unit(pooled_low, text_proj):
    proj_out = dot(pooled_low, text_proj)
    inverse_z = lax.rsqrt(jnp.sum(proj_out * proj_out, -1, keepdims=True) + EPS)
    return proj_out * inverse_z, inverse_z


def branch_grad(grad_unit, unit_text, inverse_z, text_proj, lengths):
    grad_projout = (
        inverse_z * (grad_unit - unit_text * jnp.sum(unit_text * grad_unit, -1, keepdims=True))
    ).astype(bf16)
    return dot_nt(grad_projout, text_proj) / lengths


def loss_kernel(
    where_ref, early_hbm, image_ref, proj_ref, pair_loss, own_grads, own_branch, branch,
    unit, inverse, scores, sgrad, early_ref, sem,
):
    copy = pltpu.make_async_copy(early_hbm.at[:, pl.ds(0, EARLY)], early_ref, sem)
    copy.start()
    copy.wait()
    total = image_ref.shape[0]
    number = own_grads.shape[0]
    chip, mine = where_ref[0], where_ref[1]
    block = 256
    for row in range(0, total, block):
        span = slice(row, row + block)
        proj_out = dot(early_ref[span, 0:D], proj_ref[...])
        inverse_z = lax.rsqrt(jnp.sum(proj_out * proj_out, -1, keepdims=True) + EPS)
        inverse[span, :] = jnp.broadcast_to(inverse_z, (block, 128))
        unit[span, :] = proj_out * inverse_z
        scores[span, :] = dot_nt(unit[span, :].astype(bf16), image_ref[...]) * SCALE
    place = lax.broadcasted_iota(jnp.int32, (1, total), 1) // number
    chips = total // (2 * number)
    away = place % chips
    other = place // chips
    from_chip = chip ^ (away // 4 + 4 * (away % 4)) if chips == 16 else None
    image_id = (from_chip * 2 + (mine ^ other)) * number + (
        lax.broadcasted_iota(jnp.int32, (1, total), 1) % number
    )
    column_max = jnp.max(scores[...], 0, keepdims=True)
    column_sum = jnp.zeros((1, total), f32)
    for row in range(0, total, block):
        column_sum += jnp.sum(
            jnp.exp(scores[row : row + block, :] - column_max), 0, keepdims=True
        )
    column_total = column_max + jnp.log(column_sum)
    for row in range(0, total, block):
        span = slice(row, row + block)
        values = scores[span, :]
        row_max = jnp.max(values, 1, keepdims=True)
        powers = jnp.exp(values - row_max)
        by_text = powers * (0.5 / jnp.sum(powers, 1, keepdims=True))
        by_image = jnp.exp(values - column_max) * (0.5 / column_sum)
        text_id = lax.broadcasted_iota(jnp.int32, (block, 1), 0) + row
        same = jnp.where(text_id == image_id, 1.0, 0.0)
        sgrad[span, :] = (by_text + by_image - same).astype(bf16)
        grad_unit = dot(sgrad[span, :], image_ref[...]) * SCALE
        unit_text = unit[span, :]
        grad_proj = (
            inverse[span, 0:1]
            * (grad_unit - unit_text * jnp.sum(unit_text * grad_unit, -1, keepdims=True))
        ).astype(bf16)
        unit[span, :] = dot_nt(grad_proj, proj_ref[...]) / early_ref[span, D : D + 1].astype(f32)
        branch[span, :] = unit[span, :].astype(bf16)
    first = pl.multiple_of((chip * 2 + mine) * number, 32)
    own_grads[...] = unit[pl.ds(first, number), :]
    own_branch[...] = unit[pl.ds(first, number), :].astype(bf16)
    values = scores[pl.ds(first, number), :]
    row_max = jnp.max(values, 1, keepdims=True)
    row_total = row_max + jnp.log(jnp.sum(jnp.exp(values - row_max), 1, keepdims=True))
    text_id = lax.broadcasted_iota(jnp.int32, (number, 1), 0) + first
    same = jnp.where(text_id == image_id, 1.0, 0.0)
    both = 0.5 * (row_total + column_total) - values
    pair_loss[...] = jnp.broadcast_to(jnp.sum(both * same, 1, keepdims=True), (number, 128))


def loss_whole(early_all, image_all, text_proj, chip, mine, number):
    total = image_all.shape[0]
    shape = jax.ShapeDtypeStruct
    pair_loss, grads, own_branch, branch = pl.pallas_call(
        loss_kernel,
        out_shape=[
            shape((number, 128), f32),
            shape((number, D), f32),
            shape((number, D), bf16),
            shape((total, D), bf16),
        ],
        in_specs=[SM, ANY, VM, VM],
        out_specs=[VM] * 4,
        scratch_shapes=[
            pltpu.VMEM((total, D), f32),
            pltpu.VMEM((total, 128), f32),
            pltpu.VMEM((total, total), f32),
            pltpu.VMEM((total, total), bf16),
            pltpu.VMEM((total, EARLY), bf16),
            pltpu.SemaphoreType.DMA,
        ],
        compiler_params=limit(50),
        name="pair_loss",
    )(jnp.stack([chip, mine]), early_all, image_all, text_proj)
    return pair_loss[:, 0], grads, own_branch, branch


def loss_rows(pooled_all, image_all, text_proj, lengths_all, image_ids, first_row, local_pairs):
    unit_all, inverse_all = text_unit(pooled_all, text_proj)

    def own_rows(values):
        return lax.dynamic_slice_in_dim(values, first_row, local_pairs, 0)

    unit_text, inverse_z = own_rows(unit_all), own_rows(inverse_all)
    text_scores = dot_nt(unit_text.astype(bf16), image_all) * SCALE
    image_scores = dot_nt(image_all[:local_pairs], unit_all.astype(bf16)) * SCALE
    by_text, text_total = softmax_parts(text_scores, 1)
    image_total = softmax_parts(image_scores, 1)[1]
    every_total = gather_relative(image_total)
    text_ids = first_row + jnp.arange(local_pairs, dtype=jnp.int32)
    own_same = (text_ids[:, None] == image_ids).astype(f32)
    own = jnp.sum(text_scores * own_same, -1)
    pair_loss = 0.5 * (text_total[:, 0] - own) + 0.5 * (image_total[:, 0] - own)
    by_image = jnp.exp(text_scores - every_total[:, 0][None, :])
    sgrad = (0.5 * (by_text - own_same) + 0.5 * (by_image - own_same)).astype(bf16)
    grad_unit = dot(sgrad, image_all) * SCALE
    grads = branch_grad(grad_unit, unit_text, inverse_z, text_proj, own_rows(lengths_all))
    return pair_loss, grads, grads.astype(bf16), grads.astype(bf16)


def local(
    images,
    groups,
    captions,
    cap_lengths,
    img_gain_a,
    img_w_qkv,
    img_b_qv,
    img_w_out,
    img_gain_m,
    img_w_up,
    img_b_up,
    img_w_down,
    gain_attn,
    w_qkv,
    b_qv,
    w_out,
    gain_mlp,
    w_up,
    b_up,
    w_down,
    text_proj,
):
    local_pairs = images.shape[0]
    rows_total = local_pairs * CAP
    mine = lax.axis_index("rep").astype(jnp.int32)
    mine_one = mine[None]
    total_pairs = local_pairs * lax.axis_size("dp") * lax.axis_size("rep")
    whole = total_pairs <= MOST_PAIRS

    image_vec = jnp.concatenate([img_gain_a, img_b_qv, img_gain_m, img_b_up])[None]
    image_vec_other = swap(image_vec, "rep", 1)
    weights = []
    for weight in (img_w_qkv, img_w_out, img_w_up, img_w_down):
        weights += [weight, swap(weight, "rep", 1)]

    text_vec = lax.optimization_barrier(jnp.concatenate([gain_attn, b_qv, gain_mlp, b_up]))
    text_vec = text_vec.astype(f32)[None]
    flat = captions.reshape(rows_total, D)
    qkv, mixed, after, mlp, slope, attention, early = text_forward(
        flat, cap_lengths, text_vec, w_qkv, w_out, w_up, w_down
    )
    early, image_vec_other, *weights = lax.optimization_barrier((early, image_vec_other, *weights))
    early_all = lax.all_gather(
        early if whole else early[:, :EARLY], ("dp", "rep"), axis=0, tiled=True
    )
    image_emb = image_tower(
        jnp.transpose(images, (1, 0, 2)), groups, mine_one, image_vec, image_vec_other, weights
    )
    image_all = gather_relative(image_emb)
    chip = lax.axis_index("dp").astype(jnp.int32)
    if whole:
        pair_loss, grads, branch, branch_all = loss_whole(
            early_all, image_all, text_proj, chip, mine, local_pairs
        )
    else:
        chips = chip ^ jnp.array(relative_chips(), jnp.int32)
        devices = jnp.concatenate([2 * chips + mine, 2 * chips + 1 - mine])
        image_ids = (
            devices[:, None] * local_pairs + jnp.arange(local_pairs, dtype=jnp.int32)[None, :]
        ).reshape(1, total_pairs)
        pair_loss, grads, branch, branch_all = loss_rows(
            early_all[:, :D],
            image_all,
            text_proj,
            early_all[:, D : D + 1].astype(f32),
            image_ids,
            (2 * chip + mine) * local_pairs,
            local_pairs,
        )
    place = chunk_places()
    grad_pre, up_own, up_other, grad_bup = up_backward(
        place, mine_one, cap_lengths, branch, slope, mlp, w_down
    )
    arrived = swap(up_other, "rep", 1)
    grad_after, grad_mixed, grad_gain = mlp_backward(
        cap_lengths, grad_pre, grads, after, text_vec, w_up, w_out
    )
    ups, rests = streams_of(FF // 4), streams_of(D)
    up_sent, up_kept = reduce_first(up_own, arrived, ups)
    (grad_mixed,) = behind([grad_mixed], up_sent)
    up_came = reduce_swaps(up_sent, ups, 1)
    caption_grad, rest_own, rest_other = rest_backward(
        place, mine_one, qkv, attention, mixed, grad_mixed, grad_after, flat, text_vec,
        grad_gain, grad_bup, w_qkv,
    )
    rest_other, *up_came = lax.optimization_barrier((rest_other, *up_came))
    arrived = swap(rest_other, "rep", 1)
    up_sent, up_kept = reduce_add(up_came, up_kept)
    up_came = reduce_swaps(up_sent, ups, 2)
    (arrived,) = behind([arrived], up_sent)
    rest_sent, rest_kept = reduce_first(rest_own, arrived, rests)
    rest_came = reduce_swaps(rest_sent, rests, 1)
    (branch_all,) = behind([branch_all], up_sent + rest_sent)
    half = D // 2
    own_columns = lax.dynamic_slice_in_dim(branch_all, mine * half, half, 1)
    if whole:
        grad_w_down = dot_tn(early_all[:, EARLY:], own_columns)
    else:
        other_columns = lax.dynamic_slice_in_dim(branch_all, (1 - mine) * half, half, 1)
        grad_w_down = dot_tn(early[:, EARLY:], own_columns) + swap(
            dot_tn(early[:, EARLY:], other_columns).astype(bf16), "rep", 1
        ).astype(f32)
        grad_w_down = lax.psum(grad_w_down, "dp")
    up_came = behind(up_came, [grad_w_down])
    up_sent, up_kept = reduce_join(up_came, up_kept)
    up_came = reduce_swaps_far(up_sent)
    rest_came = behind(rest_came, up_sent)
    rest_sent, rest_kept = reduce_add(rest_came, rest_kept)
    rest_came = reduce_swaps(rest_sent, rests, 2)
    up_came = behind(up_came, rest_sent)
    up_chunk = reduce_last(up_came, up_kept)
    up_column = spread_first(up_chunk)
    rest_came = behind(rest_came, [up_chunk])
    rest_sent, rest_kept = reduce_join(rest_came, rest_kept)
    rest_came = reduce_swaps_far(rest_sent)
    up_column = behind(up_column, rest_sent)
    up_mine = spread_second(up_column, ups)
    up_near, up_across = spread_swaps(up_mine, ups, 2), spread_swaps(up_mine, ups, 1)
    rest_came = behind(rest_came, up_mine)
    rest_chunk = reduce_last(rest_came, rest_kept)
    rest_column = spread_first(rest_chunk)
    up_near = behind(up_near, [rest_chunk])
    up_last = spread_swaps(up_near, ups, 1)
    rest_column = behind(rest_column, up_near)
    rest_mine = spread_second(rest_column, rests)
    rest_near, rest_across = spread_swaps(rest_mine, rests, 2), spread_swaps(rest_mine, rests, 1)
    up_last = behind(up_last, rest_mine)
    rest_near = behind(rest_near, up_across)
    rest_last = spread_swaps(rest_near, rests, 1)
    grad_w_up = unpack_up(place, in_quarters(up_mine, up_near, up_across, up_last))
    (rest_last[0],) = behind([rest_last[0]], [grad_w_up])
    grad_w_qkv, grad_w_out, *small = unpack_rest(
        place, in_quarters(rest_mine, rest_near, rest_across, rest_last)
    )
    return (
        pair_loss,
        caption_grad.reshape(local_pairs, CAP, D),
        small[0],
        grad_w_qkv,
        small[1],
        grad_w_out,
        small[2],
        grad_w_up,
        small[3],
        grad_w_down,
    )


def solution(mesh):
    in_specs = (
        P(("dp", "rep"), None, None),
        P(("dp", "rep")),
        P(("dp", "rep"), None, None),
        P(("dp", "rep")),
        P("rep"),
        P("rep", None),
        P("rep"),
        P("rep", None),
        P("rep"),
        P("rep", None),
        P("rep"),
        P("rep", None),
        P(),
        P(),
        P(),
        P(),
        P(),
        P(),
        P(),
        P(),
        P(),
    )
    out_specs = (
        P(("dp", "rep")),
        P(("dp", "rep"), None, None),
        P("rep"),
        P(None, "rep"),
        P("rep"),
        P(None, "rep"),
        P("rep"),
        P(None, "rep"),
        P("rep"),
        P(None, "rep"),
    )
    return jax.shard_map(local, mesh=mesh, in_specs=in_specs, out_specs=out_specs, check_vma=False)
```

```python
import functools
import math

import jax
import jax.numpy as jnp
from jax import lax
from jax.experimental import pallas as pl
from jax.experimental.pallas import tpu as pltpu
from jax.sharding import PartitionSpec as P

D = 768
HEADS = 12
FF = 3072
ILEN = 145
LOWLEN = 50
CAP = 16

SCALE = 100.0
EPS = 1e-06
NEGATIVE = -1e30
LOG2E = math.log2(math.e)
MOST_PAIRS = 2048

UNIT = 160
UNITS = 2
PART = 48
SPAN = 29
QB = 128
BW = 3 * D // 2 + D // 2 + 128
EARLY = D + 128
CHUNKS = 16

f32 = jnp.float32
bf16 = jnp.bfloat16


def dot(left_side, right_side):
    return jnp.dot(left_side, right_side, preferred_element_type=f32)


def dot_nt(left_side, right_side):
    return lax.dot_general(
        left_side, right_side, (((1,), (1,)), ((), ())), preferred_element_type=f32
    )


def dot_tn(left_side, right_side):
    return lax.dot_general(
        left_side, right_side, (((0,), (0,)), ((), ())), preferred_element_type=f32
    )


def normalize(values):
    center = values - jnp.mean(values, -1, keepdims=True)
    inverse = lax.rsqrt(jnp.mean(center * center, -1, keepdims=True) + EPS)
    return center * inverse, inverse


def norm_back(grad, normed, inverse):
    return inverse * (
        grad
        - jnp.mean(grad, -1, keepdims=True)
        - normed * jnp.mean(grad * normed, -1, keepdims=True)
    )


def normal_cdf(values):
    return 0.5 + 0.5 * lax.erf(values * (1.0 / math.sqrt(2.0)))


def split_low(values):
    big = values.astype(bf16)
    return big, (values - big.astype(f32)).astype(bf16)


def tower_kernel(
    groups_ref,
    mine_ref,
    x_hbm,
    vec_own_ref,
    vec_other_ref,
    qkv_own,
    qkv_other,
    out_own,
    out_other,
    up_own,
    up_other,
    down_own,
    down_other,
    emb_ref,
    order,
    x_ref,
    x_wide,
    wqkv,
    wout,
    wup,
    wdown,
    gain_a,
    bqkv,
    gain_m,
    bup,
    xs,
    qkv,
    mixed,
    asum,
    hsum,
    aparts,
    hparts,
    scores,
    attention,
    sems,
):
    total = x_ref.shape[1]
    pitch = total + 8
    mine = mine_ref[0]
    copies = []
    for k in range(ILEN // SPAN):
        span = pl.ds(k * SPAN, SPAN)
        copies.append(pltpu.make_async_copy(x_hbm.at[span], x_ref.at[span], sems.at[8 + k]))
    for k, (own, other, whole) in enumerate(
        (
            (qkv_own, qkv_other, wqkv),
            (out_own, out_other, wout),
            (up_own, up_other, wup),
            (down_own, down_other, wdown),
        )
    ):
        half = own.shape[0]
        copies.append(
            pltpu.make_async_copy(own, whole.at[pl.ds(mine * half, half)], sems.at[2 * k])
        )
        copies.append(
            pltpu.make_async_copy(
                other, whole.at[pl.ds((1 - mine) * half, half)], sems.at[2 * k + 1]
            )
        )
    for copy in copies:
        copy.start()

    vec_own = vec_own_ref[...].astype(f32)
    vec_other = vec_other_ref[...].astype(f32)
    low = jnp.where(mine == 0, vec_own, vec_other)
    high = jnp.where(mine == 0, vec_other, vec_own)
    start = 0
    for dest, size, at in (
        (gain_a, D // 2, (0, D // 2)),
        (bqkv, D, (0, 2 * D)),
        (gain_m, D // 2, (0, D // 2)),
        (bup, FF // 2, (0, FF // 2)),
    ):
        dest[:, at[0] : at[0] + size] = low[:, start : start + size]
        dest[:, at[1] : at[1] + size] = high[:, start : start + size]
        start += size
    bqkv[:, D : 2 * D] = jnp.zeros((1, D), f32)

    def count(i, found):
        return found + groups_ref[i]

    n_hi = lax.fori_loop(0, total, count, 0)

    def place_one(i, state):
        hi, lo = state
        group = groups_ref[i]
        order[jnp.where(group == 1, hi, lo)] = i
        return hi + group, lo + 1 - group

    lax.fori_loop(0, total, place_one, (0, n_hi))
    n_units = n_hi + (total - n_hi + 2) // 3

    xs[...] = jnp.zeros_like(xs)
    first = lax.broadcasted_iota(jnp.int32, (1, 128), 1) < 64
    key_at = lax.broadcasted_iota(jnp.int32, (UNIT, UNIT), 1)
    row_at = lax.broadcasted_iota(jnp.int32, (UNIT, UNIT), 0)
    sub = lax.broadcasted_iota(jnp.int32, (8, 1), 0)

    def place(unit, k):
        last = jnp.minimum(unit, n_units - 1)
        is_hi = last < n_hi
        where = jnp.where(is_hi, last, n_hi + 3 * (last - n_hi) + k)
        return order[jnp.minimum(where, total - 1)], is_hi

    def keep_parts(values, j, dest, col, width):
        rows = values.reshape(UNIT // 8, 8, width)
        parts = [
            jnp.sum(rows[0:6], 0),
            rows[6],
            jnp.sum(rows[7:12], 0),
            rows[12],
            jnp.sum(rows[13:18], 0),
            rows[18],
        ]
        for k, part in enumerate(parts):
            dest[j * PART + k * 8 : j * PART + k * 8 + 8, col : col + width] = part

    loads = copies[: ILEN // SPAN]
    copies = copies[ILEN // SPAN :]

    def widen(t, carry):
        for panel in range(D // 128):
            x_wide[panel, pl.ds(pl.multiple_of(t * pitch, 8), total), :] = x_ref[
                t, :, panel * 128 : (panel + 1) * 128
            ].astype(f32)
        return carry

    for k, load in enumerate(loads):
        load.wait()
        lax.fori_loop(k * SPAN, (k + 1) * SPAN, widen, 0)
    for copy in copies[:2]:
        copy.wait()

    def body(step, carry):
        for j in range(UNITS):
            unit = step * UNITS + j
            one, is_hi = place(unit, 0)
            two, three = place(unit, 1)[0], place(unit, 2)[0]
            base = j * UNIT

            @pl.when(is_hi)
            def _():
                for panel in range(D // 128):
                    xs[base : base + ILEN, panel * 128 : (panel + 1) * 128] = x_wide[
                        panel, pl.ds(one, ILEN, stride=pitch), :
                    ]

            @pl.when(jnp.logical_not(is_hi))
            def _():
                for k, index in enumerate((one, two, three)):
                    for panel in range(D // 128):
                        xs[
                            base + LOWLEN * k : base + LOWLEN * (k + 1),
                            panel * 128 : (panel + 1) * 128,
                        ] = x_wide[panel, pl.ds(index, LOWLEN, stride=pitch), :]

        low_rows = (normalize(xs[...])[0] * gain_a[...]).astype(bf16)
        for col in range(0, 3 * D, 256):
            values = dot(low_rows, wqkv[:, col : col + 256]) + bqkv[:, col : col + 256]
            if col < D:
                values = values * (LOG2E / 8.0)
            qkv[:, col : col + 256] = values.astype(bf16)

        @pl.when(step == 0)
        def _():
            for copy in copies[2:6]:
                copy.wait()

        for j in range(UNITS):
            is_hi = place(step * UNITS + j, 0)[1]
            base = j * UNIT
            key_seg = jnp.where(key_at < LOWLEN, 0, jnp.where(key_at < 2 * LOWLEN, 1, 2))
            row_seg = jnp.where(row_at < LOWLEN, 0, jnp.where(row_at < 2 * LOWLEN, 1, 2))
            short_ok = jnp.logical_and(key_seg == row_seg, key_at < 3 * LOWLEN)
            allowed = jnp.where(
                is_hi, (key_at < ILEN).astype(jnp.int32), short_ok.astype(jnp.int32)
            )
            bias = jnp.where(allowed > 0, 0.0, NEGATIVE)
            for p in range(HEADS // 2):
                query = qkv[base : base + UNIT, p * 128 : (p + 1) * 128]
                key = qkv[base : base + UNIT, D + p * 128 : D + (p + 1) * 128]
                for h in range(2):
                    head = first if h == 0 else jnp.logical_not(first)
                    at = (j * HEADS + 2 * p + h) * UNIT
                    scores[at : at + UNIT, :] = (
                        dot_nt(jnp.where(head, query, jnp.zeros_like(query)), key) + bias
                    )
        for j in range(UNITS):
            part = slice(j * HEADS * UNIT, (j + 1) * HEADS * UNIT)
            values = scores[part, :]
            powers = jnp.exp2(values - jnp.max(values, 1, keepdims=True))
            attention[part, :] = powers.astype(bf16)
        for j in range(UNITS):
            base = j * UNIT
            for p in range(HEADS // 2):
                lanes = slice(p * 128, (p + 1) * 128)
                value = qkv[base : base + UNIT, 2 * D + p * 128 : 2 * D + (p + 1) * 128]
                outs = []
                at = (j * HEADS + 2 * p) * UNIT
                value_one = jnp.concatenate([value, jnp.ones_like(value)], 1)
                for h in range(2):
                    summed = dot(attention[at + h * UNIT : at + (h + 1) * UNIT, :], value_one)
                    outs.append(summed[:, :128] / summed[:, 128:])
                mixed[base : base + UNIT, lanes] = jnp.where(first, outs[0], outs[1]).astype(bf16)
        for col in range(0, D, 256):
            xs[:, col : col + 256] += dot(mixed[...], wout[:, col : col + 256])
        for j in range(UNITS):
            keep_parts(xs[j * UNIT : (j + 1) * UNIT, :], j, aparts, 0, D)
        low_two = (normalize(xs[...])[0] * gain_m[...]).astype(bf16)
        width = 1024
        for col in range(0, FF, width):
            pre_act = dot(low_two, wup[:, col : col + width]) + bup[:, col : col + width]
            hidden = pre_act * normal_cdf(pre_act)
            for j in range(UNITS):
                keep_parts(hidden[j * UNIT : (j + 1) * UNIT], j, hparts, col, width)
        for j in range(UNITS):
            unit = step * UNITS + j
            one, is_hi = place(unit, 0)
            two, three = place(unit, 1)[0], place(unit, 2)[0]

            def rows_of(index):
                return pl.ds(pl.multiple_of(index * 8, 8), 8)

            @pl.when(is_hi)
            def _():
                for src, dest in ((aparts, asum), (hparts, hsum)):
                    part = [src[j * PART + k * 8 : j * PART + k * 8 + 8, :] for k in range(6)]
                    dest[rows_of(one), :] = (
                        (part[0] + part[1])
                        + (part[2] + part[3])
                        + (part[4] + jnp.where(sub < 1, part[5], 0.0))
                    )

            @pl.when(jnp.logical_not(is_hi))
            def _():
                for src, dest in ((aparts, asum), (hparts, hsum)):
                    part = [src[j * PART + k * 8 : j * PART + k * 8 + 8, :] for k in range(6)]
                    dest[rows_of(three), :] = (
                        jnp.where(sub < 4, 0.0, part[3])
                        + part[4]
                        + jnp.where(sub < 6, part[5], 0.0)
                    )
                    dest[rows_of(two), :] = (
                        jnp.where(sub < 2, 0.0, part[1])
                        + part[2]
                        + jnp.where(sub < 4, part[3], 0.0)
                    )
                    dest[rows_of(one), :] = part[0] + jnp.where(sub < 2, part[1], 0.0)

        return carry

    lax.fori_loop(0, (n_units + UNITS - 1) // UNITS, body, 0)
    for copy in copies[6:]:
        copy.wait()
    which = lax.broadcasted_iota(jnp.int32, (total, 128), 0)
    scale = jnp.zeros((total, 128), f32)
    for i in range(total):
        scale = jnp.where(
            which == i, jnp.where(groups_ref[i] == 1, 1.0 / ILEN, 1.0 / LOWLEN), scale
        )
    scale = scale[:, 0:1]
    big, rest = split_low(jnp.sum(hsum[...].reshape(total, 8, FF), 1) * scale)
    product = dot(jnp.concatenate([big, rest], 0), wdown[...])
    pooled = jnp.sum(asum[...].reshape(total, 8, D), 1) * scale + product[:total] + product[total:]
    emb_ref[...] = (
        pooled * lax.rsqrt(jnp.sum(pooled * pooled, -1, keepdims=True) + EPS)
    ).astype(bf16)


VM = pl.BlockSpec(memory_space=pltpu.VMEM)
SM = pl.BlockSpec(memory_space=pltpu.SMEM)
ANY = pl.BlockSpec(memory_space=pltpu.HBM)


def limit(mebibytes):
    return pltpu.CompilerParams(vmem_limit_bytes=mebibytes * 1024 * 1024)


def image_tower(images, groups, mine, vec_own, vec_other, weights):
    number = images.shape[1]
    rows = UNITS * UNIT
    flops = number * 100 * 2 * (4 * D * D + D * FF)
    return pl.pallas_call(
        tower_kernel,
        out_shape=jax.ShapeDtypeStruct((number, D), bf16),
        in_specs=[SM, SM, ANY, VM, VM] + [ANY] * 8,
        out_specs=VM,
        scratch_shapes=[
            pltpu.SMEM((number,), jnp.int32),
            pltpu.VMEM(images.shape, bf16),
            pltpu.VMEM((D // 128, ILEN * (number + 8), 128), f32),
            pltpu.VMEM((D, 3 * D), bf16),
            pltpu.VMEM((D, D), bf16),
            pltpu.VMEM((D, FF), bf16),
            pltpu.VMEM((FF, D), bf16),
            pltpu.VMEM((1, D), f32),
            pltpu.VMEM((1, 3 * D), f32),
            pltpu.VMEM((1, D), f32),
            pltpu.VMEM((1, FF), f32),
            pltpu.VMEM((rows, D), f32),
            pltpu.VMEM((rows, 3 * D), bf16),
            pltpu.VMEM((rows, D), bf16),
            pltpu.VMEM((number * 8, D), f32),
            pltpu.VMEM((number * 8, FF), f32),
            pltpu.VMEM((UNITS * PART, D), f32),
            pltpu.VMEM((UNITS * PART, FF), f32),
            pltpu.VMEM((UNITS * HEADS * UNIT, UNIT), f32),
            pltpu.VMEM((UNITS * HEADS * UNIT, UNIT), bf16),
            pltpu.SemaphoreType.DMA((8 + ILEN // SPAN,)),
        ],
        compiler_params=limit(62),
        cost_estimate=pl.CostEstimate(
            flops=flops, bytes_accessed=24 * 1024 * 1024, transcendentals=0
        ),
        name="image_tower",
    )(groups, mine, images, vec_own, vec_other, *weights)


def lens_along(lens_ref, start, number):
    owner = lax.broadcasted_iota(jnp.int32, (1, number * CAP), 1) // CAP
    lens = jnp.zeros((1, number * CAP), jnp.int32)
    for c in range(number):
        lens = jnp.where(owner == c, lens_ref[start + c], lens)
    return lens


def score_bias(lens_ref, block):
    per = QB // CAP
    position = lax.broadcasted_iota(jnp.int32, (1, QB), 1) % CAP
    valid = position < lens_along(lens_ref, block * per, per)
    rows = lax.broadcasted_iota(jnp.int32, (QB, QB), 0) // CAP
    columns = lax.broadcasted_iota(jnp.int32, (QB, QB), 1) // CAP
    return jnp.where(jnp.logical_and(rows == columns, valid), 0.0, NEGATIVE)


def forward_kernel(
    lens_ref,
    x_ref,
    vec_ref,
    wqkv_ref,
    wout_ref,
    wup_ref,
    wdown_ref,
    qkv,
    mixed,
    after,
    mlp,
    slope,
    attention,
    early,
    hidden,
    scores,
):
    rows = x_ref.shape[0]
    number = rows // CAP
    first = lax.broadcasted_iota(jnp.int32, (1, 128), 1) < 64
    normed, _ = normalize(x_ref[...].astype(f32))
    low = (normed * vec_ref[:, 0:D]).astype(bf16)
    for col in range(0, 3 * D, 256):
        values = dot(low, wqkv_ref[:, col : col + 256])
        if col < D:
            values = values + vec_ref[:, D + col : D + col + 256]
        if col >= 2 * D:
            values = values + vec_ref[:, col : col + 256]
        values = values.astype(bf16)
        if col < D:
            values = values * jnp.asarray(0.125, bf16)
        qkv[:, col : col + 256] = values
    for block in range(rows // QB):
        bias = score_bias(lens_ref, block)
        span = slice(block * QB, (block + 1) * QB)
        for p in range(HEADS // 2):
            query = qkv[span, p * 128 : (p + 1) * 128]
            key = qkv[span, D + p * 128 : D + (p + 1) * 128]
            for h in range(2):
                head = first if h == 0 else jnp.logical_not(first)
                at = (block * HEADS + 2 * p + h) * QB
                scores[at : at + QB, :] = (
                    dot_nt(jnp.where(head, query, jnp.zeros_like(query)), key) * LOG2E + bias
                )
    for block in range(rows // QB):
        part = slice(block * HEADS * QB, (block + 1) * HEADS * QB)
        values = scores[part, :]
        powers = jnp.exp2(values - jnp.max(values, 1, keepdims=True))
        attention[part, :] = (powers * (1.0 / jnp.sum(powers, 1, keepdims=True))).astype(bf16)
    for block in range(rows // QB):
        span = slice(block * QB, (block + 1) * QB)
        for p in range(HEADS // 2):
            value = qkv[span, 2 * D + p * 128 : 2 * D + (p + 1) * 128]
            at = (block * HEADS + 2 * p) * QB
            outs = [dot(attention[at + h * QB : at + (h + 1) * QB, :], value) for h in range(2)]
            mixed[span, p * 128 : (p + 1) * 128] = jnp.where(first, outs[0], outs[1]).astype(bf16)
    for col in range(0, D, 256):
        after[:, col : col + 256] = x_ref[:, col : col + 256].astype(f32) + dot(
            mixed[...], wout_ref[:, col : col + 256]
        )
    mlp[...] = (normalize(after[...])[0] * vec_ref[:, 3 * D : 4 * D]).astype(bf16)
    lens = lens_along(lens_ref, 0, number)
    position = lax.broadcasted_iota(jnp.int32, (1, rows), 1)
    owner = (
        lax.broadcasted_iota(jnp.int32, (number, rows), 0)
        == lax.broadcasted_iota(jnp.int32, (number, rows), 1) // CAP
    )
    members = jnp.where(jnp.logical_and(owner, position % CAP < lens), 1.0, 0.0)
    pool = members.astype(bf16)
    count = jnp.sum(members, 1, keepdims=True)
    width = 512
    for col in range(0, FF, width):
        span = slice(col, col + width)
        pre_act = dot(mlp[...], wup_ref[:, span]) + vec_ref[:, 4 * D + col : 4 * D + col + width]
        phi = normal_cdf(pre_act)
        hidden[:, span] = (pre_act * phi).astype(bf16)
        density = jnp.exp2(pre_act * pre_act * (-0.5 * LOG2E)) * (1.0 / math.sqrt(2.0 * math.pi))
        slope[:, span] = (phi + pre_act * density).astype(bf16)
    big, rest = split_low(dot(pool, hidden[...]))
    after_big, after_rest = split_low(after[...])
    pooled = (
        dot(pool, after_big)
        + dot(pool, after_rest)
        + dot(big, wdown_ref[...])
        + dot(rest, wdown_ref[...])
    )
    early[:, 0:D] = (pooled / count).astype(bf16)
    early[:, D:EARLY] = jnp.broadcast_to(count, (number, EARLY - D)).astype(bf16)
    early[:, EARLY:] = big


def text_forward(captions, lens, vec, w_qkv, w_out, w_up, w_down):
    rows = captions.shape[0]
    shape = jax.ShapeDtypeStruct
    return pl.pallas_call(
        forward_kernel,
        out_shape=[
            shape((rows, 3 * D), bf16),
            shape((rows, D), bf16),
            shape((rows, D), f32),
            shape((rows, D), bf16),
            shape((rows, FF), bf16),
            shape((rows * HEADS, QB), bf16),
            shape((rows // CAP, EARLY + FF), bf16),
        ],
        in_specs=[SM] + [VM] * 6,
        out_specs=[VM] * 7,
        scratch_shapes=[pltpu.VMEM((rows, FF), bf16), pltpu.VMEM((rows * HEADS, QB), f32)],
        compiler_params=limit(60),
        cost_estimate=pl.CostEstimate(
            flops=2 * rows * (4 * D * D + 2 * D * FF),
            bytes_accessed=24 * 1024 * 1024,
            transcendentals=0,
        ),
        name="text_forward",
    )(lens, captions, vec, w_qkv, w_out, w_up, w_down)


def put_chunks(dest, values, place_ref, stream, col):
    rows = values.shape[0] // CHUNKS
    for chunk in range(CHUNKS):
        at = pl.multiple_of(place_ref[stream, chunk] * rows, 16)
        dest[pl.ds(at, rows), col : col + values.shape[1]] = values[
            chunk * rows : (chunk + 1) * rows
        ].astype(dest.dtype)


def up_kernel(
    place_ref, mine_ref, lens_ref, branch_ref, slope_ref, mlp_ref, wdown_ref,
    grad_pre, own, other, grad_bup, grad_hidden, mlp_t,
):
    number = slope_ref.shape[0] // CAP
    half = FF // 2
    mine = mine_ref[0]
    for col in range(0, FF, 512):
        grad_hidden[:, col : col + 512] = dot_nt(branch_ref[...], wdown_ref[col : col + 512, :])
    position = lax.broadcasted_iota(jnp.int32, (CAP, 1), 0)
    for c in range(number):
        span = slice(c * CAP, (c + 1) * CAP)
        keep = jnp.where(position < lens_ref[c], 1.0, 0.0)
        grad_pre[span, :] = (
            grad_hidden[c : c + 1, :] * slope_ref[span, :].astype(f32) * keep
        ).astype(bf16)
    mlp_t[...] = mlp_ref[...].T
    for which, dest in ((1 - mine, other), (mine, own)):
        for col in range(0, half, 384):
            lanes = pl.ds(pl.multiple_of(which * half + col, 128), 384)
            put_chunks(dest, dot(mlp_t[...], grad_pre[:, lanes]), place_ref, 2 * col // half, col)
    for col in range(0, FF, 512):
        grad_bup[:, col : col + 512] = jnp.sum(
            grad_pre[:, col : col + 512].astype(f32), 0, keepdims=True
        )


def up_backward(place, mine, lens, branch, slope, mlp, w_down):
    rows = slope.shape[0]
    shape = jax.ShapeDtypeStruct
    return pl.pallas_call(
        up_kernel,
        out_shape=[
            shape((rows, FF), bf16),
            shape((D, FF // 2), f32),
            shape((D, FF // 2), bf16),
            shape((1, FF), f32),
        ],
        in_specs=[SM, SM, SM] + [VM] * 4,
        out_specs=[VM] * 4,
        scratch_shapes=[pltpu.VMEM((rows // CAP, FF), f32), pltpu.VMEM((D, rows), bf16)],
        compiler_params=limit(32),
        cost_estimate=pl.CostEstimate(
            flops=2 * rows * D * FF, bytes_accessed=20 * 1024 * 1024, transcendentals=0
        ),
        name="up_backward",
    )(place, mine, lens, branch, slope, mlp, w_down)


def mlp_kernel(
    lens_ref, pre_ref, grad_ref, after_ref, vec_ref, wup_ref, wout_ref,
    grad_after, grad_mixed, grad_gain, grad_out,
):
    number = after_ref.shape[0] // CAP
    grad_mlp = dot_nt(pre_ref[...], wup_ref[...])
    normed_two, inverse_two = normalize(after_ref[...])
    grad_gain[...] = jnp.sum(grad_mlp * normed_two, 0, keepdims=True)
    grad_after[...] = norm_back(grad_mlp * vec_ref[:, 3 * D : 4 * D], normed_two, inverse_two)
    position = lax.broadcasted_iota(jnp.int32, (CAP, 1), 0)
    for c in range(number):
        keep = jnp.where(position < lens_ref[c], 1.0, 0.0)
        grad_after[c * CAP : (c + 1) * CAP, :] += grad_ref[c : c + 1, :] * keep
    grad_out[...] = grad_after[...].astype(bf16)
    for col in range(0, D, 256):
        grad_mixed[:, col : col + 256] = dot_nt(
            grad_out[...], wout_ref[col : col + 256, :]
        ).astype(bf16)


def mlp_backward(lens, grad_pre, grads, after, vec, w_up, w_out):
    rows = after.shape[0]
    shape = jax.ShapeDtypeStruct
    return pl.pallas_call(
        mlp_kernel,
        out_shape=[shape((rows, D), f32), shape((rows, D), bf16), shape((1, D), f32)],
        in_specs=[SM] + [VM] * 6,
        out_specs=[VM] * 3,
        scratch_shapes=[pltpu.VMEM((rows, D), bf16)],
        compiler_params=limit(36),
        cost_estimate=pl.CostEstimate(
            flops=2 * rows * (D * D + D * FF), bytes_accessed=20 * 1024 * 1024, transcendentals=0
        ),
        name="mlp_backward",
    )(lens, grad_pre, grads, after, vec, w_up, w_out)


def attention_kernel(
    qkv_ref, att_ref, mixed_ref, grad_ref, grad_proj, grad_att, means, grad_s, *, start
):
    first = lax.broadcasted_iota(jnp.int32, (1, 128), 1) < 64
    ones = jnp.ones((128, QB), bf16)
    heads = (first, jnp.logical_not(first))
    blocks = grad_proj.shape[0] // QB
    for block in range(blocks):
        span = slice(start + block * QB, start + (block + 1) * QB)
        for p in range(HEADS // 2):
            at = p * 128
            value = qkv_ref[span, 2 * D + at : 2 * D + at + 128]
            grad = grad_ref[span, at : at + 128]
            product = (grad.astype(f32) * mixed_ref[span, at : at + 128].astype(f32)).astype(bf16)
            for h, head in enumerate(heads):
                to = (block * HEADS + 2 * p + h) * QB
                grad_att[to : to + QB, :] = dot_nt(
                    jnp.where(head, grad, jnp.zeros_like(grad)), value
                )
                means[to : to + QB, :] = dot(
                    jnp.where(head, product, jnp.zeros_like(product)), ones
                )
    for block in range(blocks):
        part = slice(block * HEADS * QB, (block + 1) * HEADS * QB)
        place = (start // QB + block) * HEADS * QB
        low = att_ref[place : place + HEADS * QB, :].astype(f32)
        grad_s[part, :] = (low * (grad_att[part, :] - means[part, :])).astype(bf16)
    for block in range(blocks):
        span = slice(start + block * QB, start + (block + 1) * QB)
        dest = slice(block * QB, (block + 1) * QB)
        for p in range(HEADS // 2):
            at = p * 128
            query = qkv_ref[span, at : at + 128]
            key = qkv_ref[span, D + at : D + at + 128]
            grad = grad_ref[span, at : at + 128]
            grad_q, grad_k, grad_v = [], [], []
            for h in range(2):
                to = (block * HEADS + 2 * p + h) * QB
                place = ((start // QB + block) * HEADS + 2 * p + h) * QB
                sgrad = grad_s[to : to + QB, :]
                grad_q.append(dot(sgrad, key))
                grad_k.append(dot_tn(sgrad, query))
                grad_v.append(dot_tn(att_ref[place : place + QB, :], grad))
            for k, (parts, scale) in enumerate(((grad_q, 0.125), (grad_k, 1.0), (grad_v, 1.0))):
                grad_proj[dest, k * D + at : k * D + at + 128] = (
                    jnp.where(first, parts[0], parts[1]) * scale
                ).astype(bf16)


def input_kernel(
    proj_ref, after_ref, x_ref, vec_ref, gain_ref, bup_ref, wqkv_ref, caption_grad, sums, input_low
):
    gain_a = vec_ref[:, 0:D]
    normed_one, inverse_one = normalize(x_ref[...].astype(f32))
    input_low[...] = (normed_one * gain_a).astype(bf16)
    grad_in = dot_nt(proj_ref[...], wqkv_ref[...])
    sums[:, 0:D] = jnp.sum(grad_in * normed_one, 0, keepdims=True)
    sums[:, D : 2 * D] = jnp.sum(proj_ref[:, 0:D].astype(f32), 0, keepdims=True)
    sums[:, 2 * D : 3 * D] = jnp.sum(proj_ref[:, 2 * D :].astype(f32), 0, keepdims=True)
    sums[:, 3 * D : 4 * D] = gain_ref[...]
    sums[:, 4 * D :] = bup_ref[...]
    caption_grad[...] = after_ref[...] + norm_back(grad_in * gain_a, normed_one, inverse_one)


def proj_kernel(
    place_ref, mine_ref, proj_ref, after_ref, mixed_ref, input_ref, sums, own, other, lhs_t, grad_out
):
    chunk_rows = D // CHUNKS
    mine = mine_ref[0]
    lhs_t[...] = input_ref[...].T
    half_out, half_qkv = D // 2, 3 * D // 2
    for which, dest in ((1 - mine, other), (mine, own)):
        for col in range(0, half_qkv, 384):
            lanes = pl.ds(pl.multiple_of(which * half_qkv + col, 128), 384)
            put_chunks(dest, dot(lhs_t[...], proj_ref[:, lanes]), place_ref, col // 768, col)
    lhs_t[...] = mixed_ref[...].T
    grad_out[...] = after_ref[...].astype(bf16)
    for which, dest in ((1 - mine, other), (mine, own)):
        lanes = pl.ds(pl.multiple_of(which * half_out, 128), half_out)
        put_chunks(dest, dot(lhs_t[...], grad_out[:, lanes]), place_ref, 1, half_qkv)
    for which, dest in ((1 - mine, other), (mine, own)):
        dest[:, BW - 128 :] = jnp.zeros((D, 128), dest.dtype)
        pieces = []
        for start, size in ((0, D), (D, 2 * D), (3 * D, D), (4 * D, FF)):
            for k in range(0, size // 2, 128):
                at = pl.multiple_of(start + which * (size // 2) + k, 128)
                pieces.append(sums[:, pl.ds(at, 128)])
        pieces += [jnp.zeros_like(pieces[0])] * (32 - len(pieces))
        at = pl.multiple_of(place_ref[1, 0] * chunk_rows, 16)
        dest[pl.ds(at, 32), BW - 128 :] = jnp.concatenate(pieces, 0).astype(dest.dtype)


def rest_kernel(
    place_ref, mine_ref, qkv_ref, att_ref, mixed_ref, grad_ref, after_ref, x_ref, vec_ref,
    gain_ref, bup_ref, wqkv_ref, caption_grad, own, other,
    grad_proj, sums, input_low, grad_att, means, grad_s, lhs_t, grad_out,
):
    attention_kernel(
        qkv_ref, att_ref, mixed_ref, grad_ref, grad_proj, grad_att, means, grad_s, start=0
    )
    input_kernel(
        grad_proj, after_ref, x_ref, vec_ref, gain_ref, bup_ref, wqkv_ref,
        caption_grad, sums, input_low,
    )
    proj_kernel(
        place_ref, mine_ref, grad_proj, after_ref, mixed_ref, input_low, sums,
        own, other, lhs_t, grad_out,
    )


def rest_backward(
    place, mine, qkv, attention, mixed, grad_mixed, grad_after, captions, vec, grad_gain, grad_bup, w_qkv
):
    rows = captions.shape[0]
    shape = jax.ShapeDtypeStruct
    return pl.pallas_call(
        rest_kernel,
        out_shape=[shape((rows, D), f32), shape((D, BW), f32), shape((D, BW), bf16)],
        in_specs=[SM, SM] + [VM] * 10,
        out_specs=[VM] * 3,
        scratch_shapes=[
            pltpu.VMEM((rows, 3 * D), bf16),
            pltpu.VMEM((1, 4 * D + FF), f32),
            pltpu.VMEM((rows, D), bf16),
            pltpu.VMEM((rows * HEADS, QB), f32),
            pltpu.VMEM((rows * HEADS, QB), f32),
            pltpu.VMEM((rows * HEADS, QB), bf16),
            pltpu.VMEM((D, rows), bf16),
            pltpu.VMEM((rows, D), bf16),
        ],
        compiler_params=limit(46),
        cost_estimate=pl.CostEstimate(
            flops=2 * rows * 48 * D * D, bytes_accessed=60 * 1024 * 1024, transcendentals=0
        ),
        name="rest_backward",
    )(
        place, mine, qkv, attention, mixed, grad_mixed, grad_after, captions, vec,
        grad_gain, grad_bup, w_qkv,
    )


def dp_bits():
    bits, bit = [], 1
    while bit < lax.axis_size("dp"):
        bits.append(bit)
        bit *= 2
    return bits


def swap(values, axis, bit):
    size = lax.axis_size(axis)
    return lax.ppermute(values, axis, [(place, place ^ bit) for place in range(size)])


def gather_relative(values):
    bits = dp_bits()
    while bits:
        pair = bits[-2:]
        bits = bits[:-2]
        offsets = [0]
        for bit in pair:
            offsets += [entry + bit for entry in offsets]
        values = jnp.concatenate([swap(values, "dp", k) if k else values for k in offsets], 0)
    return jnp.concatenate([values, swap(values, "rep", 1)], 0)


def relative_chips():
    bits, table = dp_bits(), [0]
    while bits:
        pair = bits[-2:]
        bits = bits[:-2]
        offsets = [0]
        for bit in pair:
            offsets += [entry + bit for entry in offsets]
        table = [entry ^ k for k in offsets for entry in table]
    return table


def chunk_places():
    away = jnp.arange(CHUNKS, dtype=jnp.int32) ^ (lax.axis_index("dp") % CHUNKS)
    one, two, rest = away % 2, away // 2 % 2, away // 4
    return jnp.stack([one * 8 + two * 4 + rest, two * 8 + one * 4 + rest]).astype(jnp.int32)


def streams_of(width):
    return ((slice(0, width), 1, 2), (slice(width, None), 2, 1))


def reduce_first(own, arrived, streams):
    half = own.shape[0] // 2

    def both(rows, lanes):
        return own[rows, lanes] + arrived[rows, lanes].astype(f32)

    sent = [both(slice(half, None), lanes).astype(bf16) for lanes, _, _ in streams]
    return sent, [both(slice(0, half), lanes) for lanes, _, _ in streams]


def reduce_swaps(sent, streams, stage):
    return [swap(piece, "dp", stream[stage]) for piece, stream in zip(sent, streams)]


def reduce_add(came, kept):
    half = kept[0].shape[0] // 2
    totals = [total + got.astype(f32) for total, got in zip(kept, came)]
    return [total[half:].astype(bf16) for total in totals], [total[:half] for total in totals]


def reduce_join(came, kept):
    total = jnp.concatenate([total + got.astype(f32) for total, got in zip(kept, came)], 1)
    rows = total.shape[0] // 4
    return [total[k * rows : (k + 1) * rows].astype(bf16) for k in (1, 2, 3)], total[:rows]


def reduce_last(parts, total):
    total = total + sum(part.astype(f32) for part in parts)
    for bit in dp_bits()[4:]:
        total = total + swap(total.astype(bf16), "dp", bit).astype(f32)
    return total.astype(bf16)


def spread_first(chunk):
    return [swap(chunk, "dp", 4 * k) if k else chunk for k in range(4)]


def spread_second(column, streams):
    return [jnp.concatenate([piece[:, lanes] for piece in column], 0) for lanes, _, _ in streams]


def spread_swaps(pieces, streams, stage):
    return [swap(piece, "dp", stream[stage]) for piece, stream in zip(pieces, streams)]


def reduce_swaps_far(sent):
    return [swap(piece, "dp", 4 * (k + 1)) for k, piece in enumerate(sent)]


def in_quarters(*quarters):
    return [quarter[stream] for stream in range(2) for quarter in quarters]


def behind(values, others):
    return list(lax.optimization_barrier((*values, *others))[: len(values)])


def each_chunk(place_ref):
    rows = D // CHUNKS
    place = place_ref[0, 0]
    me = place // 8 + 2 * (place // 4 % 2) + 4 * (place % 4)
    for stream in range(2):
        for quarter in range(4):
            for k in range(4):
                high, low = quarter // 2, quarter % 2
                away = (high + 2 * low if stream == 0 else low + 2 * high) + 4 * k
                chunk = me ^ away
                at = pl.ds(pl.multiple_of(chunk * rows, 16), rows)
                yield stream, stream * 4 + quarter, slice(k * rows, (k + 1) * rows), chunk, at


def unpack_up_kernel(place_ref, *refs):
    parts, g_up = refs[:8], refs[8]
    for stream, part, span, _, at in each_chunk(place_ref):
        lanes = slice(stream * FF // 4, (stream + 1) * FF // 4)
        g_up[at, lanes] = parts[part][span, :].astype(f32)


def unpack_rest_kernel(place_ref, *refs):
    parts, (g_qkv, g_out), vectors = refs[:8], refs[8:10], refs[10:]
    for stream, part, span, chunk, at in each_chunk(place_ref):
        rest = parts[part][span, :].astype(f32)
        if stream == 0:
            g_qkv[at, 0:D] = rest
            continue
        g_qkv[at, D:] = rest[:, : D // 2]
        g_out[at, :] = rest[:, D // 2 : D]

        @pl.when(chunk == 0)
        def _():
            row = 0
            for dest in vectors:
                for lane in range(0, dest.shape[0], 128):
                    dest[lane : lane + 128] = rest[row, D:]
                    row += 1


def unpack_up(place, parts):
    return pl.pallas_call(
        unpack_up_kernel,
        out_shape=jax.ShapeDtypeStruct((D, FF // 2), f32),
        in_specs=[SM] + [VM] * 8,
        out_specs=VM,
        compiler_params=limit(20),
        name="unpack_up",
    )(place, *parts)


def unpack_rest(place, parts):
    shape = jax.ShapeDtypeStruct
    return pl.pallas_call(
        unpack_rest_kernel,
        out_shape=[
            shape((D, 3 * D // 2), f32),
            shape((D, D // 2), f32),
            shape((D // 2,), f32),
            shape((D,), f32),
            shape((D // 2,), f32),
            shape((FF // 2,), f32),
        ],
        in_specs=[SM] + [VM] * 8,
        out_specs=[VM] * 6,
        compiler_params=limit(20),
        name="unpack_rest",
    )(place, *parts)


def softmax_parts(scores, axis):
    maxima = jnp.max(scores, axis, keepdims=True)
    powers = jnp.exp(scores - maxima)
    totals = jnp.sum(powers, axis, keepdims=True)
    return powers / totals, maxima + jnp.log(totals)


def text_unit(pooled_low, text_proj):
    proj_out = dot(pooled_low, text_proj)
    inverse_z = lax.rsqrt(jnp.sum(proj_out * proj_out, -1, keepdims=True) + EPS)
    return proj_out * inverse_z, inverse_z


def branch_grad(grad_unit, unit_text, inverse_z, text_proj, lengths):
    grad_projout = (
        inverse_z * (grad_unit - unit_text * jnp.sum(unit_text * grad_unit, -1, keepdims=True))
    ).astype(bf16)
    return dot_nt(grad_projout, text_proj) / lengths


def loss_kernel(
    where_ref, early_hbm, image_ref, proj_ref, pair_loss, own_grads, own_branch, branch,
    unit, inverse, scores, sgrad, early_ref, sem,
):
    copy = pltpu.make_async_copy(early_hbm.at[:, pl.ds(0, EARLY)], early_ref, sem)
    copy.start()
    copy.wait()
    total = image_ref.shape[0]
    number = own_grads.shape[0]
    chip, mine = where_ref[0], where_ref[1]
    block = 256
    for row in range(0, total, block):
        span = slice(row, row + block)
        proj_out = dot(early_ref[span, 0:D], proj_ref[...])
        inverse_z = lax.rsqrt(jnp.sum(proj_out * proj_out, -1, keepdims=True) + EPS)
        inverse[span, :] = jnp.broadcast_to(inverse_z, (block, 128))
        unit[span, :] = proj_out * inverse_z
        scores[span, :] = dot_nt(unit[span, :].astype(bf16), image_ref[...]) * SCALE
    place = lax.broadcasted_iota(jnp.int32, (1, total), 1) // number
    chips = total // (2 * number)
    away = place % chips
    other = place // chips
    from_chip = chip ^ (away // 4 + 4 * (away % 4)) if chips == 16 else None
    image_id = (from_chip * 2 + (mine ^ other)) * number + (
        lax.broadcasted_iota(jnp.int32, (1, total), 1) % number
    )
    column_max = jnp.max(scores[...], 0, keepdims=True)
    column_sum = jnp.zeros((1, total), f32)
    for row in range(0, total, block):
        column_sum += jnp.sum(
            jnp.exp(scores[row : row + block, :] - column_max), 0, keepdims=True
        )
    column_total = column_max + jnp.log(column_sum)
    for row in range(0, total, block):
        span = slice(row, row + block)
        values = scores[span, :]
        row_max = jnp.max(values, 1, keepdims=True)
        powers = jnp.exp(values - row_max)
        by_text = powers * (0.5 / jnp.sum(powers, 1, keepdims=True))
        by_image = jnp.exp(values - column_max) * (0.5 / column_sum)
        text_id = lax.broadcasted_iota(jnp.int32, (block, 1), 0) + row
        same = jnp.where(text_id == image_id, 1.0, 0.0)
        sgrad[span, :] = (by_text + by_image - same).astype(bf16)
        grad_unit = dot(sgrad[span, :], image_ref[...]) * SCALE
        unit_text = unit[span, :]
        grad_proj = (
            inverse[span, 0:1]
            * (grad_unit - unit_text * jnp.sum(unit_text * grad_unit, -1, keepdims=True))
        ).astype(bf16)
        unit[span, :] = dot_nt(grad_proj, proj_ref[...]) / early_ref[span, D : D + 1].astype(f32)
        branch[span, :] = unit[span, :].astype(bf16)
    first = pl.multiple_of((chip * 2 + mine) * number, 32)
    own_grads[...] = unit[pl.ds(first, number), :]
    own_branch[...] = unit[pl.ds(first, number), :].astype(bf16)
    values = scores[pl.ds(first, number), :]
    row_max = jnp.max(values, 1, keepdims=True)
    row_total = row_max + jnp.log(jnp.sum(jnp.exp(values - row_max), 1, keepdims=True))
    text_id = lax.broadcasted_iota(jnp.int32, (number, 1), 0) + first
    same = jnp.where(text_id == image_id, 1.0, 0.0)
    both = 0.5 * (row_total + column_total) - values
    pair_loss[...] = jnp.broadcast_to(jnp.sum(both * same, 1, keepdims=True), (number, 128))


def loss_whole(early_all, image_all, text_proj, chip, mine, number):
    total = image_all.shape[0]
    shape = jax.ShapeDtypeStruct
    pair_loss, grads, own_branch, branch = pl.pallas_call(
        loss_kernel,
        out_shape=[
            shape((number, 128), f32),
            shape((number, D), f32),
            shape((number, D), bf16),
            shape((total, D), bf16),
        ],
        in_specs=[SM, ANY, VM, VM],
        out_specs=[VM] * 4,
        scratch_shapes=[
            pltpu.VMEM((total, D), f32),
            pltpu.VMEM((total, 128), f32),
            pltpu.VMEM((total, total), f32),
            pltpu.VMEM((total, total), bf16),
            pltpu.VMEM((total, EARLY), bf16),
            pltpu.SemaphoreType.DMA,
        ],
        compiler_params=limit(30),
        name="pair_loss",
    )(jnp.stack([chip, mine]), early_all, image_all, text_proj)
    return pair_loss[:, 0], grads, own_branch, branch


def loss_rows(pooled_all, image_all, text_proj, lengths_all, image_ids, first_row, local_pairs):
    unit_all, inverse_all = text_unit(pooled_all, text_proj)

    def own_rows(values):
        return lax.dynamic_slice_in_dim(values, first_row, local_pairs, 0)

    unit_text, inverse_z = own_rows(unit_all), own_rows(inverse_all)
    text_scores = dot_nt(unit_text.astype(bf16), image_all) * SCALE
    image_scores = dot_nt(image_all[:local_pairs], unit_all.astype(bf16)) * SCALE
    by_text, text_total = softmax_parts(text_scores, 1)
    image_total = softmax_parts(image_scores, 1)[1]
    every_total = gather_relative(image_total)
    text_ids = first_row + jnp.arange(local_pairs, dtype=jnp.int32)
    own_same = (text_ids[:, None] == image_ids).astype(f32)
    own = jnp.sum(text_scores * own_same, -1)
    pair_loss = 0.5 * (text_total[:, 0] - own) + 0.5 * (image_total[:, 0] - own)
    by_image = jnp.exp(text_scores - every_total[:, 0][None, :])
    sgrad = (0.5 * (by_text - own_same) + 0.5 * (by_image - own_same)).astype(bf16)
    grad_unit = dot(sgrad, image_all) * SCALE
    grads = branch_grad(grad_unit, unit_text, inverse_z, text_proj, own_rows(lengths_all))
    return pair_loss, grads, grads.astype(bf16), grads.astype(bf16)


def local(
    images,
    groups,
    captions,
    cap_lengths,
    img_gain_a,
    img_w_qkv,
    img_b_qv,
    img_w_out,
    img_gain_m,
    img_w_up,
    img_b_up,
    img_w_down,
    gain_attn,
    w_qkv,
    b_qv,
    w_out,
    gain_mlp,
    w_up,
    b_up,
    w_down,
    text_proj,
):
    local_pairs = images.shape[0]
    rows_total = local_pairs * CAP
    mine = lax.axis_index("rep").astype(jnp.int32)
    mine_one = mine[None]
    total_pairs = local_pairs * lax.axis_size("dp") * lax.axis_size("rep")
    whole = total_pairs <= MOST_PAIRS

    image_vec = jnp.concatenate([img_gain_a, img_b_qv, img_gain_m, img_b_up])[None]
    image_vec_other = swap(image_vec, "rep", 1)
    weights = []
    for weight in (img_w_qkv, img_w_out, img_w_up, img_w_down):
        weights += [weight, swap(weight, "rep", 1)]

    text_vec = lax.optimization_barrier(jnp.concatenate([gain_attn, b_qv, gain_mlp, b_up]))
    text_vec = text_vec.astype(f32)[None]
    flat = captions.reshape(rows_total, D)
    qkv, mixed, after, mlp, slope, attention, early = text_forward(
        flat, cap_lengths, text_vec, w_qkv, w_out, w_up, w_down
    )
    early, image_vec_other, *weights = lax.optimization_barrier((early, image_vec_other, *weights))
    early_all = lax.all_gather(
        early if whole else early[:, :EARLY], ("dp", "rep"), axis=0, tiled=True
    )
    image_emb = image_tower(
        jnp.transpose(images, (1, 0, 2)), groups, mine_one, image_vec, image_vec_other, weights
    )
    image_all = gather_relative(image_emb)
    chip = lax.axis_index("dp").astype(jnp.int32)
    if whole:
        pair_loss, grads, branch, branch_all = loss_whole(
            early_all, image_all, text_proj, chip, mine, local_pairs
        )
    else:
        chips = chip ^ jnp.array(relative_chips(), jnp.int32)
        devices = jnp.concatenate([2 * chips + mine, 2 * chips + 1 - mine])
        image_ids = (
            devices[:, None] * local_pairs + jnp.arange(local_pairs, dtype=jnp.int32)[None, :]
        ).reshape(1, total_pairs)
        pair_loss, grads, branch, branch_all = loss_rows(
            early_all[:, :D],
            image_all,
            text_proj,
            early_all[:, D : D + 1].astype(f32),
            image_ids,
            (2 * chip + mine) * local_pairs,
            local_pairs,
        )
    place = chunk_places()
    grad_pre, up_own, up_other, grad_bup = up_backward(
        place, mine_one, cap_lengths, branch, slope, mlp, w_down
    )
    arrived = swap(up_other, "rep", 1)
    grad_after, grad_mixed, grad_gain = mlp_backward(
        cap_lengths, grad_pre, grads, after, text_vec, w_up, w_out
    )
    ups, rests = streams_of(FF // 4), streams_of(D)
    up_sent, up_kept = reduce_first(up_own, arrived, ups)
    (grad_mixed,) = behind([grad_mixed], up_sent)
    up_came = reduce_swaps(up_sent, ups, 1)
    caption_grad, rest_own, rest_other = rest_backward(
        place, mine_one, qkv, attention, mixed, grad_mixed, grad_after, flat, text_vec,
        grad_gain, grad_bup, w_qkv,
    )
    rest_other, *up_came = lax.optimization_barrier((rest_other, *up_came))
    arrived = swap(rest_other, "rep", 1)
    up_sent, up_kept = reduce_add(up_came, up_kept)
    up_came = reduce_swaps(up_sent, ups, 2)
    (arrived,) = behind([arrived], up_sent)
    rest_sent, rest_kept = reduce_first(rest_own, arrived, rests)
    rest_came = reduce_swaps(rest_sent, rests, 1)
    up_came = behind(up_came, rest_sent)
    up_sent, up_kept = reduce_join(up_came, up_kept)
    up_came = reduce_swaps_far(up_sent)
    (branch_all,) = behind([branch_all], up_sent)
    half = D // 2
    own_columns = lax.dynamic_slice_in_dim(branch_all, mine * half, half, 1)
    if whole:
        grad_w_down = dot_tn(early_all[:, EARLY:], own_columns)
    else:
        other_columns = lax.dynamic_slice_in_dim(branch_all, (1 - mine) * half, half, 1)
        grad_w_down = dot_tn(early[:, EARLY:], own_columns) + swap(
            dot_tn(early[:, EARLY:], other_columns).astype(bf16), "rep", 1
        ).astype(f32)
        grad_w_down = lax.psum(grad_w_down, "dp")
    rest_came = behind(rest_came, [grad_w_down])
    rest_sent, rest_kept = reduce_add(rest_came, rest_kept)
    rest_came = reduce_swaps(rest_sent, rests, 2)
    up_came = behind(up_came, rest_sent)
    up_chunk = reduce_last(up_came, up_kept)
    up_column = spread_first(up_chunk)
    rest_came = behind(rest_came, [up_chunk])
    rest_sent, rest_kept = reduce_join(rest_came, rest_kept)
    rest_came = reduce_swaps_far(rest_sent)
    up_column = behind(up_column, rest_sent)
    up_mine = spread_second(up_column, ups)
    up_near, up_across = spread_swaps(up_mine, ups, 2), spread_swaps(up_mine, ups, 1)
    rest_came = behind(rest_came, up_mine)
    rest_chunk = reduce_last(rest_came, rest_kept)
    rest_column = spread_first(rest_chunk)
    up_near = behind(up_near, [rest_chunk])
    up_last = spread_swaps(up_near, ups, 1)
    rest_column = behind(rest_column, up_near)
    rest_mine = spread_second(rest_column, rests)
    rest_near, rest_across = spread_swaps(rest_mine, rests, 2), spread_swaps(rest_mine, rests, 1)
    up_last = behind(up_last, rest_mine)
    grad_w_up = unpack_up(place, in_quarters(up_mine, up_near, up_across, up_last))
    rest_near = behind(rest_near, [grad_w_up])
    rest_last = spread_swaps(rest_near, rests, 1)
    grad_w_qkv, grad_w_out, *small = unpack_rest(
        place, in_quarters(rest_mine, rest_near, rest_across, rest_last)
    )
    return (
        pair_loss,
        caption_grad.reshape(local_pairs, CAP, D),
        small[0],
        grad_w_qkv,
        small[1],
        grad_w_out,
        small[2],
        grad_w_up,
        small[3],
        grad_w_down,
    )


def solution(mesh):
    in_specs = (
        P(("dp", "rep"), None, None),
        P(("dp", "rep")),
        P(("dp", "rep"), None, None),
        P(("dp", "rep")),
        P("rep"),
        P("rep", None),
        P("rep"),
        P("rep", None),
        P("rep"),
        P("rep", None),
        P("rep"),
        P("rep", None),
        P(),
        P(),
        P(),
        P(),
        P(),
        P(),
        P(),
        P(),
        P(),
    )
    out_specs = (
        P(("dp", "rep")),
        P(("dp", "rep"), None, None),
        P("rep"),
        P(None, "rep"),
        P("rep"),
        P(None, "rep"),
        P("rep"),
        P(None, "rep"),
        P("rep"),
        P(None, "rep"),
    )
    return jax.shard_map(local, mesh=mesh, in_specs=in_specs, out_specs=out_specs, check_vma=False)
```

```python
import functools
import math

import jax
import jax.numpy as jnp
from jax import lax
from jax.experimental import pallas as pl
from jax.experimental.pallas import tpu as pltpu
from jax.sharding import PartitionSpec as P

D = 768
HEADS = 12
FF = 3072
ILEN = 145
LOWLEN = 50
CAP = 16

SCALE = 100.0
EPS = 1e-06
NEGATIVE = -1e30
LOG2E = math.log2(math.e)
MOST_PAIRS = 2048

UNIT = 160
UNITS = 2
PART = 48
SPAN = 29
QB = 128
BW = 3 * D // 2 + D // 2 + 128
EARLY = D + 128
CHUNKS = 16

f32 = jnp.float32
bf16 = jnp.bfloat16


def dot(left_side, right_side):
    return jnp.dot(left_side, right_side, preferred_element_type=f32)


def dot_nt(left_side, right_side):
    return lax.dot_general(
        left_side, right_side, (((1,), (1,)), ((), ())), preferred_element_type=f32
    )


def dot_tn(left_side, right_side):
    return lax.dot_general(
        left_side, right_side, (((0,), (0,)), ((), ())), preferred_element_type=f32
    )


def normalize(values):
    center = values - jnp.mean(values, -1, keepdims=True)
    inverse = lax.rsqrt(jnp.mean(center * center, -1, keepdims=True) + EPS)
    return center * inverse, inverse


def norm_back(grad, normed, inverse):
    return inverse * (
        grad
        - jnp.mean(grad, -1, keepdims=True)
        - normed * jnp.mean(grad * normed, -1, keepdims=True)
    )


def normal_cdf(values):
    return 0.5 + 0.5 * lax.erf(values * (1.0 / math.sqrt(2.0)))


def split_low(values):
    big = values.astype(bf16)
    return big, (values - big.astype(f32)).astype(bf16)


def tower_kernel(
    groups_ref,
    mine_ref,
    x_hbm,
    vec_own_ref,
    vec_other_ref,
    qkv_own,
    qkv_other,
    out_own,
    out_other,
    up_own,
    up_other,
    down_own,
    down_other,
    emb_ref,
    order,
    x_ref,
    x_wide,
    wqkv,
    wout,
    wup,
    wdown,
    gain_a,
    bqkv,
    gain_m,
    bup,
    xs,
    qkv,
    mixed,
    asum,
    hsum,
    aparts,
    hparts,
    scores,
    attention,
    sems,
):
    total = x_ref.shape[1]
    pitch = total + 8
    mine = mine_ref[0]
    copies = []
    for k in range(ILEN // SPAN):
        span = pl.ds(k * SPAN, SPAN)
        copies.append(pltpu.make_async_copy(x_hbm.at[span], x_ref.at[span], sems.at[8 + k]))
    for k, (own, other, whole) in enumerate(
        (
            (qkv_own, qkv_other, wqkv),
            (out_own, out_other, wout),
            (up_own, up_other, wup),
            (down_own, down_other, wdown),
        )
    ):
        half = own.shape[0]
        copies.append(
            pltpu.make_async_copy(own, whole.at[pl.ds(mine * half, half)], sems.at[2 * k])
        )
        copies.append(
            pltpu.make_async_copy(
                other, whole.at[pl.ds((1 - mine) * half, half)], sems.at[2 * k + 1]
            )
        )
    for copy in copies:
        copy.start()

    vec_own = vec_own_ref[...].astype(f32)
    vec_other = vec_other_ref[...].astype(f32)
    low = jnp.where(mine == 0, vec_own, vec_other)
    high = jnp.where(mine == 0, vec_other, vec_own)
    start = 0
    for dest, size, at in (
        (gain_a, D // 2, (0, D // 2)),
        (bqkv, D, (0, 2 * D)),
        (gain_m, D // 2, (0, D // 2)),
        (bup, FF // 2, (0, FF // 2)),
    ):
        dest[:, at[0] : at[0] + size] = low[:, start : start + size]
        dest[:, at[1] : at[1] + size] = high[:, start : start + size]
        start += size
    bqkv[:, D : 2 * D] = jnp.zeros((1, D), f32)

    def count(i, found):
        return found + groups_ref[i]

    n_hi = lax.fori_loop(0, total, count, 0)

    def place_one(i, state):
        hi, lo = state
        group = groups_ref[i]
        order[jnp.where(group == 1, hi, lo)] = i
        return hi + group, lo + 1 - group

    lax.fori_loop(0, total, place_one, (0, n_hi))
    n_units = n_hi + (total - n_hi + 2) // 3

    xs[...] = jnp.zeros_like(xs)
    first = lax.broadcasted_iota(jnp.int32, (1, 128), 1) < 64
    key_at = lax.broadcasted_iota(jnp.int32, (UNIT, UNIT), 1)
    row_at = lax.broadcasted_iota(jnp.int32, (UNIT, UNIT), 0)
    sub = lax.broadcasted_iota(jnp.int32, (8, 1), 0)

    def place(unit, k):
        last = jnp.minimum(unit, n_units - 1)
        is_hi = last < n_hi
        where = jnp.where(is_hi, last, n_hi + 3 * (last - n_hi) + k)
        return order[jnp.minimum(where, total - 1)], is_hi

    def keep_parts(values, j, dest, col, width):
        rows = values.reshape(UNIT // 8, 8, width)
        parts = [
            jnp.sum(rows[0:6], 0),
            rows[6],
            jnp.sum(rows[7:12], 0),
            rows[12],
            jnp.sum(rows[13:18], 0),
            rows[18],
        ]
        for k, part in enumerate(parts):
            dest[j * PART + k * 8 : j * PART + k * 8 + 8, col : col + width] = part

    loads = copies[: ILEN // SPAN]
    copies = copies[ILEN // SPAN :]

    def widen(t, carry):
        for panel in range(D // 128):
            x_wide[panel, pl.ds(pl.multiple_of(t * pitch, 8), total), :] = x_ref[
                t, :, panel * 128 : (panel + 1) * 128
            ].astype(f32)
        return carry

    for k, load in enumerate(loads):
        load.wait()
        lax.fori_loop(k * SPAN, (k + 1) * SPAN, widen, 0)
    for copy in copies[:2]:
        copy.wait()

    def body(step, carry):
        for j in range(UNITS):
            unit = step * UNITS + j
            one, is_hi = place(unit, 0)
            two, three = place(unit, 1)[0], place(unit, 2)[0]
            base = j * UNIT

            @pl.when(is_hi)
            def _():
                for panel in range(D // 128):
                    xs[base : base + ILEN, panel * 128 : (panel + 1) * 128] = x_wide[
                        panel, pl.ds(one, ILEN, stride=pitch), :
                    ]

            @pl.when(jnp.logical_not(is_hi))
            def _():
                for k, index in enumerate((one, two, three)):
                    for panel in range(D // 128):
                        xs[
                            base + LOWLEN * k : base + LOWLEN * (k + 1),
                            panel * 128 : (panel + 1) * 128,
                        ] = x_wide[panel, pl.ds(index, LOWLEN, stride=pitch), :]

        low_rows = (normalize(xs[...])[0] * gain_a[...]).astype(bf16)
        for col in range(0, 3 * D, 256):
            values = dot(low_rows, wqkv[:, col : col + 256]) + bqkv[:, col : col + 256]
            if col < D:
                values = values * (LOG2E / 8.0)
            qkv[:, col : col + 256] = values.astype(bf16)

        @pl.when(step == 0)
        def _():
            for copy in copies[2:6]:
                copy.wait()

        for j in range(UNITS):
            is_hi = place(step * UNITS + j, 0)[1]
            base = j * UNIT
            key_seg = jnp.where(key_at < LOWLEN, 0, jnp.where(key_at < 2 * LOWLEN, 1, 2))
            row_seg = jnp.where(row_at < LOWLEN, 0, jnp.where(row_at < 2 * LOWLEN, 1, 2))
            short_ok = jnp.logical_and(key_seg == row_seg, key_at < 3 * LOWLEN)
            allowed = jnp.where(
                is_hi, (key_at < ILEN).astype(jnp.int32), short_ok.astype(jnp.int32)
            )
            bias = jnp.where(allowed > 0, 0.0, NEGATIVE)
            for p in range(HEADS // 2):
                query = qkv[base : base + UNIT, p * 128 : (p + 1) * 128]
                key = qkv[base : base + UNIT, D + p * 128 : D + (p + 1) * 128]
                for h in range(2):
                    head = first if h == 0 else jnp.logical_not(first)
                    at = (j * HEADS + 2 * p + h) * UNIT
                    scores[at : at + UNIT, :] = (
                        dot_nt(jnp.where(head, query, jnp.zeros_like(query)), key) + bias
                    )
        for j in range(UNITS):
            part = slice(j * HEADS * UNIT, (j + 1) * HEADS * UNIT)
            values = scores[part, :]
            powers = jnp.exp2(values - jnp.max(values, 1, keepdims=True))
            attention[part, :] = powers.astype(bf16)
        for j in range(UNITS):
            base = j * UNIT
            for p in range(HEADS // 2):
                lanes = slice(p * 128, (p + 1) * 128)
                value = qkv[base : base + UNIT, 2 * D + p * 128 : 2 * D + (p + 1) * 128]
                outs = []
                at = (j * HEADS + 2 * p) * UNIT
                value_one = jnp.concatenate([value, jnp.ones_like(value)], 1)
                for h in range(2):
                    summed = dot(attention[at + h * UNIT : at + (h + 1) * UNIT, :], value_one)
                    outs.append(summed[:, :128] / summed[:, 128:])
                mixed[base : base + UNIT, lanes] = jnp.where(first, outs[0], outs[1]).astype(bf16)
        for col in range(0, D, 256):
            xs[:, col : col + 256] += dot(mixed[...], wout[:, col : col + 256])
        for j in range(UNITS):
            keep_parts(xs[j * UNIT : (j + 1) * UNIT, :], j, aparts, 0, D)
        low_two = (normalize(xs[...])[0] * gain_m[...]).astype(bf16)
        width = 1024
        for col in range(0, FF, width):
            pre_act = dot(low_two, wup[:, col : col + width]) + bup[:, col : col + width]
            hidden = pre_act * normal_cdf(pre_act)
            for j in range(UNITS):
                keep_parts(hidden[j * UNIT : (j + 1) * UNIT], j, hparts, col, width)
        for j in range(UNITS):
            unit = step * UNITS + j
            one, is_hi = place(unit, 0)
            two, three = place(unit, 1)[0], place(unit, 2)[0]

            def rows_of(index):
                return pl.ds(pl.multiple_of(index * 8, 8), 8)

            @pl.when(is_hi)
            def _():
                for src, dest in ((aparts, asum), (hparts, hsum)):
                    part = [src[j * PART + k * 8 : j * PART + k * 8 + 8, :] for k in range(6)]
                    dest[rows_of(one), :] = (
                        (part[0] + part[1])
                        + (part[2] + part[3])
                        + (part[4] + jnp.where(sub < 1, part[5], 0.0))
                    )

            @pl.when(jnp.logical_not(is_hi))
            def _():
                for src, dest in ((aparts, asum), (hparts, hsum)):
                    part = [src[j * PART + k * 8 : j * PART + k * 8 + 8, :] for k in range(6)]
                    dest[rows_of(three), :] = (
                        jnp.where(sub < 4, 0.0, part[3])
                        + part[4]
                        + jnp.where(sub < 6, part[5], 0.0)
                    )
                    dest[rows_of(two), :] = (
                        jnp.where(sub < 2, 0.0, part[1])
                        + part[2]
                        + jnp.where(sub < 4, part[3], 0.0)
                    )
                    dest[rows_of(one), :] = part[0] + jnp.where(sub < 2, part[1], 0.0)

        return carry

    lax.fori_loop(0, (n_units + UNITS - 1) // UNITS, body, 0)
    for copy in copies[6:]:
        copy.wait()
    which = lax.broadcasted_iota(jnp.int32, (total, 128), 0)
    scale = jnp.zeros((total, 128), f32)
    for i in range(total):
        scale = jnp.where(
            which == i, jnp.where(groups_ref[i] == 1, 1.0 / ILEN, 1.0 / LOWLEN), scale
        )
    scale = scale[:, 0:1]
    big, rest = split_low(jnp.sum(hsum[...].reshape(total, 8, FF), 1) * scale)
    product = dot(jnp.concatenate([big, rest], 0), wdown[...])
    pooled = jnp.sum(asum[...].reshape(total, 8, D), 1) * scale + product[:total] + product[total:]
    emb_ref[...] = (
        pooled * lax.rsqrt(jnp.sum(pooled * pooled, -1, keepdims=True) + EPS)
    ).astype(bf16)


VM = pl.BlockSpec(memory_space=pltpu.VMEM)
SM = pl.BlockSpec(memory_space=pltpu.SMEM)
ANY = pl.BlockSpec(memory_space=pltpu.HBM)


def limit(mebibytes):
    return pltpu.CompilerParams(vmem_limit_bytes=mebibytes * 1024 * 1024)


def image_tower(images, groups, mine, vec_own, vec_other, weights):
    number = images.shape[1]
    rows = UNITS * UNIT
    flops = number * 100 * 2 * (4 * D * D + D * FF)
    return pl.pallas_call(
        tower_kernel,
        out_shape=jax.ShapeDtypeStruct((number, D), bf16),
        in_specs=[SM, SM, ANY, VM, VM] + [ANY] * 8,
        out_specs=VM,
        scratch_shapes=[
            pltpu.SMEM((number,), jnp.int32),
            pltpu.VMEM(images.shape, bf16),
            pltpu.VMEM((D // 128, ILEN * (number + 8), 128), f32),
            pltpu.VMEM((D, 3 * D), bf16),
            pltpu.VMEM((D, D), bf16),
            pltpu.VMEM((D, FF), bf16),
            pltpu.VMEM((FF, D), bf16),
            pltpu.VMEM((1, D), f32),
            pltpu.VMEM((1, 3 * D), f32),
            pltpu.VMEM((1, D), f32),
            pltpu.VMEM((1, FF), f32),
            pltpu.VMEM((rows, D), f32),
            pltpu.VMEM((rows, 3 * D), bf16),
            pltpu.VMEM((rows, D), bf16),
            pltpu.VMEM((number * 8, D), f32),
            pltpu.VMEM((number * 8, FF), f32),
            pltpu.VMEM((UNITS * PART, D), f32),
            pltpu.VMEM((UNITS * PART, FF), f32),
            pltpu.VMEM((UNITS * HEADS * UNIT, UNIT), f32),
            pltpu.VMEM((UNITS * HEADS * UNIT, UNIT), bf16),
            pltpu.SemaphoreType.DMA((8 + ILEN // SPAN,)),
        ],
        compiler_params=limit(62),
        cost_estimate=pl.CostEstimate(
            flops=flops, bytes_accessed=24 * 1024 * 1024, transcendentals=0
        ),
        name="image_tower",
    )(groups, mine, images, vec_own, vec_other, *weights)


def lens_along(lens_ref, start, number):
    owner = lax.broadcasted_iota(jnp.int32, (1, number * CAP), 1) // CAP
    lens = jnp.zeros((1, number * CAP), jnp.int32)
    for c in range(number):
        lens = jnp.where(owner == c, lens_ref[start + c], lens)
    return lens


def score_bias(lens_ref, block):
    per = QB // CAP
    position = lax.broadcasted_iota(jnp.int32, (1, QB), 1) % CAP
    valid = position < lens_along(lens_ref, block * per, per)
    rows = lax.broadcasted_iota(jnp.int32, (QB, QB), 0) // CAP
    columns = lax.broadcasted_iota(jnp.int32, (QB, QB), 1) // CAP
    return jnp.where(jnp.logical_and(rows == columns, valid), 0.0, NEGATIVE)


def forward_kernel(
    lens_ref,
    x_ref,
    vec_ref,
    wqkv_ref,
    wout_ref,
    wup_ref,
    wdown_ref,
    qkv,
    mixed,
    after,
    mlp,
    slope,
    attention,
    early,
    hidden,
    scores,
):
    rows = x_ref.shape[0]
    number = rows // CAP
    first = lax.broadcasted_iota(jnp.int32, (1, 128), 1) < 64
    normed, _ = normalize(x_ref[...].astype(f32))
    low = (normed * vec_ref[:, 0:D]).astype(bf16)
    for col in range(0, 3 * D, 256):
        values = dot(low, wqkv_ref[:, col : col + 256])
        if col < D:
            values = values + vec_ref[:, D + col : D + col + 256]
        if col >= 2 * D:
            values = values + vec_ref[:, col : col + 256]
        values = values.astype(bf16)
        if col < D:
            values = values * jnp.asarray(0.125, bf16)
        qkv[:, col : col + 256] = values
    for block in range(rows // QB):
        bias = score_bias(lens_ref, block)
        span = slice(block * QB, (block + 1) * QB)
        for p in range(HEADS // 2):
            query = qkv[span, p * 128 : (p + 1) * 128]
            key = qkv[span, D + p * 128 : D + (p + 1) * 128]
            for h in range(2):
                head = first if h == 0 else jnp.logical_not(first)
                at = (block * HEADS + 2 * p + h) * QB
                scores[at : at + QB, :] = (
                    dot_nt(jnp.where(head, query, jnp.zeros_like(query)), key) * LOG2E + bias
                )
    for block in range(rows // QB):
        part = slice(block * HEADS * QB, (block + 1) * HEADS * QB)
        values = scores[part, :]
        powers = jnp.exp2(values - jnp.max(values, 1, keepdims=True))
        attention[part, :] = (powers * (1.0 / jnp.sum(powers, 1, keepdims=True))).astype(bf16)
    for block in range(rows // QB):
        span = slice(block * QB, (block + 1) * QB)
        for p in range(HEADS // 2):
            value = qkv[span, 2 * D + p * 128 : 2 * D + (p + 1) * 128]
            at = (block * HEADS + 2 * p) * QB
            outs = [dot(attention[at + h * QB : at + (h + 1) * QB, :], value) for h in range(2)]
            mixed[span, p * 128 : (p + 1) * 128] = jnp.where(first, outs[0], outs[1]).astype(bf16)
    for col in range(0, D, 256):
        after[:, col : col + 256] = x_ref[:, col : col + 256].astype(f32) + dot(
            mixed[...], wout_ref[:, col : col + 256]
        )
    mlp[...] = (normalize(after[...])[0] * vec_ref[:, 3 * D : 4 * D]).astype(bf16)
    lens = lens_along(lens_ref, 0, number)
    position = lax.broadcasted_iota(jnp.int32, (1, rows), 1)
    owner = (
        lax.broadcasted_iota(jnp.int32, (number, rows), 0)
        == lax.broadcasted_iota(jnp.int32, (number, rows), 1) // CAP
    )
    members = jnp.where(jnp.logical_and(owner, position % CAP < lens), 1.0, 0.0)
    pool = members.astype(bf16)
    count = jnp.sum(members, 1, keepdims=True)
    width = 512
    for col in range(0, FF, width):
        span = slice(col, col + width)
        pre_act = dot(mlp[...], wup_ref[:, span]) + vec_ref[:, 4 * D + col : 4 * D + col + width]
        phi = normal_cdf(pre_act)
        hidden[:, span] = (pre_act * phi).astype(bf16)
        density = jnp.exp2(pre_act * pre_act * (-0.5 * LOG2E)) * (1.0 / math.sqrt(2.0 * math.pi))
        slope[:, span] = (phi + pre_act * density).astype(bf16)
    big, rest = split_low(dot(pool, hidden[...]))
    after_big, after_rest = split_low(after[...])
    pooled = (
        dot(pool, after_big)
        + dot(pool, after_rest)
        + dot(big, wdown_ref[...])
        + dot(rest, wdown_ref[...])
    )
    early[:, 0:D] = (pooled / count).astype(bf16)
    early[:, D:EARLY] = jnp.broadcast_to(count, (number, EARLY - D)).astype(bf16)
    early[:, EARLY:] = big


def text_forward(captions, lens, vec, w_qkv, w_out, w_up, w_down):
    rows = captions.shape[0]
    shape = jax.ShapeDtypeStruct
    return pl.pallas_call(
        forward_kernel,
        out_shape=[
            shape((rows, 3 * D), bf16),
            shape((rows, D), bf16),
            shape((rows, D), f32),
            shape((rows, D), bf16),
            shape((rows, FF), bf16),
            shape((rows * HEADS, QB), bf16),
            shape((rows // CAP, EARLY + FF), bf16),
        ],
        in_specs=[SM] + [VM] * 6,
        out_specs=[VM] * 7,
        scratch_shapes=[pltpu.VMEM((rows, FF), bf16), pltpu.VMEM((rows * HEADS, QB), f32)],
        compiler_params=limit(60),
        cost_estimate=pl.CostEstimate(
            flops=2 * rows * (4 * D * D + 2 * D * FF),
            bytes_accessed=24 * 1024 * 1024,
            transcendentals=0,
        ),
        name="text_forward",
    )(lens, captions, vec, w_qkv, w_out, w_up, w_down)


def put_chunks(dest, values, place_ref, stream, col):
    rows = values.shape[0] // CHUNKS
    for chunk in range(CHUNKS):
        at = pl.multiple_of(place_ref[stream, chunk] * rows, 16)
        dest[pl.ds(at, rows), col : col + values.shape[1]] = values[
            chunk * rows : (chunk + 1) * rows
        ].astype(dest.dtype)


def up_kernel(
    place_ref, mine_ref, lens_ref, branch_ref, slope_ref, mlp_ref, wdown_ref,
    grad_pre, own, other, grad_bup, grad_hidden, mlp_t,
):
    number = slope_ref.shape[0] // CAP
    half = FF // 2
    mine = mine_ref[0]
    for col in range(0, FF, 512):
        grad_hidden[:, col : col + 512] = dot_nt(branch_ref[...], wdown_ref[col : col + 512, :])
    position = lax.broadcasted_iota(jnp.int32, (CAP, 1), 0)
    for c in range(number):
        span = slice(c * CAP, (c + 1) * CAP)
        keep = jnp.where(position < lens_ref[c], 1.0, 0.0)
        grad_pre[span, :] = (
            grad_hidden[c : c + 1, :] * slope_ref[span, :].astype(f32) * keep
        ).astype(bf16)
    mlp_t[...] = mlp_ref[...].T
    for which, dest in ((1 - mine, other), (mine, own)):
        for col in range(0, half, 384):
            lanes = pl.ds(pl.multiple_of(which * half + col, 128), 384)
            put_chunks(dest, dot(mlp_t[...], grad_pre[:, lanes]), place_ref, 2 * col // half, col)
    for col in range(0, FF, 512):
        grad_bup[:, col : col + 512] = jnp.sum(
            grad_pre[:, col : col + 512].astype(f32), 0, keepdims=True
        )


def up_backward(place, mine, lens, branch, slope, mlp, w_down):
    rows = slope.shape[0]
    shape = jax.ShapeDtypeStruct
    return pl.pallas_call(
        up_kernel,
        out_shape=[
            shape((rows, FF), bf16),
            shape((D, FF // 2), f32),
            shape((D, FF // 2), bf16),
            shape((1, FF), f32),
        ],
        in_specs=[SM, SM, SM] + [VM] * 4,
        out_specs=[VM] * 4,
        scratch_shapes=[pltpu.VMEM((rows // CAP, FF), f32), pltpu.VMEM((D, rows), bf16)],
        compiler_params=limit(24),
        cost_estimate=pl.CostEstimate(
            flops=2 * rows * D * FF, bytes_accessed=20 * 1024 * 1024, transcendentals=0
        ),
        name="up_backward",
    )(place, mine, lens, branch, slope, mlp, w_down)


def mlp_kernel(
    lens_ref, pre_ref, grad_ref, after_ref, vec_ref, wup_ref, wout_ref,
    grad_after, grad_mixed, grad_gain, grad_out,
):
    number = after_ref.shape[0] // CAP
    grad_mlp = dot_nt(pre_ref[...], wup_ref[...])
    normed_two, inverse_two = normalize(after_ref[...])
    grad_gain[...] = jnp.sum(grad_mlp * normed_two, 0, keepdims=True)
    grad_after[...] = norm_back(grad_mlp * vec_ref[:, 3 * D : 4 * D], normed_two, inverse_two)
    position = lax.broadcasted_iota(jnp.int32, (CAP, 1), 0)
    for c in range(number):
        keep = jnp.where(position < lens_ref[c], 1.0, 0.0)
        grad_after[c * CAP : (c + 1) * CAP, :] += grad_ref[c : c + 1, :] * keep
    grad_out[...] = grad_after[...].astype(bf16)
    for col in range(0, D, 256):
        grad_mixed[:, col : col + 256] = dot_nt(
            grad_out[...], wout_ref[col : col + 256, :]
        ).astype(bf16)


def mlp_backward(lens, grad_pre, grads, after, vec, w_up, w_out):
    rows = after.shape[0]
    shape = jax.ShapeDtypeStruct
    return pl.pallas_call(
        mlp_kernel,
        out_shape=[shape((rows, D), f32), shape((rows, D), bf16), shape((1, D), f32)],
        in_specs=[SM] + [VM] * 6,
        out_specs=[VM] * 3,
        scratch_shapes=[pltpu.VMEM((rows, D), bf16)],
        compiler_params=limit(28),
        cost_estimate=pl.CostEstimate(
            flops=2 * rows * (D * D + D * FF), bytes_accessed=20 * 1024 * 1024, transcendentals=0
        ),
        name="mlp_backward",
    )(lens, grad_pre, grads, after, vec, w_up, w_out)


def attention_kernel(
    qkv_ref, att_ref, mixed_ref, grad_ref, grad_proj, grad_att, means, grad_s, *, start
):
    first = lax.broadcasted_iota(jnp.int32, (1, 128), 1) < 64
    ones = jnp.ones((128, QB), bf16)
    heads = (first, jnp.logical_not(first))
    blocks = grad_proj.shape[0] // QB
    for block in range(blocks):
        span = slice(start + block * QB, start + (block + 1) * QB)
        for p in range(HEADS // 2):
            at = p * 128
            value = qkv_ref[span, 2 * D + at : 2 * D + at + 128]
            grad = grad_ref[span, at : at + 128]
            product = (grad.astype(f32) * mixed_ref[span, at : at + 128].astype(f32)).astype(bf16)
            for h, head in enumerate(heads):
                to = (block * HEADS + 2 * p + h) * QB
                grad_att[to : to + QB, :] = dot_nt(
                    jnp.where(head, grad, jnp.zeros_like(grad)), value
                )
                means[to : to + QB, :] = dot(
                    jnp.where(head, product, jnp.zeros_like(product)), ones
                )
    for block in range(blocks):
        part = slice(block * HEADS * QB, (block + 1) * HEADS * QB)
        place = (start // QB + block) * HEADS * QB
        low = att_ref[place : place + HEADS * QB, :].astype(f32)
        grad_s[part, :] = (low * (grad_att[part, :] - means[part, :])).astype(bf16)
    for block in range(blocks):
        span = slice(start + block * QB, start + (block + 1) * QB)
        dest = slice(block * QB, (block + 1) * QB)
        for p in range(HEADS // 2):
            at = p * 128
            query = qkv_ref[span, at : at + 128]
            key = qkv_ref[span, D + at : D + at + 128]
            grad = grad_ref[span, at : at + 128]
            grad_q, grad_k, grad_v = [], [], []
            for h in range(2):
                to = (block * HEADS + 2 * p + h) * QB
                place = ((start // QB + block) * HEADS + 2 * p + h) * QB
                sgrad = grad_s[to : to + QB, :]
                grad_q.append(dot(sgrad, key))
                grad_k.append(dot_tn(sgrad, query))
                grad_v.append(dot_tn(att_ref[place : place + QB, :], grad))
            for k, (parts, scale) in enumerate(((grad_q, 0.125), (grad_k, 1.0), (grad_v, 1.0))):
                grad_proj[dest, k * D + at : k * D + at + 128] = (
                    jnp.where(first, parts[0], parts[1]) * scale
                ).astype(bf16)


def input_kernel(
    proj_ref, after_ref, x_ref, vec_ref, gain_ref, bup_ref, wqkv_ref, caption_grad, sums, input_low
):
    gain_a = vec_ref[:, 0:D]
    normed_one, inverse_one = normalize(x_ref[...].astype(f32))
    input_low[...] = (normed_one * gain_a).astype(bf16)
    grad_in = dot_nt(proj_ref[...], wqkv_ref[...])
    sums[:, 0:D] = jnp.sum(grad_in * normed_one, 0, keepdims=True)
    sums[:, D : 2 * D] = jnp.sum(proj_ref[:, 0:D].astype(f32), 0, keepdims=True)
    sums[:, 2 * D : 3 * D] = jnp.sum(proj_ref[:, 2 * D :].astype(f32), 0, keepdims=True)
    sums[:, 3 * D : 4 * D] = gain_ref[...]
    sums[:, 4 * D :] = bup_ref[...]
    caption_grad[...] = after_ref[...] + norm_back(grad_in * gain_a, normed_one, inverse_one)


def proj_kernel(
    place_ref, mine_ref, proj_ref, after_ref, mixed_ref, input_ref, sums, own, other, lhs_t, grad_out
):
    chunk_rows = D // CHUNKS
    mine = mine_ref[0]
    lhs_t[...] = input_ref[...].T
    half_out, half_qkv = D // 2, 3 * D // 2
    for which, dest in ((1 - mine, other), (mine, own)):
        for col in range(0, half_qkv, 384):
            lanes = pl.ds(pl.multiple_of(which * half_qkv + col, 128), 384)
            put_chunks(dest, dot(lhs_t[...], proj_ref[:, lanes]), place_ref, col // 768, col)
    lhs_t[...] = mixed_ref[...].T
    grad_out[...] = after_ref[...].astype(bf16)
    for which, dest in ((1 - mine, other), (mine, own)):
        lanes = pl.ds(pl.multiple_of(which * half_out, 128), half_out)
        put_chunks(dest, dot(lhs_t[...], grad_out[:, lanes]), place_ref, 1, half_qkv)
    for which, dest in ((1 - mine, other), (mine, own)):
        dest[:, BW - 128 :] = jnp.zeros((D, 128), dest.dtype)
        pieces = []
        for start, size in ((0, D), (D, 2 * D), (3 * D, D), (4 * D, FF)):
            for k in range(0, size // 2, 128):
                at = pl.multiple_of(start + which * (size // 2) + k, 128)
                pieces.append(sums[:, pl.ds(at, 128)])
        pieces += [jnp.zeros_like(pieces[0])] * (32 - len(pieces))
        at = pl.multiple_of(place_ref[1, 0] * chunk_rows, 16)
        dest[pl.ds(at, 32), BW - 128 :] = jnp.concatenate(pieces, 0).astype(dest.dtype)


def rest_kernel(
    place_ref, mine_ref, qkv_ref, att_ref, mixed_ref, grad_ref, after_ref, x_ref, vec_ref,
    gain_ref, bup_ref, wqkv_ref, caption_grad, own, other,
    grad_proj, sums, input_low, grad_att, means, grad_s, lhs_t, grad_out,
):
    attention_kernel(
        qkv_ref, att_ref, mixed_ref, grad_ref, grad_proj, grad_att, means, grad_s, start=0
    )
    input_kernel(
        grad_proj, after_ref, x_ref, vec_ref, gain_ref, bup_ref, wqkv_ref,
        caption_grad, sums, input_low,
    )
    proj_kernel(
        place_ref, mine_ref, grad_proj, after_ref, mixed_ref, input_low, sums,
        own, other, lhs_t, grad_out,
    )


def rest_backward(
    place, mine, qkv, attention, mixed, grad_mixed, grad_after, captions, vec, grad_gain, grad_bup, w_qkv
):
    rows = captions.shape[0]
    shape = jax.ShapeDtypeStruct
    return pl.pallas_call(
        rest_kernel,
        out_shape=[shape((rows, D), f32), shape((D, BW), f32), shape((D, BW), bf16)],
        in_specs=[SM, SM] + [VM] * 10,
        out_specs=[VM] * 3,
        scratch_shapes=[
            pltpu.VMEM((rows, 3 * D), bf16),
            pltpu.VMEM((1, 4 * D + FF), f32),
            pltpu.VMEM((rows, D), bf16),
            pltpu.VMEM((rows * HEADS, QB), f32),
            pltpu.VMEM((rows * HEADS, QB), f32),
            pltpu.VMEM((rows * HEADS, QB), bf16),
            pltpu.VMEM((D, rows), bf16),
            pltpu.VMEM((rows, D), bf16),
        ],
        compiler_params=limit(44),
        cost_estimate=pl.CostEstimate(
            flops=2 * rows * 48 * D * D, bytes_accessed=60 * 1024 * 1024, transcendentals=0
        ),
        name="rest_backward",
    )(
        place, mine, qkv, attention, mixed, grad_mixed, grad_after, captions, vec,
        grad_gain, grad_bup, w_qkv,
    )


def dp_bits():
    bits, bit = [], 1
    while bit < lax.axis_size("dp"):
        bits.append(bit)
        bit *= 2
    return bits


def swap(values, axis, bit):
    size = lax.axis_size(axis)
    return lax.ppermute(values, axis, [(place, place ^ bit) for place in range(size)])


def gather_relative(values):
    bits = dp_bits()
    while bits:
        pair = bits[-2:]
        bits = bits[:-2]
        offsets = [0]
        for bit in pair:
            offsets += [entry + bit for entry in offsets]
        values = jnp.concatenate([swap(values, "dp", k) if k else values for k in offsets], 0)
    return jnp.concatenate([values, swap(values, "rep", 1)], 0)


def relative_chips():
    bits, table = dp_bits(), [0]
    while bits:
        pair = bits[-2:]
        bits = bits[:-2]
        offsets = [0]
        for bit in pair:
            offsets += [entry + bit for entry in offsets]
        table = [entry ^ k for k in offsets for entry in table]
    return table


def chunk_places():
    away = jnp.arange(CHUNKS, dtype=jnp.int32) ^ (lax.axis_index("dp") % CHUNKS)
    one, two, rest = away % 2, away // 2 % 2, away // 4
    return jnp.stack([one * 8 + two * 4 + rest, two * 8 + one * 4 + rest]).astype(jnp.int32)


def streams_of(width):
    return ((slice(0, width), 1, 2), (slice(width, None), 2, 1))


def reduce_first(own, arrived, streams):
    half = own.shape[0] // 2

    def both(rows, lanes):
        return own[rows, lanes] + arrived[rows, lanes].astype(f32)

    sent = [both(slice(half, None), lanes).astype(bf16) for lanes, _, _ in streams]
    return sent, [both(slice(0, half), lanes) for lanes, _, _ in streams]


def reduce_swaps(sent, streams, stage):
    return [swap(piece, "dp", stream[stage]) for piece, stream in zip(sent, streams)]


def reduce_add(came, kept):
    half = kept[0].shape[0] // 2
    totals = [total + got.astype(f32) for total, got in zip(kept, came)]
    return [total[half:].astype(bf16) for total in totals], [total[:half] for total in totals]


def reduce_join(came, kept):
    total = jnp.concatenate([total + got.astype(f32) for total, got in zip(kept, came)], 1)
    rows = total.shape[0] // 4
    return [total[k * rows : (k + 1) * rows].astype(bf16) for k in (1, 2, 3)], total[:rows]


def reduce_last(parts, total):
    total = total + sum(part.astype(f32) for part in parts)
    for bit in dp_bits()[4:]:
        total = total + swap(total.astype(bf16), "dp", bit).astype(f32)
    return total.astype(bf16)


def spread_first(chunk):
    return [swap(chunk, "dp", 4 * k) if k else chunk for k in range(4)]


def spread_second(column, streams):
    return [jnp.concatenate([piece[:, lanes] for piece in column], 0) for lanes, _, _ in streams]


def spread_swaps(pieces, streams, stage):
    return [swap(piece, "dp", stream[stage]) for piece, stream in zip(pieces, streams)]


def reduce_swaps_far(sent):
    return [swap(piece, "dp", 4 * (k + 1)) for k, piece in enumerate(sent)]


def in_quarters(*quarters):
    return [quarter[stream] for stream in range(2) for quarter in quarters]


def behind(values, others):
    return list(lax.optimization_barrier((*values, *others))[: len(values)])


def each_chunk(place_ref):
    rows = D // CHUNKS
    place = place_ref[0, 0]
    me = place // 8 + 2 * (place // 4 % 2) + 4 * (place % 4)
    for stream in range(2):
        for quarter in range(4):
            for k in range(4):
                high, low = quarter // 2, quarter % 2
                away = (high + 2 * low if stream == 0 else low + 2 * high) + 4 * k
                chunk = me ^ away
                at = pl.ds(pl.multiple_of(chunk * rows, 16), rows)
                yield stream, stream * 4 + quarter, slice(k * rows, (k + 1) * rows), chunk, at


def unpack_up_kernel(place_ref, *refs):
    parts, g_up = refs[:8], refs[8]
    for stream, part, span, _, at in each_chunk(place_ref):
        lanes = slice(stream * FF // 4, (stream + 1) * FF // 4)
        g_up[at, lanes] = parts[part][span, :].astype(f32)


def unpack_rest_kernel(place_ref, *refs):
    parts, (g_qkv, g_out), vectors = refs[:8], refs[8:10], refs[10:]
    for stream, part, span, chunk, at in each_chunk(place_ref):
        rest = parts[part][span, :].astype(f32)
        if stream == 0:
            g_qkv[at, 0:D] = rest
            continue
        g_qkv[at, D:] = rest[:, : D // 2]
        g_out[at, :] = rest[:, D // 2 : D]

        @pl.when(chunk == 0)
        def _():
            row = 0
            for dest in vectors:
                for lane in range(0, dest.shape[0], 128):
                    dest[lane : lane + 128] = rest[row, D:]
                    row += 1


def unpack_up(place, parts):
    return pl.pallas_call(
        unpack_up_kernel,
        out_shape=jax.ShapeDtypeStruct((D, FF // 2), f32),
        in_specs=[SM] + [VM] * 8,
        out_specs=VM,
        compiler_params=limit(20),
        name="unpack_up",
    )(place, *parts)


def unpack_rest(place, parts):
    shape = jax.ShapeDtypeStruct
    return pl.pallas_call(
        unpack_rest_kernel,
        out_shape=[
            shape((D, 3 * D // 2), f32),
            shape((D, D // 2), f32),
            shape((D // 2,), f32),
            shape((D,), f32),
            shape((D // 2,), f32),
            shape((FF // 2,), f32),
        ],
        in_specs=[SM] + [VM] * 8,
        out_specs=[VM] * 6,
        compiler_params=limit(20),
        name="unpack_rest",
    )(place, *parts)


def softmax_parts(scores, axis):
    maxima = jnp.max(scores, axis, keepdims=True)
    powers = jnp.exp(scores - maxima)
    totals = jnp.sum(powers, axis, keepdims=True)
    return powers / totals, maxima + jnp.log(totals)


def text_unit(pooled_low, text_proj):
    proj_out = dot(pooled_low, text_proj)
    inverse_z = lax.rsqrt(jnp.sum(proj_out * proj_out, -1, keepdims=True) + EPS)
    return proj_out * inverse_z, inverse_z


def branch_grad(grad_unit, unit_text, inverse_z, text_proj, lengths):
    grad_projout = (
        inverse_z * (grad_unit - unit_text * jnp.sum(unit_text * grad_unit, -1, keepdims=True))
    ).astype(bf16)
    return dot_nt(grad_projout, text_proj) / lengths


def loss_kernel(
    where_ref, early_ref, image_ref, proj_ref, pair_loss, own_grads, own_branch, branch,
    unit, inverse, scores, sgrad,
):
    total = image_ref.shape[0]
    number = own_grads.shape[0]
    chip, mine = where_ref[0], where_ref[1]
    block = 256
    for row in range(0, total, block):
        span = slice(row, row + block)
        proj_out = dot(early_ref[span, 0:D], proj_ref[...])
        inverse_z = lax.rsqrt(jnp.sum(proj_out * proj_out, -1, keepdims=True) + EPS)
        inverse[span, :] = jnp.broadcast_to(inverse_z, (block, 128))
        unit[span, :] = proj_out * inverse_z
        scores[span, :] = dot_nt(unit[span, :].astype(bf16), image_ref[...]) * SCALE
    place = lax.broadcasted_iota(jnp.int32, (1, total), 1) // number
    chips = total // (2 * number)
    away = place % chips
    other = place // chips
    from_chip = chip ^ (away // 4 + 4 * (away % 4)) if chips == 16 else None
    image_id = (from_chip * 2 + (mine ^ other)) * number + (
        lax.broadcasted_iota(jnp.int32, (1, total), 1) % number
    )
    column_max = jnp.max(scores[...], 0, keepdims=True)
    column_sum = jnp.zeros((1, total), f32)
    for row in range(0, total, block):
        column_sum += jnp.sum(
            jnp.exp(scores[row : row + block, :] - column_max), 0, keepdims=True
        )
    column_total = column_max + jnp.log(column_sum)
    for row in range(0, total, block):
        span = slice(row, row + block)
        values = scores[span, :]
        row_max = jnp.max(values, 1, keepdims=True)
        powers = jnp.exp(values - row_max)
        by_text = powers * (0.5 / jnp.sum(powers, 1, keepdims=True))
        by_image = jnp.exp(values - column_max) * (0.5 / column_sum)
        text_id = lax.broadcasted_iota(jnp.int32, (block, 1), 0) + row
        same = jnp.where(text_id == image_id, 1.0, 0.0)
        sgrad[span, :] = (by_text + by_image - same).astype(bf16)
        grad_unit = dot(sgrad[span, :], image_ref[...]) * SCALE
        unit_text = unit[span, :]
        grad_proj = (
            inverse[span, 0:1]
            * (grad_unit - unit_text * jnp.sum(unit_text * grad_unit, -1, keepdims=True))
        ).astype(bf16)
        unit[span, :] = dot_nt(grad_proj, proj_ref[...]) / early_ref[span, D : D + 1].astype(f32)
        branch[span, :] = unit[span, :].astype(bf16)
    first = pl.multiple_of((chip * 2 + mine) * number, 32)
    own_grads[...] = unit[pl.ds(first, number), :]
    own_branch[...] = unit[pl.ds(first, number), :].astype(bf16)
    values = scores[pl.ds(first, number), :]
    row_max = jnp.max(values, 1, keepdims=True)
    row_total = row_max + jnp.log(jnp.sum(jnp.exp(values - row_max), 1, keepdims=True))
    text_id = lax.broadcasted_iota(jnp.int32, (number, 1), 0) + first
    same = jnp.where(text_id == image_id, 1.0, 0.0)
    both = 0.5 * (row_total + column_total) - values
    pair_loss[...] = jnp.broadcast_to(jnp.sum(both * same, 1, keepdims=True), (number, 128))


def loss_whole(early_all, image_all, text_proj, chip, mine, number):
    total = image_all.shape[0]
    shape = jax.ShapeDtypeStruct
    pair_loss, grads, own_branch, branch = pl.pallas_call(
        loss_kernel,
        out_shape=[
            shape((number, 128), f32),
            shape((number, D), f32),
            shape((number, D), bf16),
            shape((total, D), bf16),
        ],
        in_specs=[SM] + [VM] * 3,
        out_specs=[VM] * 4,
        scratch_shapes=[
            pltpu.VMEM((total, D), f32),
            pltpu.VMEM((total, 128), f32),
            pltpu.VMEM((total, total), f32),
            pltpu.VMEM((total, total), bf16),
        ],
        compiler_params=limit(26),
        name="pair_loss",
    )(jnp.stack([chip, mine]), early_all[:, :EARLY], image_all, text_proj)
    return pair_loss[:, 0], grads, own_branch, branch


def loss_rows(pooled_all, image_all, text_proj, lengths_all, image_ids, first_row, local_pairs):
    unit_all, inverse_all = text_unit(pooled_all, text_proj)

    def own_rows(values):
        return lax.dynamic_slice_in_dim(values, first_row, local_pairs, 0)

    unit_text, inverse_z = own_rows(unit_all), own_rows(inverse_all)
    text_scores = dot_nt(unit_text.astype(bf16), image_all) * SCALE
    image_scores = dot_nt(image_all[:local_pairs], unit_all.astype(bf16)) * SCALE
    by_text, text_total = softmax_parts(text_scores, 1)
    image_total = softmax_parts(image_scores, 1)[1]
    every_total = gather_relative(image_total)
    text_ids = first_row + jnp.arange(local_pairs, dtype=jnp.int32)
    own_same = (text_ids[:, None] == image_ids).astype(f32)
    own = jnp.sum(text_scores * own_same, -1)
    pair_loss = 0.5 * (text_total[:, 0] - own) + 0.5 * (image_total[:, 0] - own)
    by_image = jnp.exp(text_scores - every_total[:, 0][None, :])
    sgrad = (0.5 * (by_text - own_same) + 0.5 * (by_image - own_same)).astype(bf16)
    grad_unit = dot(sgrad, image_all) * SCALE
    grads = branch_grad(grad_unit, unit_text, inverse_z, text_proj, own_rows(lengths_all))
    return pair_loss, grads, grads.astype(bf16), grads.astype(bf16)


def local(
    images,
    groups,
    captions,
    cap_lengths,
    img_gain_a,
    img_w_qkv,
    img_b_qv,
    img_w_out,
    img_gain_m,
    img_w_up,
    img_b_up,
    img_w_down,
    gain_attn,
    w_qkv,
    b_qv,
    w_out,
    gain_mlp,
    w_up,
    b_up,
    w_down,
    text_proj,
):
    local_pairs = images.shape[0]
    rows_total = local_pairs * CAP
    mine = lax.axis_index("rep").astype(jnp.int32)
    mine_one = mine[None]
    total_pairs = local_pairs * lax.axis_size("dp") * lax.axis_size("rep")
    whole = total_pairs <= MOST_PAIRS

    image_vec = jnp.concatenate([img_gain_a, img_b_qv, img_gain_m, img_b_up])[None]
    image_vec_other = swap(image_vec, "rep", 1)
    weights = []
    for weight in (img_w_qkv, img_w_out, img_w_up, img_w_down):
        weights += [weight, swap(weight, "rep", 1)]

    text_vec = lax.optimization_barrier(jnp.concatenate([gain_attn, b_qv, gain_mlp, b_up]))
    text_vec = text_vec.astype(f32)[None]
    flat = captions.reshape(rows_total, D)
    qkv, mixed, after, mlp, slope, attention, early = text_forward(
        flat, cap_lengths, text_vec, w_qkv, w_out, w_up, w_down
    )
    early, image_vec_other, *weights = lax.optimization_barrier((early, image_vec_other, *weights))
    early_all = lax.all_gather(
        early if whole else early[:, :EARLY], ("dp", "rep"), axis=0, tiled=True
    )
    image_emb = image_tower(
        jnp.transpose(images, (1, 0, 2)), groups, mine_one, image_vec, image_vec_other, weights
    )
    image_all = gather_relative(image_emb)
    chip = lax.axis_index("dp").astype(jnp.int32)
    if whole:
        pair_loss, grads, branch, branch_all = loss_whole(
            early_all, image_all, text_proj, chip, mine, local_pairs
        )
    else:
        chips = chip ^ jnp.array(relative_chips(), jnp.int32)
        devices = jnp.concatenate([2 * chips + mine, 2 * chips + 1 - mine])
        image_ids = (
            devices[:, None] * local_pairs + jnp.arange(local_pairs, dtype=jnp.int32)[None, :]
        ).reshape(1, total_pairs)
        pair_loss, grads, branch, branch_all = loss_rows(
            early_all[:, :D],
            image_all,
            text_proj,
            early_all[:, D : D + 1].astype(f32),
            image_ids,
            (2 * chip + mine) * local_pairs,
            local_pairs,
        )
    place = chunk_places()
    grad_pre, up_own, up_other, grad_bup = up_backward(
        place, mine_one, cap_lengths, branch, slope, mlp, w_down
    )
    arrived = swap(up_other, "rep", 1)
    grad_after, grad_mixed, grad_gain = mlp_backward(
        cap_lengths, grad_pre, grads, after, text_vec, w_up, w_out
    )
    ups, rests = streams_of(FF // 4), streams_of(D)
    up_sent, up_kept = reduce_first(up_own, arrived, ups)
    (grad_mixed,) = behind([grad_mixed], up_sent)
    up_came = reduce_swaps(up_sent, ups, 1)
    caption_grad, rest_own, rest_other = rest_backward(
        place, mine_one, qkv, attention, mixed, grad_mixed, grad_after, flat, text_vec,
        grad_gain, grad_bup, w_qkv,
    )
    rest_other, *up_came = lax.optimization_barrier((rest_other, *up_came))
    arrived = swap(rest_other, "rep", 1)
    up_sent, up_kept = reduce_add(up_came, up_kept)
    up_came = reduce_swaps(up_sent, ups, 2)
    (arrived,) = behind([arrived], up_sent)
    rest_sent, rest_kept = reduce_first(rest_own, arrived, rests)
    rest_came = reduce_swaps(rest_sent, rests, 1)
    up_came = behind(up_came, rest_sent)
    up_sent, up_kept = reduce_join(up_came, up_kept)
    up_came = reduce_swaps_far(up_sent)
    (branch_all,) = behind([branch_all], up_sent)
    half = D // 2
    own_columns = lax.dynamic_slice_in_dim(branch_all, mine * half, half, 1)
    if whole:
        grad_w_down = dot_tn(early_all[:, EARLY:], own_columns)
    else:
        other_columns = lax.dynamic_slice_in_dim(branch_all, (1 - mine) * half, half, 1)
        grad_w_down = dot_tn(early[:, EARLY:], own_columns) + swap(
            dot_tn(early[:, EARLY:], other_columns).astype(bf16), "rep", 1
        ).astype(f32)
        grad_w_down = lax.psum(grad_w_down, "dp")
    rest_came = behind(rest_came, [grad_w_down])
    rest_sent, rest_kept = reduce_add(rest_came, rest_kept)
    rest_came = reduce_swaps(rest_sent, rests, 2)
    up_came = behind(up_came, rest_sent)
    up_chunk = reduce_last(up_came, up_kept)
    up_column = spread_first(up_chunk)
    rest_came = behind(rest_came, [up_chunk])
    rest_sent, rest_kept = reduce_join(rest_came, rest_kept)
    rest_came = reduce_swaps_far(rest_sent)
    up_column = behind(up_column, rest_sent)
    up_mine = spread_second(up_column, ups)
    up_near, up_across = spread_swaps(up_mine, ups, 2), spread_swaps(up_mine, ups, 1)
    rest_came = behind(rest_came, up_near + up_across)
    rest_chunk = reduce_last(rest_came, rest_kept)
    rest_column = spread_first(rest_chunk)
    up_near = behind(up_near, [rest_chunk])
    up_last = spread_swaps(up_near, ups, 1)
    rest_column = behind(rest_column, up_near)
    rest_mine = spread_second(rest_column, rests)
    rest_near, rest_across = spread_swaps(rest_mine, rests, 2), spread_swaps(rest_mine, rests, 1)
    up_last = behind(up_last, rest_mine)
    grad_w_up = unpack_up(place, in_quarters(up_mine, up_near, up_across, up_last))
    rest_near = behind(rest_near, [grad_w_up])
    rest_last = spread_swaps(rest_near, rests, 1)
    grad_w_qkv, grad_w_out, *small = unpack_rest(
        place, in_quarters(rest_mine, rest_near, rest_across, rest_last)
    )
    return (
        pair_loss,
        caption_grad.reshape(local_pairs, CAP, D),
        small[0],
        grad_w_qkv,
        small[1],
        grad_w_out,
        small[2],
        grad_w_up,
        small[3],
        grad_w_down,
    )


def solution(mesh):
    in_specs = (
        P(("dp", "rep"), None, None),
        P(("dp", "rep")),
        P(("dp", "rep"), None, None),
        P(("dp", "rep")),
        P("rep"),
        P("rep", None),
        P("rep"),
        P("rep", None),
        P("rep"),
        P("rep", None),
        P("rep"),
        P("rep", None),
        P(),
        P(),
        P(),
        P(),
        P(),
        P(),
        P(),
        P(),
        P(),
    )
    out_specs = (
        P(("dp", "rep")),
        P(("dp", "rep"), None, None),
        P("rep"),
        P(None, "rep"),
        P("rep"),
        P(None, "rep"),
        P("rep"),
        P(None, "rep"),
        P("rep"),
        P(None, "rep"),
    )
    return jax.shard_map(local, mesh=mesh, in_specs=in_specs, out_specs=out_specs, check_vma=False)
```

```python
import functools
import math

import jax
import jax.numpy as jnp
from jax import lax
from jax.experimental import pallas as pl
from jax.experimental.pallas import tpu as pltpu
from jax.sharding import PartitionSpec as P

D = 768
HEADS = 12
FF = 3072
ILEN = 145
LOWLEN = 50
CAP = 16

SCALE = 100.0
EPS = 1e-06
NEGATIVE = -1e30
LOG2E = math.log2(math.e)
MOST_PAIRS = 2048

UNIT = 160
UNITS = 2
PART = 48
SPAN = 29
QB = 128
BW = 3 * D // 2 + D // 2 + 128
EARLY = D + 128
CHUNKS = 16

f32 = jnp.float32
bf16 = jnp.bfloat16


def dot(left_side, right_side):
    return jnp.dot(left_side, right_side, preferred_element_type=f32)


def dot_nt(left_side, right_side):
    return lax.dot_general(
        left_side, right_side, (((1,), (1,)), ((), ())), preferred_element_type=f32
    )


def dot_tn(left_side, right_side):
    return lax.dot_general(
        left_side, right_side, (((0,), (0,)), ((), ())), preferred_element_type=f32
    )


def normalize(values):
    center = values - jnp.mean(values, -1, keepdims=True)
    inverse = lax.rsqrt(jnp.mean(center * center, -1, keepdims=True) + EPS)
    return center * inverse, inverse


def norm_back(grad, normed, inverse):
    return inverse * (
        grad
        - jnp.mean(grad, -1, keepdims=True)
        - normed * jnp.mean(grad * normed, -1, keepdims=True)
    )


def normal_cdf(values):
    return 0.5 + 0.5 * lax.erf(values * (1.0 / math.sqrt(2.0)))


def split_low(values):
    big = values.astype(bf16)
    return big, (values - big.astype(f32)).astype(bf16)


def tower_kernel(
    groups_ref,
    mine_ref,
    x_hbm,
    vec_own_ref,
    vec_other_ref,
    qkv_own,
    qkv_other,
    out_own,
    out_other,
    up_own,
    up_other,
    down_own,
    down_other,
    emb_ref,
    order,
    x_ref,
    x_wide,
    wqkv,
    wout,
    wup,
    wdown,
    gain_a,
    bqkv,
    gain_m,
    bup,
    xs,
    qkv,
    mixed,
    asum,
    hsum,
    aparts,
    hparts,
    scores,
    attention,
    sems,
):
    total = x_ref.shape[1]
    pitch = total + 8
    mine = mine_ref[0]
    copies = []
    for k in range(ILEN // SPAN):
        span = pl.ds(k * SPAN, SPAN)
        copies.append(pltpu.make_async_copy(x_hbm.at[span], x_ref.at[span], sems.at[8 + k]))
    for k, (own, other, whole) in enumerate(
        (
            (qkv_own, qkv_other, wqkv),
            (out_own, out_other, wout),
            (up_own, up_other, wup),
            (down_own, down_other, wdown),
        )
    ):
        half = own.shape[0]
        copies.append(
            pltpu.make_async_copy(own, whole.at[pl.ds(mine * half, half)], sems.at[2 * k])
        )
        copies.append(
            pltpu.make_async_copy(
                other, whole.at[pl.ds((1 - mine) * half, half)], sems.at[2 * k + 1]
            )
        )
    for copy in copies:
        copy.start()

    vec_own = vec_own_ref[...].astype(f32)
    vec_other = vec_other_ref[...].astype(f32)
    low = jnp.where(mine == 0, vec_own, vec_other)
    high = jnp.where(mine == 0, vec_other, vec_own)
    start = 0
    for dest, size, at in (
        (gain_a, D // 2, (0, D // 2)),
        (bqkv, D, (0, 2 * D)),
        (gain_m, D // 2, (0, D // 2)),
        (bup, FF // 2, (0, FF // 2)),
    ):
        dest[:, at[0] : at[0] + size] = low[:, start : start + size]
        dest[:, at[1] : at[1] + size] = high[:, start : start + size]
        start += size
    bqkv[:, D : 2 * D] = jnp.zeros((1, D), f32)

    def count(i, found):
        return found + groups_ref[i]

    n_hi = lax.fori_loop(0, total, count, 0)

    def place_one(i, state):
        hi, lo = state
        group = groups_ref[i]
        order[jnp.where(group == 1, hi, lo)] = i
        return hi + group, lo + 1 - group

    lax.fori_loop(0, total, place_one, (0, n_hi))
    n_units = n_hi + (total - n_hi + 2) // 3

    xs[...] = jnp.zeros_like(xs)
    first = lax.broadcasted_iota(jnp.int32, (1, 128), 1) < 64
    key_at = lax.broadcasted_iota(jnp.int32, (UNIT, UNIT), 1)
    row_at = lax.broadcasted_iota(jnp.int32, (UNIT, UNIT), 0)
    sub = lax.broadcasted_iota(jnp.int32, (8, 1), 0)

    def place(unit, k):
        last = jnp.minimum(unit, n_units - 1)
        is_hi = last < n_hi
        where = jnp.where(is_hi, last, n_hi + 3 * (last - n_hi) + k)
        return order[jnp.minimum(where, total - 1)], is_hi

    def keep_parts(values, j, dest, col, width):
        rows = values.reshape(UNIT // 8, 8, width)
        parts = [
            jnp.sum(rows[0:6], 0),
            rows[6],
            jnp.sum(rows[7:12], 0),
            rows[12],
            jnp.sum(rows[13:18], 0),
            rows[18],
        ]
        for k, part in enumerate(parts):
            dest[j * PART + k * 8 : j * PART + k * 8 + 8, col : col + width] = part

    loads = copies[: ILEN // SPAN]
    copies = copies[ILEN // SPAN :]

    def widen(t, carry):
        for panel in range(D // 128):
            x_wide[panel, pl.ds(pl.multiple_of(t * pitch, 8), total), :] = x_ref[
                t, :, panel * 128 : (panel + 1) * 128
            ].astype(f32)
        return carry

    for k, load in enumerate(loads):
        load.wait()
        lax.fori_loop(k * SPAN, (k + 1) * SPAN, widen, 0)
    for copy in copies[:2]:
        copy.wait()

    def body(step, carry):
        for j in range(UNITS):
            unit = step * UNITS + j
            one, is_hi = place(unit, 0)
            two, three = place(unit, 1)[0], place(unit, 2)[0]
            base = j * UNIT

            @pl.when(is_hi)
            def _():
                for panel in range(D // 128):
                    xs[base : base + ILEN, panel * 128 : (panel + 1) * 128] = x_wide[
                        panel, pl.ds(one, ILEN, stride=pitch), :
                    ]

            @pl.when(jnp.logical_not(is_hi))
            def _():
                for k, index in enumerate((one, two, three)):
                    for panel in range(D // 128):
                        xs[
                            base + LOWLEN * k : base + LOWLEN * (k + 1),
                            panel * 128 : (panel + 1) * 128,
                        ] = x_wide[panel, pl.ds(index, LOWLEN, stride=pitch), :]

        low_rows = (normalize(xs[...])[0] * gain_a[...]).astype(bf16)
        for col in range(0, 3 * D, 256):
            values = dot(low_rows, wqkv[:, col : col + 256]) + bqkv[:, col : col + 256]
            if col < D:
                values = values * (LOG2E / 8.0)
            qkv[:, col : col + 256] = values.astype(bf16)

        @pl.when(step == 0)
        def _():
            for copy in copies[2:6]:
                copy.wait()

        for j in range(UNITS):
            is_hi = place(step * UNITS + j, 0)[1]
            base = j * UNIT
            key_seg = jnp.where(key_at < LOWLEN, 0, jnp.where(key_at < 2 * LOWLEN, 1, 2))
            row_seg = jnp.where(row_at < LOWLEN, 0, jnp.where(row_at < 2 * LOWLEN, 1, 2))
            short_ok = jnp.logical_and(key_seg == row_seg, key_at < 3 * LOWLEN)
            allowed = jnp.where(
                is_hi, (key_at < ILEN).astype(jnp.int32), short_ok.astype(jnp.int32)
            )
            bias = jnp.where(allowed > 0, 0.0, NEGATIVE)
            for p in range(HEADS // 2):
                query = qkv[base : base + UNIT, p * 128 : (p + 1) * 128]
                key = qkv[base : base + UNIT, D + p * 128 : D + (p + 1) * 128]
                for h in range(2):
                    head = first if h == 0 else jnp.logical_not(first)
                    at = (j * HEADS + 2 * p + h) * UNIT
                    scores[at : at + UNIT, :] = (
                        dot_nt(jnp.where(head, query, jnp.zeros_like(query)), key) + bias
                    )
        for j in range(UNITS):
            part = slice(j * HEADS * UNIT, (j + 1) * HEADS * UNIT)
            values = scores[part, :]
            powers = jnp.exp2(values - jnp.max(values, 1, keepdims=True))
            attention[part, :] = powers.astype(bf16)
        for j in range(UNITS):
            base = j * UNIT
            for p in range(HEADS // 2):
                lanes = slice(p * 128, (p + 1) * 128)
                value = qkv[base : base + UNIT, 2 * D + p * 128 : 2 * D + (p + 1) * 128]
                outs = []
                at = (j * HEADS + 2 * p) * UNIT
                value_one = jnp.concatenate([value, jnp.ones_like(value)], 1)
                for h in range(2):
                    summed = dot(attention[at + h * UNIT : at + (h + 1) * UNIT, :], value_one)
                    outs.append(summed[:, :128] / summed[:, 128:])
                mixed[base : base + UNIT, lanes] = jnp.where(first, outs[0], outs[1]).astype(bf16)
        for col in range(0, D, 256):
            xs[:, col : col + 256] += dot(mixed[...], wout[:, col : col + 256])
        for j in range(UNITS):
            keep_parts(xs[j * UNIT : (j + 1) * UNIT, :], j, aparts, 0, D)
        low_two = (normalize(xs[...])[0] * gain_m[...]).astype(bf16)
        width = 1024
        for col in range(0, FF, width):
            pre_act = dot(low_two, wup[:, col : col + width]) + bup[:, col : col + width]
            hidden = pre_act * normal_cdf(pre_act)
            for j in range(UNITS):
                keep_parts(hidden[j * UNIT : (j + 1) * UNIT], j, hparts, col, width)
        for j in range(UNITS):
            unit = step * UNITS + j
            one, is_hi = place(unit, 0)
            two, three = place(unit, 1)[0], place(unit, 2)[0]

            def rows_of(index):
                return pl.ds(pl.multiple_of(index * 8, 8), 8)

            @pl.when(is_hi)
            def _():
                for src, dest in ((aparts, asum), (hparts, hsum)):
                    part = [src[j * PART + k * 8 : j * PART + k * 8 + 8, :] for k in range(6)]
                    dest[rows_of(one), :] = (
                        (part[0] + part[1])
                        + (part[2] + part[3])
                        + (part[4] + jnp.where(sub < 1, part[5], 0.0))
                    )

            @pl.when(jnp.logical_not(is_hi))
            def _():
                for src, dest in ((aparts, asum), (hparts, hsum)):
                    part = [src[j * PART + k * 8 : j * PART + k * 8 + 8, :] for k in range(6)]
                    dest[rows_of(three), :] = (
                        jnp.where(sub < 4, 0.0, part[3])
                        + part[4]
                        + jnp.where(sub < 6, part[5], 0.0)
                    )
                    dest[rows_of(two), :] = (
                        jnp.where(sub < 2, 0.0, part[1])
                        + part[2]
                        + jnp.where(sub < 4, part[3], 0.0)
                    )
                    dest[rows_of(one), :] = part[0] + jnp.where(sub < 2, part[1], 0.0)

        return carry

    lax.fori_loop(0, (n_units + UNITS - 1) // UNITS, body, 0)
    for copy in copies[6:]:
        copy.wait()
    which = lax.broadcasted_iota(jnp.int32, (total, 128), 0)
    scale = jnp.zeros((total, 128), f32)
    for i in range(total):
        scale = jnp.where(
            which == i, jnp.where(groups_ref[i] == 1, 1.0 / ILEN, 1.0 / LOWLEN), scale
        )
    scale = scale[:, 0:1]
    big, rest = split_low(jnp.sum(hsum[...].reshape(total, 8, FF), 1) * scale)
    product = dot(jnp.concatenate([big, rest], 0), wdown[...])
    pooled = jnp.sum(asum[...].reshape(total, 8, D), 1) * scale + product[:total] + product[total:]
    emb_ref[...] = (
        pooled * lax.rsqrt(jnp.sum(pooled * pooled, -1, keepdims=True) + EPS)
    ).astype(bf16)


VM = pl.BlockSpec(memory_space=pltpu.VMEM)
SM = pl.BlockSpec(memory_space=pltpu.SMEM)
ANY = pl.BlockSpec(memory_space=pltpu.HBM)


def limit(mebibytes):
    return pltpu.CompilerParams(vmem_limit_bytes=mebibytes * 1024 * 1024)


def image_tower(images, groups, mine, vec_own, vec_other, weights):
    number = images.shape[1]
    rows = UNITS * UNIT
    flops = number * 100 * 2 * (4 * D * D + D * FF)
    return pl.pallas_call(
        tower_kernel,
        out_shape=jax.ShapeDtypeStruct((number, D), bf16),
        in_specs=[SM, SM, ANY, VM, VM] + [ANY] * 8,
        out_specs=VM,
        scratch_shapes=[
            pltpu.SMEM((number,), jnp.int32),
            pltpu.VMEM(images.shape, bf16),
            pltpu.VMEM((D // 128, ILEN * (number + 8), 128), f32),
            pltpu.VMEM((D, 3 * D), bf16),
            pltpu.VMEM((D, D), bf16),
            pltpu.VMEM((D, FF), bf16),
            pltpu.VMEM((FF, D), bf16),
            pltpu.VMEM((1, D), f32),
            pltpu.VMEM((1, 3 * D), f32),
            pltpu.VMEM((1, D), f32),
            pltpu.VMEM((1, FF), f32),
            pltpu.VMEM((rows, D), f32),
            pltpu.VMEM((rows, 3 * D), bf16),
            pltpu.VMEM((rows, D), bf16),
            pltpu.VMEM((number * 8, D), f32),
            pltpu.VMEM((number * 8, FF), f32),
            pltpu.VMEM((UNITS * PART, D), f32),
            pltpu.VMEM((UNITS * PART, FF), f32),
            pltpu.VMEM((UNITS * HEADS * UNIT, UNIT), f32),
            pltpu.VMEM((UNITS * HEADS * UNIT, UNIT), bf16),
            pltpu.SemaphoreType.DMA((8 + ILEN // SPAN,)),
        ],
        compiler_params=limit(62),
        cost_estimate=pl.CostEstimate(
            flops=flops, bytes_accessed=24 * 1024 * 1024, transcendentals=0
        ),
        name="image_tower",
    )(groups, mine, images, vec_own, vec_other, *weights)


def lens_along(lens_ref, start, number):
    owner = lax.broadcasted_iota(jnp.int32, (1, number * CAP), 1) // CAP
    lens = jnp.zeros((1, number * CAP), jnp.int32)
    for c in range(number):
        lens = jnp.where(owner == c, lens_ref[start + c], lens)
    return lens


def score_bias(lens_ref, block):
    per = QB // CAP
    position = lax.broadcasted_iota(jnp.int32, (1, QB), 1) % CAP
    valid = position < lens_along(lens_ref, block * per, per)
    rows = lax.broadcasted_iota(jnp.int32, (QB, QB), 0) // CAP
    columns = lax.broadcasted_iota(jnp.int32, (QB, QB), 1) // CAP
    return jnp.where(jnp.logical_and(rows == columns, valid), 0.0, NEGATIVE)


def forward_kernel(
    lens_ref,
    x_ref,
    vec_ref,
    wqkv_ref,
    wout_ref,
    wup_ref,
    wdown_ref,
    qkv,
    mixed,
    after,
    mlp,
    slope,
    attention,
    early,
    hidden,
    scores,
):
    rows = x_ref.shape[0]
    number = rows // CAP
    first = lax.broadcasted_iota(jnp.int32, (1, 128), 1) < 64
    normed, _ = normalize(x_ref[...].astype(f32))
    low = (normed * vec_ref[:, 0:D]).astype(bf16)
    for col in range(0, 3 * D, 256):
        values = dot(low, wqkv_ref[:, col : col + 256])
        if col < D:
            values = values + vec_ref[:, D + col : D + col + 256]
        if col >= 2 * D:
            values = values + vec_ref[:, col : col + 256]
        values = values.astype(bf16)
        if col < D:
            values = values * jnp.asarray(0.125, bf16)
        qkv[:, col : col + 256] = values
    for block in range(rows // QB):
        bias = score_bias(lens_ref, block)
        span = slice(block * QB, (block + 1) * QB)
        for p in range(HEADS // 2):
            query = qkv[span, p * 128 : (p + 1) * 128]
            key = qkv[span, D + p * 128 : D + (p + 1) * 128]
            for h in range(2):
                head = first if h == 0 else jnp.logical_not(first)
                at = (block * HEADS + 2 * p + h) * QB
                scores[at : at + QB, :] = (
                    dot_nt(jnp.where(head, query, jnp.zeros_like(query)), key) * LOG2E + bias
                )
    for block in range(rows // QB):
        part = slice(block * HEADS * QB, (block + 1) * HEADS * QB)
        values = scores[part, :]
        powers = jnp.exp2(values - jnp.max(values, 1, keepdims=True))
        attention[part, :] = (powers * (1.0 / jnp.sum(powers, 1, keepdims=True))).astype(bf16)
    for block in range(rows // QB):
        span = slice(block * QB, (block + 1) * QB)
        for p in range(HEADS // 2):
            value = qkv[span, 2 * D + p * 128 : 2 * D + (p + 1) * 128]
            at = (block * HEADS + 2 * p) * QB
            outs = [dot(attention[at + h * QB : at + (h + 1) * QB, :], value) for h in range(2)]
            mixed[span, p * 128 : (p + 1) * 128] = jnp.where(first, outs[0], outs[1]).astype(bf16)
    for col in range(0, D, 256):
        after[:, col : col + 256] = x_ref[:, col : col + 256].astype(f32) + dot(
            mixed[...], wout_ref[:, col : col + 256]
        )
    mlp[...] = (normalize(after[...])[0] * vec_ref[:, 3 * D : 4 * D]).astype(bf16)
    lens = lens_along(lens_ref, 0, number)
    position = lax.broadcasted_iota(jnp.int32, (1, rows), 1)
    owner = (
        lax.broadcasted_iota(jnp.int32, (number, rows), 0)
        == lax.broadcasted_iota(jnp.int32, (number, rows), 1) // CAP
    )
    members = jnp.where(jnp.logical_and(owner, position % CAP < lens), 1.0, 0.0)
    pool = members.astype(bf16)
    count = jnp.sum(members, 1, keepdims=True)
    width = 512
    for col in range(0, FF, width):
        span = slice(col, col + width)
        pre_act = dot(mlp[...], wup_ref[:, span]) + vec_ref[:, 4 * D + col : 4 * D + col + width]
        phi = normal_cdf(pre_act)
        hidden[:, span] = (pre_act * phi).astype(bf16)
        density = jnp.exp2(pre_act * pre_act * (-0.5 * LOG2E)) * (1.0 / math.sqrt(2.0 * math.pi))
        slope[:, span] = (phi + pre_act * density).astype(bf16)
    big, rest = split_low(dot(pool, hidden[...]))
    after_big, after_rest = split_low(after[...])
    pooled = (
        dot(pool, after_big)
        + dot(pool, after_rest)
        + dot(big, wdown_ref[...])
        + dot(rest, wdown_ref[...])
    )
    early[:, 0:D] = (pooled / count).astype(bf16)
    early[:, D:EARLY] = jnp.broadcast_to(count, (number, EARLY - D)).astype(bf16)
    early[:, EARLY:] = big


def text_forward(captions, lens, vec, w_qkv, w_out, w_up, w_down):
    rows = captions.shape[0]
    shape = jax.ShapeDtypeStruct
    return pl.pallas_call(
        forward_kernel,
        out_shape=[
            shape((rows, 3 * D), bf16),
            shape((rows, D), bf16),
            shape((rows, D), f32),
            shape((rows, D), bf16),
            shape((rows, FF), bf16),
            shape((rows * HEADS, QB), bf16),
            shape((rows // CAP, EARLY + FF), bf16),
        ],
        in_specs=[SM] + [VM] * 6,
        out_specs=[VM] * 7,
        scratch_shapes=[pltpu.VMEM((rows, FF), bf16), pltpu.VMEM((rows * HEADS, QB), f32)],
        compiler_params=limit(60),
        cost_estimate=pl.CostEstimate(
            flops=2 * rows * (4 * D * D + 2 * D * FF),
            bytes_accessed=24 * 1024 * 1024,
            transcendentals=0,
        ),
        name="text_forward",
    )(lens, captions, vec, w_qkv, w_out, w_up, w_down)


def put_chunks(dest, values, place_ref, stream, col):
    rows = values.shape[0] // CHUNKS
    for chunk in range(CHUNKS):
        at = pl.multiple_of(place_ref[stream, chunk] * rows, 16)
        dest[pl.ds(at, rows), col : col + values.shape[1]] = values[
            chunk * rows : (chunk + 1) * rows
        ].astype(dest.dtype)


def up_kernel(
    place_ref, mine_ref, lens_ref, branch_ref, slope_ref, mlp_ref, wdown_ref,
    grad_pre, own, other, grad_bup, grad_hidden, mlp_t,
):
    number = slope_ref.shape[0] // CAP
    half = FF // 2
    mine = mine_ref[0]
    for col in range(0, FF, 512):
        grad_hidden[:, col : col + 512] = dot_nt(branch_ref[...], wdown_ref[col : col + 512, :])
    position = lax.broadcasted_iota(jnp.int32, (CAP, 1), 0)
    for c in range(number):
        span = slice(c * CAP, (c + 1) * CAP)
        keep = jnp.where(position < lens_ref[c], 1.0, 0.0)
        grad_pre[span, :] = (
            grad_hidden[c : c + 1, :] * slope_ref[span, :].astype(f32) * keep
        ).astype(bf16)
    mlp_t[...] = mlp_ref[...].T
    for which, dest in ((1 - mine, other), (mine, own)):
        for col in range(0, half, 384):
            lanes = pl.ds(pl.multiple_of(which * half + col, 128), 384)
            put_chunks(dest, dot(mlp_t[...], grad_pre[:, lanes]), place_ref, 2 * col // half, col)
    for col in range(0, FF, 512):
        grad_bup[:, col : col + 512] = jnp.sum(
            grad_pre[:, col : col + 512].astype(f32), 0, keepdims=True
        )


def up_backward(place, mine, lens, branch, slope, mlp, w_down):
    rows = slope.shape[0]
    shape = jax.ShapeDtypeStruct
    return pl.pallas_call(
        up_kernel,
        out_shape=[
            shape((rows, FF), bf16),
            shape((D, FF // 2), f32),
            shape((D, FF // 2), bf16),
            shape((1, FF), f32),
        ],
        in_specs=[SM, SM, SM] + [VM] * 4,
        out_specs=[VM] * 4,
        scratch_shapes=[pltpu.VMEM((rows // CAP, FF), f32), pltpu.VMEM((D, rows), bf16)],
        compiler_params=limit(24),
        cost_estimate=pl.CostEstimate(
            flops=2 * rows * D * FF, bytes_accessed=20 * 1024 * 1024, transcendentals=0
        ),
        name="up_backward",
    )(place, mine, lens, branch, slope, mlp, w_down)


def mlp_kernel(
    lens_ref, pre_ref, grad_ref, after_ref, vec_ref, wup_ref, wout_ref,
    grad_after, grad_mixed, grad_gain, grad_out,
):
    number = after_ref.shape[0] // CAP
    grad_mlp = dot_nt(pre_ref[...], wup_ref[...])
    normed_two, inverse_two = normalize(after_ref[...])
    grad_gain[...] = jnp.sum(grad_mlp * normed_two, 0, keepdims=True)
    grad_after[...] = norm_back(grad_mlp * vec_ref[:, 3 * D : 4 * D], normed_two, inverse_two)
    position = lax.broadcasted_iota(jnp.int32, (CAP, 1), 0)
    for c in range(number):
        keep = jnp.where(position < lens_ref[c], 1.0, 0.0)
        grad_after[c * CAP : (c + 1) * CAP, :] += grad_ref[c : c + 1, :] * keep
    grad_out[...] = grad_after[...].astype(bf16)
    for col in range(0, D, 256):
        grad_mixed[:, col : col + 256] = dot_nt(
            grad_out[...], wout_ref[col : col + 256, :]
        ).astype(bf16)


def mlp_backward(lens, grad_pre, grads, after, vec, w_up, w_out):
    rows = after.shape[0]
    shape = jax.ShapeDtypeStruct
    return pl.pallas_call(
        mlp_kernel,
        out_shape=[shape((rows, D), f32), shape((rows, D), bf16), shape((1, D), f32)],
        in_specs=[SM] + [VM] * 6,
        out_specs=[VM] * 3,
        scratch_shapes=[pltpu.VMEM((rows, D), bf16)],
        compiler_params=limit(28),
        cost_estimate=pl.CostEstimate(
            flops=2 * rows * (D * D + D * FF), bytes_accessed=20 * 1024 * 1024, transcendentals=0
        ),
        name="mlp_backward",
    )(lens, grad_pre, grads, after, vec, w_up, w_out)


def attention_kernel(
    qkv_ref, att_ref, mixed_ref, grad_ref, grad_proj, grad_att, means, grad_s, *, start
):
    first = lax.broadcasted_iota(jnp.int32, (1, 128), 1) < 64
    ones = jnp.ones((128, QB), bf16)
    heads = (first, jnp.logical_not(first))
    blocks = grad_proj.shape[0] // QB
    for block in range(blocks):
        span = slice(start + block * QB, start + (block + 1) * QB)
        for p in range(HEADS // 2):
            at = p * 128
            value = qkv_ref[span, 2 * D + at : 2 * D + at + 128]
            grad = grad_ref[span, at : at + 128]
            product = (grad.astype(f32) * mixed_ref[span, at : at + 128].astype(f32)).astype(bf16)
            for h, head in enumerate(heads):
                to = (block * HEADS + 2 * p + h) * QB
                grad_att[to : to + QB, :] = dot_nt(
                    jnp.where(head, grad, jnp.zeros_like(grad)), value
                )
                means[to : to + QB, :] = dot(
                    jnp.where(head, product, jnp.zeros_like(product)), ones
                )
    for block in range(blocks):
        part = slice(block * HEADS * QB, (block + 1) * HEADS * QB)
        place = (start // QB + block) * HEADS * QB
        low = att_ref[place : place + HEADS * QB, :].astype(f32)
        grad_s[part, :] = (low * (grad_att[part, :] - means[part, :])).astype(bf16)
    for block in range(blocks):
        span = slice(start + block * QB, start + (block + 1) * QB)
        dest = slice(block * QB, (block + 1) * QB)
        for p in range(HEADS // 2):
            at = p * 128
            query = qkv_ref[span, at : at + 128]
            key = qkv_ref[span, D + at : D + at + 128]
            grad = grad_ref[span, at : at + 128]
            grad_q, grad_k, grad_v = [], [], []
            for h in range(2):
                to = (block * HEADS + 2 * p + h) * QB
                place = ((start // QB + block) * HEADS + 2 * p + h) * QB
                sgrad = grad_s[to : to + QB, :]
                grad_q.append(dot(sgrad, key))
                grad_k.append(dot_tn(sgrad, query))
                grad_v.append(dot_tn(att_ref[place : place + QB, :], grad))
            for k, (parts, scale) in enumerate(((grad_q, 0.125), (grad_k, 1.0), (grad_v, 1.0))):
                grad_proj[dest, k * D + at : k * D + at + 128] = (
                    jnp.where(first, parts[0], parts[1]) * scale
                ).astype(bf16)


def input_kernel(
    proj_ref, after_ref, x_ref, vec_ref, gain_ref, bup_ref, wqkv_ref, caption_grad, sums, input_low
):
    gain_a = vec_ref[:, 0:D]
    normed_one, inverse_one = normalize(x_ref[...].astype(f32))
    input_low[...] = (normed_one * gain_a).astype(bf16)
    grad_in = dot_nt(proj_ref[...], wqkv_ref[...])
    sums[:, 0:D] = jnp.sum(grad_in * normed_one, 0, keepdims=True)
    sums[:, D : 2 * D] = jnp.sum(proj_ref[:, 0:D].astype(f32), 0, keepdims=True)
    sums[:, 2 * D : 3 * D] = jnp.sum(proj_ref[:, 2 * D :].astype(f32), 0, keepdims=True)
    sums[:, 3 * D : 4 * D] = gain_ref[...]
    sums[:, 4 * D :] = bup_ref[...]
    caption_grad[...] = after_ref[...] + norm_back(grad_in * gain_a, normed_one, inverse_one)


def proj_kernel(
    place_ref, mine_ref, proj_ref, after_ref, mixed_ref, input_ref, sums, own, other, lhs_t, grad_out
):
    chunk_rows = D // CHUNKS
    mine = mine_ref[0]
    lhs_t[...] = input_ref[...].T
    half_out, half_qkv = D // 2, 3 * D // 2
    for which, dest in ((1 - mine, other), (mine, own)):
        for col in range(0, half_qkv, 384):
            lanes = pl.ds(pl.multiple_of(which * half_qkv + col, 128), 384)
            put_chunks(dest, dot(lhs_t[...], proj_ref[:, lanes]), place_ref, col // 768, col)
    lhs_t[...] = mixed_ref[...].T
    grad_out[...] = after_ref[...].astype(bf16)
    for which, dest in ((1 - mine, other), (mine, own)):
        lanes = pl.ds(pl.multiple_of(which * half_out, 128), half_out)
        put_chunks(dest, dot(lhs_t[...], grad_out[:, lanes]), place_ref, 1, half_qkv)
    for which, dest in ((1 - mine, other), (mine, own)):
        dest[:, BW - 128 :] = jnp.zeros((D, 128), dest.dtype)
        pieces = []
        for start, size in ((0, D), (D, 2 * D), (3 * D, D), (4 * D, FF)):
            for k in range(0, size // 2, 128):
                at = pl.multiple_of(start + which * (size // 2) + k, 128)
                pieces.append(sums[:, pl.ds(at, 128)])
        pieces += [jnp.zeros_like(pieces[0])] * (32 - len(pieces))
        at = pl.multiple_of(place_ref[1, 0] * chunk_rows, 16)
        dest[pl.ds(at, 32), BW - 128 :] = jnp.concatenate(pieces, 0).astype(dest.dtype)


def rest_kernel(
    place_ref, mine_ref, qkv_ref, att_ref, mixed_ref, grad_ref, after_ref, x_ref, vec_ref,
    gain_ref, bup_ref, wqkv_ref, caption_grad, own, other,
    grad_proj, sums, input_low, grad_att, means, grad_s, lhs_t, grad_out,
):
    attention_kernel(
        qkv_ref, att_ref, mixed_ref, grad_ref, grad_proj, grad_att, means, grad_s, start=0
    )
    input_kernel(
        grad_proj, after_ref, x_ref, vec_ref, gain_ref, bup_ref, wqkv_ref,
        caption_grad, sums, input_low,
    )
    proj_kernel(
        place_ref, mine_ref, grad_proj, after_ref, mixed_ref, input_low, sums,
        own, other, lhs_t, grad_out,
    )


def rest_backward(
    place, mine, qkv, attention, mixed, grad_mixed, grad_after, captions, vec, grad_gain, grad_bup, w_qkv
):
    rows = captions.shape[0]
    shape = jax.ShapeDtypeStruct
    return pl.pallas_call(
        rest_kernel,
        out_shape=[shape((rows, D), f32), shape((D, BW), f32), shape((D, BW), bf16)],
        in_specs=[SM, SM] + [VM] * 10,
        out_specs=[VM] * 3,
        scratch_shapes=[
            pltpu.VMEM((rows, 3 * D), bf16),
            pltpu.VMEM((1, 4 * D + FF), f32),
            pltpu.VMEM((rows, D), bf16),
            pltpu.VMEM((rows * HEADS, QB), f32),
            pltpu.VMEM((rows * HEADS, QB), f32),
            pltpu.VMEM((rows * HEADS, QB), bf16),
            pltpu.VMEM((D, rows), bf16),
            pltpu.VMEM((rows, D), bf16),
        ],
        compiler_params=limit(44),
        cost_estimate=pl.CostEstimate(
            flops=2 * rows * 48 * D * D, bytes_accessed=60 * 1024 * 1024, transcendentals=0
        ),
        name="rest_backward",
    )(
        place, mine, qkv, attention, mixed, grad_mixed, grad_after, captions, vec,
        grad_gain, grad_bup, w_qkv,
    )


def dp_bits():
    bits, bit = [], 1
    while bit < lax.axis_size("dp"):
        bits.append(bit)
        bit *= 2
    return bits


def swap(values, axis, bit):
    size = lax.axis_size(axis)
    return lax.ppermute(values, axis, [(place, place ^ bit) for place in range(size)])


def gather_relative(values):
    bits = dp_bits()
    while bits:
        pair = bits[-2:]
        bits = bits[:-2]
        offsets = [0]
        for bit in pair:
            offsets += [entry + bit for entry in offsets]
        values = jnp.concatenate([swap(values, "dp", k) if k else values for k in offsets], 0)
    return jnp.concatenate([values, swap(values, "rep", 1)], 0)


def relative_chips():
    bits, table = dp_bits(), [0]
    while bits:
        pair = bits[-2:]
        bits = bits[:-2]
        offsets = [0]
        for bit in pair:
            offsets += [entry + bit for entry in offsets]
        table = [entry ^ k for k in offsets for entry in table]
    return table


def chunk_places():
    away = jnp.arange(CHUNKS, dtype=jnp.int32) ^ (lax.axis_index("dp") % CHUNKS)
    one, two, rest = away % 2, away // 2 % 2, away // 4
    return jnp.stack([one * 8 + two * 4 + rest, two * 8 + one * 4 + rest]).astype(jnp.int32)


def streams_of(width):
    return ((slice(0, width), 1, 2), (slice(width, None), 2, 1))


def reduce_first(own, arrived, streams):
    half = own.shape[0] // 2

    def both(rows, lanes):
        return own[rows, lanes] + arrived[rows, lanes].astype(f32)

    sent = [both(slice(half, None), lanes).astype(bf16) for lanes, _, _ in streams]
    return sent, [both(slice(0, half), lanes) for lanes, _, _ in streams]


def reduce_swaps(sent, streams, stage):
    return [swap(piece, "dp", stream[stage]) for piece, stream in zip(sent, streams)]


def reduce_add(came, kept):
    half = kept[0].shape[0] // 2
    totals = [total + got.astype(f32) for total, got in zip(kept, came)]
    return [total[half:].astype(bf16) for total in totals], [total[:half] for total in totals]


def reduce_join(came, kept):
    total = jnp.concatenate([total + got.astype(f32) for total, got in zip(kept, came)], 1)
    rows = total.shape[0] // 4
    return [total[k * rows : (k + 1) * rows].astype(bf16) for k in (1, 2, 3)], total[:rows]


def reduce_last(parts, total):
    total = total + sum(part.astype(f32) for part in parts)
    for bit in dp_bits()[4:]:
        total = total + swap(total.astype(bf16), "dp", bit).astype(f32)
    return total.astype(bf16)


def spread_first(chunk):
    return [swap(chunk, "dp", 4 * k) if k else chunk for k in range(4)]


def spread_second(column, streams):
    return [jnp.concatenate([piece[:, lanes] for piece in column], 0) for lanes, _, _ in streams]


def spread_swaps(pieces, streams, stage):
    return [swap(piece, "dp", stream[stage]) for piece, stream in zip(pieces, streams)]


def reduce_swaps_far(sent):
    return [swap(piece, "dp", 4 * (k + 1)) for k, piece in enumerate(sent)]


def in_quarters(*quarters):
    return [quarter[stream] for stream in range(2) for quarter in quarters]


def behind(values, others):
    return list(lax.optimization_barrier((*values, *others))[: len(values)])


def each_chunk(place_ref):
    rows = D // CHUNKS
    place = place_ref[0, 0]
    me = place // 8 + 2 * (place // 4 % 2) + 4 * (place % 4)
    for stream in range(2):
        for quarter in range(4):
            for k in range(4):
                high, low = quarter // 2, quarter % 2
                away = (high + 2 * low if stream == 0 else low + 2 * high) + 4 * k
                chunk = me ^ away
                at = pl.ds(pl.multiple_of(chunk * rows, 16), rows)
                yield stream, stream * 4 + quarter, slice(k * rows, (k + 1) * rows), chunk, at


def unpack_up_kernel(place_ref, *refs):
    parts, g_up = refs[:8], refs[8]
    for stream, part, span, _, at in each_chunk(place_ref):
        lanes = slice(stream * FF // 4, (stream + 1) * FF // 4)
        g_up[at, lanes] = parts[part][span, :].astype(f32)


def unpack_rest_kernel(place_ref, *refs):
    parts, (g_qkv, g_out), vectors = refs[:8], refs[8:10], refs[10:]
    for stream, part, span, chunk, at in each_chunk(place_ref):
        rest = parts[part][span, :].astype(f32)
        if stream == 0:
            g_qkv[at, 0:D] = rest
            continue
        g_qkv[at, D:] = rest[:, : D // 2]
        g_out[at, :] = rest[:, D // 2 : D]

        @pl.when(chunk == 0)
        def _():
            row = 0
            for dest in vectors:
                for lane in range(0, dest.shape[0], 128):
                    dest[lane : lane + 128] = rest[row, D:]
                    row += 1


def unpack_up(place, parts):
    return pl.pallas_call(
        unpack_up_kernel,
        out_shape=jax.ShapeDtypeStruct((D, FF // 2), f32),
        in_specs=[SM] + [VM] * 8,
        out_specs=VM,
        compiler_params=limit(20),
        name="unpack_up",
    )(place, *parts)


def unpack_rest(place, parts):
    shape = jax.ShapeDtypeStruct
    return pl.pallas_call(
        unpack_rest_kernel,
        out_shape=[
            shape((D, 3 * D // 2), f32),
            shape((D, D // 2), f32),
            shape((D // 2,), f32),
            shape((D,), f32),
            shape((D // 2,), f32),
            shape((FF // 2,), f32),
        ],
        in_specs=[SM] + [VM] * 8,
        out_specs=[VM] * 6,
        compiler_params=limit(20),
        name="unpack_rest",
    )(place, *parts)


def softmax_parts(scores, axis):
    maxima = jnp.max(scores, axis, keepdims=True)
    powers = jnp.exp(scores - maxima)
    totals = jnp.sum(powers, axis, keepdims=True)
    return powers / totals, maxima + jnp.log(totals)


def text_unit(pooled_low, text_proj):
    proj_out = dot(pooled_low, text_proj)
    inverse_z = lax.rsqrt(jnp.sum(proj_out * proj_out, -1, keepdims=True) + EPS)
    return proj_out * inverse_z, inverse_z


def branch_grad(grad_unit, unit_text, inverse_z, text_proj, lengths):
    grad_projout = (
        inverse_z * (grad_unit - unit_text * jnp.sum(unit_text * grad_unit, -1, keepdims=True))
    ).astype(bf16)
    return dot_nt(grad_projout, text_proj) / lengths


def loss_kernel(
    where_ref, early_ref, image_ref, proj_ref, pair_loss, own_grads, own_branch, branch,
    unit, inverse, scores, sgrad,
):
    total = image_ref.shape[0]
    number = own_grads.shape[0]
    chip, mine = where_ref[0], where_ref[1]
    block = 256
    for row in range(0, total, block):
        span = slice(row, row + block)
        proj_out = dot(early_ref[span, 0:D], proj_ref[...])
        inverse_z = lax.rsqrt(jnp.sum(proj_out * proj_out, -1, keepdims=True) + EPS)
        inverse[span, :] = jnp.broadcast_to(inverse_z, (block, 128))
        unit[span, :] = proj_out * inverse_z
        scores[span, :] = dot_nt(unit[span, :].astype(bf16), image_ref[...]) * SCALE
    place = lax.broadcasted_iota(jnp.int32, (1, total), 1) // number
    chips = total // (2 * number)
    away = place % chips
    other = place // chips
    from_chip = chip ^ (away // 4 + 4 * (away % 4)) if chips == 16 else None
    image_id = (from_chip * 2 + (mine ^ other)) * number + (
        lax.broadcasted_iota(jnp.int32, (1, total), 1) % number
    )
    column_max = jnp.max(scores[...], 0, keepdims=True)
    column_sum = jnp.zeros((1, total), f32)
    for row in range(0, total, block):
        column_sum += jnp.sum(
            jnp.exp(scores[row : row + block, :] - column_max), 0, keepdims=True
        )
    column_total = column_max + jnp.log(column_sum)
    for row in range(0, total, block):
        span = slice(row, row + block)
        values = scores[span, :]
        row_max = jnp.max(values, 1, keepdims=True)
        powers = jnp.exp(values - row_max)
        by_text = powers * (0.5 / jnp.sum(powers, 1, keepdims=True))
        by_image = jnp.exp(values - column_max) * (0.5 / column_sum)
        text_id = lax.broadcasted_iota(jnp.int32, (block, 1), 0) + row
        same = jnp.where(text_id == image_id, 1.0, 0.0)
        sgrad[span, :] = (by_text + by_image - same).astype(bf16)
        grad_unit = dot(sgrad[span, :], image_ref[...]) * SCALE
        unit_text = unit[span, :]
        grad_proj = (
            inverse[span, 0:1]
            * (grad_unit - unit_text * jnp.sum(unit_text * grad_unit, -1, keepdims=True))
        ).astype(bf16)
        unit[span, :] = dot_nt(grad_proj, proj_ref[...]) / early_ref[span, D : D + 1].astype(f32)
        branch[span, :] = unit[span, :].astype(bf16)
    first = pl.multiple_of((chip * 2 + mine) * number, 32)
    own_grads[...] = unit[pl.ds(first, number), :]
    own_branch[...] = unit[pl.ds(first, number), :].astype(bf16)
    values = scores[pl.ds(first, number), :]
    row_max = jnp.max(values, 1, keepdims=True)
    row_total = row_max + jnp.log(jnp.sum(jnp.exp(values - row_max), 1, keepdims=True))
    text_id = lax.broadcasted_iota(jnp.int32, (number, 1), 0) + first
    same = jnp.where(text_id == image_id, 1.0, 0.0)
    both = 0.5 * (row_total + column_total) - values
    pair_loss[...] = jnp.broadcast_to(jnp.sum(both * same, 1, keepdims=True), (number, 128))


def loss_whole(early_all, image_all, text_proj, chip, mine, number):
    total = image_all.shape[0]
    shape = jax.ShapeDtypeStruct
    pair_loss, grads, own_branch, branch = pl.pallas_call(
        loss_kernel,
        out_shape=[
            shape((number, 128), f32),
            shape((number, D), f32),
            shape((number, D), bf16),
            shape((total, D), bf16),
        ],
        in_specs=[SM] + [VM] * 3,
        out_specs=[VM] * 4,
        scratch_shapes=[
            pltpu.VMEM((total, D), f32),
            pltpu.VMEM((total, 128), f32),
            pltpu.VMEM((total, total), f32),
            pltpu.VMEM((total, total), bf16),
        ],
        compiler_params=limit(26),
        name="pair_loss",
    )(jnp.stack([chip, mine]), early_all[:, :EARLY], image_all, text_proj)
    return pair_loss[:, 0], grads, own_branch, branch


def loss_rows(pooled_all, image_all, text_proj, lengths_all, image_ids, first_row, local_pairs):
    unit_all, inverse_all = text_unit(pooled_all, text_proj)

    def own_rows(values):
        return lax.dynamic_slice_in_dim(values, first_row, local_pairs, 0)

    unit_text, inverse_z = own_rows(unit_all), own_rows(inverse_all)
    text_scores = dot_nt(unit_text.astype(bf16), image_all) * SCALE
    image_scores = dot_nt(image_all[:local_pairs], unit_all.astype(bf16)) * SCALE
    by_text, text_total = softmax_parts(text_scores, 1)
    image_total = softmax_parts(image_scores, 1)[1]
    every_total = gather_relative(image_total)
    text_ids = first_row + jnp.arange(local_pairs, dtype=jnp.int32)
    own_same = (text_ids[:, None] == image_ids).astype(f32)
    own = jnp.sum(text_scores * own_same, -1)
    pair_loss = 0.5 * (text_total[:, 0] - own) + 0.5 * (image_total[:, 0] - own)
    by_image = jnp.exp(text_scores - every_total[:, 0][None, :])
    sgrad = (0.5 * (by_text - own_same) + 0.5 * (by_image - own_same)).astype(bf16)
    grad_unit = dot(sgrad, image_all) * SCALE
    grads = branch_grad(grad_unit, unit_text, inverse_z, text_proj, own_rows(lengths_all))
    return pair_loss, grads, grads.astype(bf16), grads.astype(bf16)


def local(
    images,
    groups,
    captions,
    cap_lengths,
    img_gain_a,
    img_w_qkv,
    img_b_qv,
    img_w_out,
    img_gain_m,
    img_w_up,
    img_b_up,
    img_w_down,
    gain_attn,
    w_qkv,
    b_qv,
    w_out,
    gain_mlp,
    w_up,
    b_up,
    w_down,
    text_proj,
):
    local_pairs = images.shape[0]
    rows_total = local_pairs * CAP
    mine = lax.axis_index("rep").astype(jnp.int32)
    mine_one = mine[None]
    total_pairs = local_pairs * lax.axis_size("dp") * lax.axis_size("rep")
    whole = total_pairs <= MOST_PAIRS

    image_vec = jnp.concatenate([img_gain_a, img_b_qv, img_gain_m, img_b_up])[None]
    image_vec_other = swap(image_vec, "rep", 1)
    weights = []
    for weight in (img_w_qkv, img_w_out, img_w_up, img_w_down):
        weights += [weight, swap(weight, "rep", 1)]

    text_vec = lax.optimization_barrier(jnp.concatenate([gain_attn, b_qv, gain_mlp, b_up]))
    text_vec = text_vec.astype(f32)[None]
    flat = captions.reshape(rows_total, D)
    qkv, mixed, after, mlp, slope, attention, early = text_forward(
        flat, cap_lengths, text_vec, w_qkv, w_out, w_up, w_down
    )
    early, image_vec_other, *weights = lax.optimization_barrier((early, image_vec_other, *weights))
    early_all = lax.all_gather(
        early if whole else early[:, :EARLY], ("dp", "rep"), axis=0, tiled=True
    )
    image_emb = image_tower(
        jnp.transpose(images, (1, 0, 2)), groups, mine_one, image_vec, image_vec_other, weights
    )
    image_all = gather_relative(image_emb)
    chip = lax.axis_index("dp").astype(jnp.int32)
    if whole:
        pair_loss, grads, branch, branch_all = loss_whole(
            early_all, image_all, text_proj, chip, mine, local_pairs
        )
    else:
        chips = chip ^ jnp.array(relative_chips(), jnp.int32)
        devices = jnp.concatenate([2 * chips + mine, 2 * chips + 1 - mine])
        image_ids = (
            devices[:, None] * local_pairs + jnp.arange(local_pairs, dtype=jnp.int32)[None, :]
        ).reshape(1, total_pairs)
        pair_loss, grads, branch, branch_all = loss_rows(
            early_all[:, :D],
            image_all,
            text_proj,
            early_all[:, D : D + 1].astype(f32),
            image_ids,
            (2 * chip + mine) * local_pairs,
            local_pairs,
        )
    place = chunk_places()
    grad_pre, up_own, up_other, grad_bup = up_backward(
        place, mine_one, cap_lengths, branch, slope, mlp, w_down
    )
    arrived = swap(up_other, "rep", 1)
    grad_after, grad_mixed, grad_gain = mlp_backward(
        cap_lengths, grad_pre, grads, after, text_vec, w_up, w_out
    )
    ups, rests = streams_of(FF // 4), streams_of(D)
    up_sent, up_kept = reduce_first(up_own, arrived, ups)
    (grad_mixed,) = behind([grad_mixed], up_sent)
    up_came = reduce_swaps(up_sent, ups, 1)
    caption_grad, rest_own, rest_other = rest_backward(
        place, mine_one, qkv, attention, mixed, grad_mixed, grad_after, flat, text_vec,
        grad_gain, grad_bup, w_qkv,
    )
    rest_other, *up_came = lax.optimization_barrier((rest_other, *up_came))
    arrived = swap(rest_other, "rep", 1)
    up_sent, up_kept = reduce_add(up_came, up_kept)
    up_came = reduce_swaps(up_sent, ups, 2)
    (arrived,) = behind([arrived], up_sent)
    rest_sent, rest_kept = reduce_first(rest_own, arrived, rests)
    rest_came = reduce_swaps(rest_sent, rests, 1)
    up_came = behind(up_came, rest_sent)
    up_sent, up_kept = reduce_join(up_came, up_kept)
    up_came = reduce_swaps_far(up_sent)
    (branch_all,) = behind([branch_all], up_sent)
    half = D // 2
    own_columns = lax.dynamic_slice_in_dim(branch_all, mine * half, half, 1)
    if whole:
        grad_w_down = dot_tn(early_all[:, EARLY:], own_columns)
    else:
        other_columns = lax.dynamic_slice_in_dim(branch_all, (1 - mine) * half, half, 1)
        grad_w_down = dot_tn(early[:, EARLY:], own_columns) + swap(
            dot_tn(early[:, EARLY:], other_columns).astype(bf16), "rep", 1
        ).astype(f32)
        grad_w_down = lax.psum(grad_w_down, "dp")
    rest_came = behind(rest_came, [grad_w_down])
    rest_sent, rest_kept = reduce_add(rest_came, rest_kept)
    rest_came = reduce_swaps(rest_sent, rests, 2)
    up_came = behind(up_came, rest_sent)
    up_chunk = reduce_last(up_came, up_kept)
    up_column = spread_first(up_chunk)
    rest_came = behind(rest_came, [up_chunk])
    rest_sent, rest_kept = reduce_join(rest_came, rest_kept)
    rest_came = reduce_swaps_far(rest_sent)
    up_column = behind(up_column, rest_sent)
    up_mine = spread_second(up_column, ups)
    up_near, up_across = spread_swaps(up_mine, ups, 2), spread_swaps(up_mine, ups, 1)
    rest_came = behind(rest_came, up_mine)
    rest_chunk = reduce_last(rest_came, rest_kept)
    (rest_chunk,) = behind([rest_chunk], up_near + up_across)
    rest_column = spread_first(rest_chunk)
    up_near = behind(up_near, [rest_chunk])
    up_last = spread_swaps(up_near, ups, 1)
    rest_column = behind(rest_column, up_near)
    rest_mine = spread_second(rest_column, rests)
    rest_near, rest_across = spread_swaps(rest_mine, rests, 2), spread_swaps(rest_mine, rests, 1)
    up_last = behind(up_last, rest_mine)
    grad_w_up = unpack_up(place, in_quarters(up_mine, up_near, up_across, up_last))
    rest_near = behind(rest_near, [grad_w_up])
    rest_last = spread_swaps(rest_near, rests, 1)
    grad_w_qkv, grad_w_out, *small = unpack_rest(
        place, in_quarters(rest_mine, rest_near, rest_across, rest_last)
    )
    return (
        pair_loss,
        caption_grad.reshape(local_pairs, CAP, D),
        small[0],
        grad_w_qkv,
        small[1],
        grad_w_out,
        small[2],
        grad_w_up,
        small[3],
        grad_w_down,
    )


def solution(mesh):
    in_specs = (
        P(("dp", "rep"), None, None),
        P(("dp", "rep")),
        P(("dp", "rep"), None, None),
        P(("dp", "rep")),
        P("rep"),
        P("rep", None),
        P("rep"),
        P("rep", None),
        P("rep"),
        P("rep", None),
        P("rep"),
        P("rep", None),
        P(),
        P(),
        P(),
        P(),
        P(),
        P(),
        P(),
        P(),
        P(),
    )
    out_specs = (
        P(("dp", "rep")),
        P(("dp", "rep"), None, None),
        P("rep"),
        P(None, "rep"),
        P("rep"),
        P(None, "rep"),
        P("rep"),
        P(None, "rep"),
        P("rep"),
        P(None, "rep"),
    )
    return jax.shard_map(local, mesh=mesh, in_specs=in_specs, out_specs=out_specs, check_vma=False)
```
